32 devices in a mesh: dp: 4 (over x, core), seq: 8 (over z, y).
Axes of the slice: x: 2, y: 2, z: 4, core: 2. Of those that a mesh axis runs over, the one named last changes fastest.
Arguments:
- hidden: bfloat16 [4, 1024, 1024], P('dp', 'seq'), may hold values from -6 to 6
- group_ids: int32 [4, 1024], P('dp'), may hold values from 0 to 4, as said below
- norm1_gain: bfloat16 [1024], replicated, may hold values from 0.25 to 1.75
- query_weight: bfloat16 [1024, 1024], replicated, may hold values from -0.09375 to 0.09375
- key_weight: bfloat16 [1024, 1024], replicated, may hold values from -0.09375 to 0.09375
- value_weight: bfloat16 [1024, 1024], replicated, may hold values from -0.1875 to 0.1875
- out_weight: bfloat16 [1024, 1024], replicated, may hold values from -0.75 to 0.75
- relative_bias: bfloat16 [32, 16], replicated, may hold values from -4 to 4
- norm2_gain: bfloat16 [1024], replicated, may hold values from 0.25 to 1.75
- gate_weight: bfloat16 [1024, 2816], replicated, may hold values from -0.1875 to 0.1875
- up_weight: bfloat16 [1024, 2816], replicated, may hold values from -0.1875 to 0.1875
- down_projection_weight: bfloat16 [2816, 1024], replicated, may hold values from -0.109375 to 0.109375
- out_grad: bfloat16 [4, 1024, 1024], P('dp', 'seq'), may hold values from -6 to 6
Outputs:
- block_out: bfloat16 [4, 1024, 1024], P('dp', 'seq')
- hidden_grad: float32 [4, 1024, 1024], P('dp', 'seq')
- norm1_gain_grad: float32 [1024], replicated
- query_weight_grad: float32 [1024, 1024], replicated
- key_weight_grad: float32 [1024, 1024], replicated
- value_weight_grad: float32 [1024, 1024], replicated
- out_weight_grad: float32 [1024, 1024], replicated
- relative_bias_grad: float32 [32, 16], replicated
- norm2_gain_grad: float32 [1024], replicated
- gate_weight_grad: float32 [1024, 2816], replicated
- up_weight_grad: float32 [1024, 2816], replicated
- down_weight_grad: float32 [2816, 1024], replicated
The draws below stay inside these ranges and needn't reach their ends.
Inputs may be any that keep to these rules, and one draw needn't show every extreme that they name: `group_ids`: along each row the ids never fall and each of the values 0 to 4 forms one run; the run of id 2 begins within the row's first 128 positions and ends within its last 128 positions.
All inputs are finite; a program needn't handle non-finite values.
Results may differ from the reference program's by a relative error of at most 0.018.
Values may be sent and summed in bfloat16 or wider, within the bound.
A program may use at most 384 MiB of HBM per device.

```python
import jax
import jax.numpy as jnp
from jax import lax

D = 1024
HEADS = 16
HEAD_DIM = 64
FF = 2816
BUCKETS = 32
TOK_DEV = 128
INNER = 1024
ROWS = 4
LEN = 1024


def draw_group_ids(key, part):

    def one_row(row_key):
        split_keys = jax.random.split(row_key, 4)
        main_start = jax.random.randint(split_keys[0], (), 2, TOK_DEV)
        first_cut = jax.random.randint(split_keys[1], (), 1, main_start)
        tail_size = jax.random.randint(split_keys[2], (), 2, TOK_DEV)
        main_end = LEN - tail_size
        last_cut = main_end + jax.random.randint(split_keys[3], (), 1, tail_size)
        position = jnp.arange(LEN, dtype=jnp.int32)
        return (position >= first_cut).astype(jnp.int32) + (position >= main_start).astype(jnp.int32) + (position >= main_end).astype(jnp.int32) + (position >= last_cut).astype(jnp.int32)
    row_keys = jax.random.split(jax.random.fold_in(key, 17), ROWS)
    return jax.vmap(one_row)(row_keys)


def level_of(rng, dims, shards, low, high):
    loudness = 1.0
    for dim, shards_of in shards:
        steps = jax.random.uniform(jax.random.fold_in(jax.random.fold_in(rng, 6), dim), (shards_of,), jnp.float32, low / len(shards), high / len(shards))
        loudness = loudness * jnp.repeat(jnp.exp(steps), dims[dim] // shards_of).reshape((-1,) + (1,) * (len(dims) - 1 - dim))
    return loudness


def scatter_about(key, extent, scale, bound, shards=(), kind=jnp.bfloat16):
    values = scale * jax.random.normal(key, extent, jnp.float32)
    if shards:
        values = values * level_of(key, extent, shards, -0.22, 0.18)
    return jnp.clip(values, -bound, bound).astype(kind)


def setup_inputs(seed: int = 0) -> dict:
    arg_keys = jax.random.split(jax.random.key(seed), 14)
    hidden = scatter_about(arg_keys[0], (ROWS, LEN, D), 1.0, 6.0, ((0, 4), (1, 8)))
    group_ids = draw_group_ids(jax.random.fold_in(arg_keys[13], 71), 0)
    norm1_gain = jnp.clip(1.0 + 0.15 * jax.random.normal(arg_keys[2], (D,), jnp.float32), 0.25, 1.75).astype(jnp.bfloat16)
    query_weight = scatter_about(arg_keys[3], (D, INNER), (4 * D) ** -0.5, 0.09375)
    key_weight = scatter_about(arg_keys[4], (D, INNER), (4 * D) ** -0.5, 0.09375)
    value_weight = scatter_about(arg_keys[5], (D, INNER), D ** -0.5, 0.1875)
    out_weight = scatter_about(arg_keys[6], (INNER, D), (max(1, 64 * INNER // LEN)) ** -0.5, 0.75)
    relative_bias = scatter_about(arg_keys[7], (BUCKETS, HEADS), 1.0, 4.0)
    norm2_gain = jnp.clip(1.0 + 0.15 * jax.random.normal(arg_keys[8], (D,), jnp.float32), 0.25, 1.75).astype(jnp.bfloat16)
    gate_weight = scatter_about(arg_keys[9], (D, FF), D ** -0.5, 0.1875)
    up_weight = scatter_about(arg_keys[10], (D, FF), D ** -0.5, 0.1875)
    down_projection_weight = scatter_about(arg_keys[11], (FF, D), FF ** -0.5, 0.109375)
    out_grad = scatter_about(arg_keys[12], (ROWS, LEN, D), 1.0, 6.0, ((0, 4), (1, 8)))
    return dict(hidden=hidden, group_ids=group_ids, norm1_gain=norm1_gain, query_weight=query_weight, key_weight=key_weight, value_weight=value_weight, out_weight=out_weight, relative_bias=relative_bias, norm2_gain=norm2_gain, gate_weight=gate_weight, up_weight=up_weight, down_projection_weight=down_projection_weight, out_grad=out_grad)


EPSILON = 1e-06
MASKED = -1e+30
THRESHOLDS = (12, 16, 23, 32, 46, 64, 91)

@jax.custom_vjp
def low(v):
    return lax.optimization_barrier(v.astype(jnp.bfloat16)).astype(jnp.float32)

@jax.custom_vjp
def low_back(v):
    return v

def low_keep(v):
    return (low(v), None)

def low_pass(kept, grad):
    return (grad,)

def back_keep(v):
    return (v, None)

def back_low(kept, grad):
    return (low(grad),)
low.defvjp(low_keep, low_pass)
low_back.defvjp(back_keep, back_low)

def bucket_of(relative):
    distance = jnp.abs(relative)
    bucket_level = jnp.full(relative.shape, 8, jnp.int32)
    for boundary in THRESHOLDS:
        bucket_level = bucket_level + (distance >= boundary).astype(jnp.int32)
    near_bucket = jnp.where(distance < 8, distance, bucket_level)
    return near_bucket + 16 * (relative > 0).astype(jnp.int32)

def matmul(left_mat, right_mat):
    return jnp.dot(left_mat, right_mat, precision=lax.Precision.HIGHEST, preferred_element_type=jnp.float32)

def rms_norm(vector, norm_gain):
    return vector * lax.rsqrt(lax.optimization_barrier(jnp.mean(vector * vector, axis=-1, keepdims=True)) + EPSILON) * norm_gain

def layer(inputs, row_groups, params):
    gain_one, w_query, w_key, w_value, w_out, bias_lookup, gain_two, w_gate, w_up, w_down = params
    length = inputs.shape[0]
    normed = low(rms_norm(inputs, gain_one))
    query_heads = low_back(low(matmul(normed, w_query))).reshape(length, HEADS, HEAD_DIM)
    key_heads = low_back(low(matmul(normed, w_key))).reshape(length, HEADS, HEAD_DIM)
    value_entries = low_back(low(matmul(normed, w_value))).reshape(length, HEADS, HEAD_DIM)
    query_block = min(512, length)
    block_count = length // query_block
    position = jnp.arange(length, dtype=jnp.int32)

    def attend(scanned):
        query_part, query_places, query_groups = scanned
        scores = jnp.einsum('qhd,khd->hqk', query_part, key_heads, precision=lax.Precision.HIGHEST)
        bucket = bucket_of(position[None, :] - query_places[:, None])
        scores = scores + jnp.transpose(bias_lookup[bucket], (2, 0, 1))
        scores = low_back(scores)
        same_group = query_groups[:, None] == row_groups[None, :]
        scores = jnp.where(same_group[None], scores, MASKED)
        row_max = lax.optimization_barrier(jnp.max(scores, axis=-1, keepdims=True))
        weights = jnp.exp(scores - row_max)
        weights = low(weights / lax.optimization_barrier(jnp.sum(weights, axis=-1, keepdims=True)))
        return jnp.einsum('hqk,khd->qhd', weights, value_entries, precision=lax.Precision.HIGHEST)
    mixed_heads = lax.map(jax.checkpoint(attend), (query_heads.reshape(block_count, query_block, HEADS, HEAD_DIM), position.reshape(block_count, query_block), row_groups.reshape(block_count, query_block)))
    mixed_heads = low_back(low(mixed_heads.reshape(length, HEADS * HEAD_DIM)))
    branch = low_back(matmul(mixed_heads, w_out))
    middle = inputs + branch
    normed_two = low(rms_norm(middle, gain_two))
    gate_proj = low_back(matmul(normed_two, w_gate))
    up_proj = low_back(matmul(normed_two, w_up))
    hidden_act = low(jax.nn.gelu(gate_proj, approximate=True) * up_proj)
    return middle + low_back(matmul(hidden_act, w_down))

def reference(hidden, group_ids, norm1_gain, query_weight, key_weight, value_weight, out_weight, relative_bias, norm2_gain, gate_weight, up_weight, down_projection_weight, out_grad):
    params = tuple((weight_arg.astype(jnp.float32) for weight_arg in (norm1_gain, query_weight, key_weight, value_weight, out_weight, relative_bias, norm2_gain, gate_weight, up_weight, down_projection_weight)))

    def one_row(totals, scanned):
        row_input, row_groups, cotangent = scanned

        def forward(layer_input, layer_params):
            return layer(layer_input, row_groups, layer_params)
        result, backward_function = jax.vjp(forward, row_input.astype(jnp.float32), params)
        input_grad, param_grads = backward_function(cotangent.astype(jnp.float32))
        totals = tuple((summed + added for summed, added in zip(totals, param_grads)))
        return (totals, (result.astype(jnp.bfloat16), input_grad))
    zeroed = tuple((jnp.zeros(weight_arg.shape, jnp.float32) for weight_arg in params))
    totals, (results, input_grads) = lax.scan(one_row, zeroed, (hidden, group_ids, out_grad))
    return (results, input_grads, totals[0], totals[1], totals[2], totals[3], totals[4], totals[5], totals[6], totals[7], totals[8], totals[9])
```

```python
import functools

import jax
import jax.numpy as jnp
from jax import lax
from jax.experimental import pallas as pl
from jax.experimental.pallas import tpu as pltpu
from jax.sharding import PartitionSpec as P

EPSILON = 1e-06
MASKED = -1e30
THRESHOLDS = (12, 16, 23, 32, 46, 64, 91)
MESH = pl.DeviceIdType.MESH
BF = jnp.bfloat16
F32 = jnp.float32
LANES = 128
ANY = pl.BlockSpec(memory_space=pl.ANY)
VMEM = pl.BlockSpec(memory_space=pltpu.VMEM)
SMEM = pl.BlockSpec(memory_space=pltpu.SMEM)


def bucket_of(relative):
    distance = jnp.abs(relative)
    bucket_level = jnp.full(relative.shape, 8, jnp.int32)
    for boundary in THRESHOLDS:
        bucket_level = bucket_level + (distance >= boundary).astype(jnp.int32)
    near_bucket = jnp.where(distance < 8, distance, bucket_level)
    return near_bucket + 16 * (relative > 0).astype(jnp.int32)


def dot(left_mat, right_mat):
    return jnp.dot(left_mat, right_mat, preferred_element_type=F32)


def dot_rows(left_mat, right_mat):
    return lax.dot_general(
        left_mat, right_mat, (((0,), (0,)), ((), ())), preferred_element_type=F32
    )


def dot_cols(left_mat, right_mat):
    return lax.dot_general(
        left_mat, right_mat, (((1,), (1,)), ((), ())), preferred_element_type=F32
    )


def ring_place(index, count):
    odd = index % 2
    return (1 - odd) * (index // 2) + odd * ((2 * count - 1 - index) // 2)


def ring_index(place, count):
    late = place // (count // 2)
    return (1 - late) * 2 * place + late * (2 * count - 1 - 2 * place)


def greet(targets):
    barrier = pltpu.get_barrier_semaphore()
    for target in targets:
        pl.semaphore_signal(barrier, inc=1, device_id=target, device_id_type=MESH)
    pl.semaphore_wait(barrier, len(targets))


def comm_params(collective_id, vmem=None):
    return pltpu.CompilerParams(
        collective_id=collective_id, has_side_effects=True, vmem_limit_bytes=vmem
    )


class Spot:
    def __init__(self, count):
        self.count = count
        self.half = count // 2
        self.me = lax.axis_index("seq")
        self.dp = lax.axis_index("dp")
        self.place = ring_place(self.me, count)
        self.nexts = tuple((self.dp, self.at(step)) for step in (1, -1))
        self.far_dp = (self.dp + 2) % 4
        self.twin_dp = self.dp + 1 - 2 * (self.dp % 2)
        self.far = (self.far_dp, self.me)
        self.twin = (self.twin_dp, self.me)
        self.others = tuple((self.dp, (self.me + step) % count) for step in range(1, count))

    def at(self, step):
        return ring_index((self.place + (step + self.count) % self.count) % self.count, self.count)

    def back(self, way, hop):
        return self.at(-hop if way == 0 else hop)


def push(source, target, send_sem, recv_sem, device):
    copy = pltpu.make_async_remote_copy(
        src_ref=source,
        dst_ref=target,
        send_sem=send_sem,
        recv_sem=recv_sem,
        device_id=device,
        device_id_type=MESH,
    )
    copy.start()
    return copy


class RingGather:
    def __init__(self, spot, own, into, send_sems, recv_sems):
        self.spot, self.own, self.into = spot, own, into
        self.send_sems, self.recv_sems = send_sems, recv_sems
        self.copies = {}

    def pieces(self, way, hop):
        return (0, 1) if hop < self.spot.half - 1 else (way,)

    def forward(self, hop, way, piece):
        spot = self.spot
        if hop >= spot.half or piece not in self.pieces(way, hop):
            return
        origin = spot.back(way, hop)
        target = self.into(origin, piece)
        self.copies[hop, way, piece] = push(
            self.own(piece) if hop == 0 else target,
            target,
            self.send_sems.at[way, hop, piece],
            self.recv_sems.at[way, hop, piece],
            spot.nexts[way],
        )

    def begin(self):
        for piece in range(2):
            for way in range(2):
                self.forward(0, way, piece)

    def step(self, hop):
        for piece in range(2):
            for way in range(2):
                if (hop, way, piece) in self.copies:
                    self.copies[hop, way, piece].wait_recv()
                    self.forward(hop + 1, way, piece)

    def finish(self):
        for copy in self.copies.values():
            copy.wait_send()


def ring_sems(count):
    return [pltpu.SemaphoreType.DMA((2, count // 2, 2))] * 2


class RingSum:
    def __init__(self, spot, term, bufs, send_sems, recv_sems):
        self.spot, self.term, self.bufs = spot, term, bufs
        self.send_sems, self.recv_sems = send_sems, recv_sems
        self.copies = {}

    def send(self, hop, way, piece, sources):
        for kind, source in enumerate(sources):
            self.copies[hop, way, piece, kind] = push(
                source,
                self.bufs[kind].at[way, hop, piece],
                self.send_sems.at[way, hop, piece, kind],
                self.recv_sems.at[way, hop, piece, kind],
                self.spot.nexts[way],
            )

    def block(self, way, hop):
        step = self.spot.half - hop
        return self.spot.at(step if way == 0 else -step)

    def begin(self):
        for way in range(2):
            self.send(0, way, way, self.term(self.block(way, 0), way))
        for way in range(2):
            self.send(1, way, 1 - way, self.term(self.block(way, 1), 1 - way))

    def step(self, hop):
        for piece in range(2):
            for way in range(2):
                if (hop, way, piece, 0) not in self.copies or hop + 1 >= self.spot.half:
                    continue
                terms = self.term(self.block(way, hop + 1), piece)
                for kind, term in enumerate(terms):
                    self.copies[hop, way, piece, kind].wait_recv()
                    buf = self.bufs[kind]
                    buf[way, hop, piece] = (
                        buf[way, hop, piece].astype(F32) + term[...].astype(F32)
                    ).astype(BF)
                self.send(
                    hop + 1, way, piece, [buf.at[way, hop, piece] for buf in self.bufs]
                )

    def total(self, piece, kind):
        last = self.spot.half - 1
        value = self.term(self.spot.me, piece)[kind][...].astype(F32)
        for way in range(2):
            self.copies[last, way, piece, kind].wait_recv()
            value = value + self.bufs[kind][way, last, piece].astype(F32)
        return value

    def finish(self):
        for copy in self.copies.values():
            copy.wait_send()


class MeshGather:
    def __init__(self, spot, x_ref, o_ref, share, sems):
        self.spot, self.x_ref, self.o_ref = spot, x_ref, o_ref
        self.ring_s, self.ring_r, self.x_s, self.x_r, self.core_s, self.core_r = sems
        rows = x_ref.shape[0]
        first = rows * share // 100 // 32 * 32
        cuts = (0, first // 2, first, first + (rows - first) // 2 // 16 * 16, rows)
        self.windows = [
            [pl.ds(cuts[2 * part + piece], cuts[2 * part + piece + 1] - cuts[2 * part + piece]) for piece in range(2)]
            for part in range(2)
        ]
        self.ring, self.x, self.core = {}, {}, {}

    def into(self, dp, origin, part, piece):
        return self.o_ref.at[dp, origin, self.windows[part][piece]]

    def pieces(self, way, hop):
        return (0, 1) if hop < self.spot.half - 1 else (way,)

    def pass_on(self, part, lane, hop, way, piece, source):
        spot = self.spot
        dp = spot.far_dp if lane else spot.dp
        origin = spot.me if way is None else spot.back(way, hop)
        target = self.into(dp, origin, part, piece)
        source = target if source is None else source
        slot = 0 if way is None else 2 * hop - 1 + way
        for onward in (0, 1) if way is None else (way,):
            if hop < spot.half and piece in self.pieces(onward, hop):
                index = (2 * part if lane == 0 else 4) + onward
                self.ring[part, lane, hop, onward, piece] = push(
                    source, target,
                    self.ring_s.at[index, hop, piece], self.ring_r.at[index, hop, piece],
                    spot.nexts[onward],
                )
        if part == 0 and lane == 0:
            self.x[part, slot, piece] = push(
                source, target,
                self.x_s.at[part, slot, piece], self.x_r.at[part, slot, piece], spot.far,
            )
        index = 2 * part + lane
        self.core[part, lane, slot, piece] = push(
            source, target,
            self.core_s.at[index, slot, piece], self.core_r.at[index, slot, piece], spot.twin,
        )

    def begin(self):
        spot = self.spot
        for piece in range(2):
            self.x[1, 0, piece] = push(
                self.x_ref.at[self.windows[1][piece]],
                self.into(spot.dp, spot.me, 1, piece),
                self.x_s.at[1, 0, piece], self.x_r.at[1, 0, piece], spot.far,
            )
        for part in range(2):
            for piece in range(2):
                self.pass_on(part, 0, 0, None, piece, self.x_ref.at[self.windows[part][piece]])

    def begin_far(self):
        for piece in range(2):
            self.x[1, 0, piece].wait_recv()
            self.pass_on(1, 1, 0, None, piece, None)

    def step(self, hop):
        for piece in range(2):
            for part, lane in ((0, 0), (1, 0), (1, 1)):
                for way in range(2):
                    key = (part, lane, hop, way, piece)
                    if key in self.ring:
                        self.ring[key].wait_recv()
                        self.pass_on(part, lane, hop + 1, way, piece, None)

    def step_far(self, hop):
        spot = self.spot
        for piece in range(2):
            for way in (None,) if hop == 0 else range(2):
                slot = 0 if way is None else 2 * hop - 1 + way
                if (0, slot, piece) in self.x:
                    self.x[0, slot, piece].wait_recv()
                    origin = spot.me if way is None else spot.back(way, hop)
                    target = self.into(spot.far_dp, origin, 0, piece)
                    self.core[0, 1, slot, piece] = push(
                        target, target,
                        self.core_s.at[1, slot, piece], self.core_r.at[1, slot, piece], spot.twin,
                    )

    def finish(self):
        for copy in self.core.values():
            copy.wait_recv()
        for copies in (self.ring, self.x, self.core):
            for copy in copies.values():
                copy.wait_send()


def mesh_sems(count):
    half = count // 2
    return [
        pltpu.SemaphoreType.DMA(shape)
        for shape in ((6, half, 2), (2, 2 * half + 1, 2), (4, 2 * half + 1, 2))
        for _ in range(2)
    ]


def ring_gather_body(count, x_ref, o_ref, own_sem, send_sems, recv_sems):
    spot = Spot(count)
    greet(spot.nexts)
    rows = x_ref.shape[0] // 2
    own = pltpu.make_async_copy(x_ref, o_ref.at[spot.me], own_sem)
    own.start()
    ring = RingGather(
        spot,
        lambda piece: x_ref.at[pl.ds(piece * rows, rows)],
        lambda origin, piece: o_ref.at[origin, pl.ds(piece * rows, rows)],
        send_sems,
        recv_sems,
    )
    ring.begin()
    for hop in range(spot.half):
        ring.step(hop)
    own.wait()
    ring.finish()


def ring_gather(block, count, collective_id, name):
    return pl.pallas_call(
        functools.partial(ring_gather_body, count),
        name=name,
        out_shape=jax.ShapeDtypeStruct((count,) + block.shape, block.dtype),
        in_specs=[ANY],
        out_specs=ANY,
        scratch_shapes=[pltpu.SemaphoreType.DMA(())] + ring_sems(count),
        compiler_params=comm_params(collective_id),
    )(block)


def exchange_body(count, parts, x_ref, o_ref, own_sems, send_sems, recv_sems):
    me = lax.axis_index("seq")
    dp = lax.axis_index("dp")
    greet([(dp, (me + step) % count) for step in range(1, count)])
    rows = x_ref.shape[0] // count
    copies = []
    columns = pl.ds(pl.multiple_of(me * LANES, LANES), LANES)
    for step in range(1, count):
        target = (me + step) % count
        for part in range(parts):
            copy = pltpu.make_async_remote_copy(
                src_ref=x_ref.at[pl.ds(target * rows, rows), pl.ds(part * LANES, LANES)],
                dst_ref=o_ref.at[part, :, columns],
                send_sem=send_sems.at[step - 1, part],
                recv_sem=recv_sems.at[step - 1, part],
                device_id=(dp, target),
                device_id_type=MESH,
            )
            copy.start()
            copies.append(copy)
    for part in range(parts):
        copy = pltpu.make_async_copy(
            x_ref.at[pl.ds(me * rows, rows), pl.ds(part * LANES, LANES)],
            o_ref.at[part, :, columns],
            own_sems.at[part],
        )
        copy.start()
        copies.append(copy)
    for copy in copies:
        copy.wait()


def exchange(block, count, collective_id, name):
    parts = block.shape[1] // LANES
    rows = block.shape[0] // count
    return pl.pallas_call(
        functools.partial(exchange_body, count, parts),
        name=name,
        out_shape=jax.ShapeDtypeStruct((parts, rows, count * LANES), block.dtype),
        in_specs=[ANY],
        out_specs=ANY,
        scratch_shapes=[
            pltpu.SemaphoreType.DMA((parts,)),
            pltpu.SemaphoreType.DMA((count - 1, parts)),
            pltpu.SemaphoreType.DMA((count - 1, parts)),
        ],
        compiler_params=comm_params(collective_id),
    )(block)


def near_buckets(rows):
    shape = (rows, rows + 2 * LANES)
    column = lax.broadcasted_iota(jnp.int32, shape, 1) - LANES
    return bucket_of(column - lax.broadcasted_iota(jnp.int32, shape, 0))


def strip_window(step, rows, length):
    return pl.ds(pl.multiple_of(length - rows - step * rows, LANES), length)


def attend_body(heads, depth, table_ref, qkv_ref, column_ids, row_ids, p_ref, mixed_ref, strip):
    step = pl.program_id(0)
    rows = column_ids.shape[0]
    length = qkv_ref.shape[0]
    low = length - rows - LANES

    @pl.when(step == 0)
    def _():
        bucket = near_buckets(rows)
        for head in range(heads):
            value = jnp.zeros(bucket.shape, F32)
            for level in range(table_ref.shape[1]):
                value = jnp.where(bucket == level, table_ref[head, level], value)
            before = jnp.full((rows, low), table_ref[head, 15], F32)
            after = jnp.full((rows, strip.shape[2] - low - bucket.shape[1]), table_ref[head, 31], F32)
            strip[head, :, :low] = before
            strip[head, :, low : low + bucket.shape[1]] = value
            strip[head, :, low + bucket.shape[1] :] = after

    same = column_ids[...] == row_ids[...]
    mine = pl.ds(step * rows, rows)
    inner = heads * depth
    window = strip_window(step, rows, length)
    for head in range(heads):
        columns = slice(head * depth, (head + 1) * depth)
        query = qkv_ref[mine, columns]
        key = qkv_ref[:, inner + head * depth : inner + (head + 1) * depth]
        value = qkv_ref[:, 2 * inner + head * depth : 2 * inner + (head + 1) * depth]
        scores = dot_cols(query, key) + strip[head, :, window]
        scores = jnp.where(same, scores, MASKED)
        top = jnp.max(scores, axis=1, keepdims=True)
        weight = jnp.exp(scores - top)
        weight = weight * (1.0 / jnp.sum(weight, axis=1, keepdims=True))
        weight = weight.astype(BF)
        p_ref[head] = weight
        mixed_ref[:, columns] = dot(weight, value).astype(BF)


def attend(qkv, groups, table, heads, depth):
    length = qkv.shape[0]
    rows = 256
    inner = heads * depth
    return pl.pallas_call(
        functools.partial(attend_body, heads, depth),
        name="attend",
        grid=(length // rows,),
        out_shape=(
            jax.ShapeDtypeStruct((heads, length, length), BF),
            jax.ShapeDtypeStruct((length, inner), BF),
        ),
        in_specs=[
            SMEM,
            pl.BlockSpec((length, 3 * inner), lambda i: (0, 0)),
            pl.BlockSpec((rows, 1), lambda i: (i, 0)),
            pl.BlockSpec((1, length), lambda i: (0, 0)),
        ],
        out_specs=(
            pl.BlockSpec((heads, rows, length), lambda i: (0, i, 0)),
            pl.BlockSpec((rows, inner), lambda i: (i, 0)),
        ),
        scratch_shapes=[pltpu.VMEM((heads, rows, 2 * length - rows), F32)],
        compiler_params=pltpu.CompilerParams(vmem_limit_bytes=48 << 20),
    )(table, qkv, groups[:, None], groups[None, :])


def tail_body(
    count,
    heads,
    depth,
    levels,
    branch_ref,
    wide_ref,
    tall_ref,
    own_out_ref,
    qkv_ref,
    p_ref,
    normed_ref,
    mixed_ref,
    feed_ref,
    proj_ref,
    own_dqkv_ref,
    table_ref,
    branch,
    dqkv,
    strip,
    keys,
    values,
    wide_buf,
    tall_buf,
    feed_block,
    packed,
    near_out,
    near_in,
    far_out,
    far_in,
    proj_block,
    ring_s,
    ring_r,
    sum_s,
    sum_r,
    trade_own,
    trade_s,
    trade_r,
    pair_s,
    pair_r,
    copy_sems,
    *gather_sems,
):
    spot = Spot(count)
    rows, width = branch_ref.shape
    length = qkv_ref.shape[0]
    inner = heads * depth
    greet(spot.others + (spot.far, spot.twin))

    half_rows = rows // 2
    ring = RingGather(
        spot,
        lambda piece: branch_ref.at[pl.ds(piece * half_rows, half_rows)],
        lambda origin, piece: branch.at[origin, pl.ds(piece * half_rows, half_rows)],
        ring_s,
        ring_r,
    )
    ring.begin()
    wide_rows, tall_rows = wide_ref.shape[1] // 2, tall_ref.shape[0] // 2
    total = RingSum(
        spot,
        lambda block, piece: (
            wide_ref.at[block, pl.ds(piece * wide_rows, wide_rows)],
            tall_ref.at[
                pl.ds(piece * tall_rows, tall_rows),
                pl.ds(pl.multiple_of(block * LANES, LANES), LANES),
            ],
        ),
        (wide_buf, tall_buf),
        sum_s,
        sum_r,
    )
    total.begin()
    branch[spot.me] = branch_ref[...]
    strip[...] = jnp.zeros_like(strip)
    keys[...] = jnp.zeros_like(keys)
    values[...] = jnp.zeros_like(values)

    def attend_block(origin):
        mine = pl.ds(pl.multiple_of(origin * rows, rows), rows)
        window = strip_window(origin, rows, length)
        grads = dot_cols(branch[origin], own_out_ref[...]).astype(BF)
        for head in range(heads):
            columns = slice(head * depth, (head + 1) * depth)
            query = qkv_ref[mine, columns]
            key = qkv_ref[:, inner + head * depth : inner + (head + 1) * depth]
            value = qkv_ref[:, 2 * inner + head * depth : 2 * inner + (head + 1) * depth]
            grad = grads[:, columns]
            weight_low = p_ref[head, mine]
            weight = weight_low.astype(F32)
            scaled = weight * dot_cols(grad, value)
            score_grad = scaled - weight * jnp.sum(scaled, axis=1, keepdims=True)
            strip[head, :, window] += score_grad
            score_low = score_grad.astype(BF)
            dqkv[mine, columns] = dot(score_low, key).astype(BF)
            keys[:, columns] += dot_rows(score_low, query)
            values[:, columns] += dot_rows(weight_low, grad)

    attend_block(spot.me)
    for hop in range(spot.half):
        ring.step(hop)
        total.step(hop)
        if hop < spot.half - 1:

            def both(side, carry, hop=hop):
                attend_block(spot.at((1 - 2 * side) * (hop + 1)))
                return carry

            lax.fori_loop(0, 2, both, 0)
        else:
            attend_block(spot.at(spot.half))

    tiles = wide_ref.shape[2] // LANES
    for piece in range(2):
        value = total.total(piece, 0).astype(BF)
        for tile in range(tiles):
            feed_block[pl.ds((2 * tile + piece) * wide_rows, wide_rows)] = value[
                :, tile * LANES : (tile + 1) * LANES
            ]
        feed_block[pl.ds(2 * tiles * wide_rows + piece * tall_rows, tall_rows)] = total.total(
            piece, 1
        ).astype(BF)
    half_sems = len(gather_sems) // 2
    feed = MeshGather(spot, feed_block, feed_ref, 62, gather_sems[:half_sems])
    feed.begin()
    feed_copy = pltpu.make_async_copy(feed_block, feed_ref.at[spot.dp, spot.me], copy_sems.at[0])
    feed_copy.start()

    dqkv[:, inner : 2 * inner] = keys[...].astype(BF)
    dqkv[:, 2 * inner :] = values[...].astype(BF)
    trades = []
    columns = pl.ds(pl.multiple_of(spot.me * LANES, LANES), LANES)
    for index, device in enumerate(spot.others):
        for part in range(3):
            trades.append(
                push(
                    dqkv.at[pl.ds(device[1] * rows, rows), pl.ds(part * LANES, LANES)],
                    own_dqkv_ref.at[part, :, columns],
                    trade_s.at[index, part],
                    trade_r.at[index, part],
                    device,
                )
            )
    for part in range(3):
        copy = pltpu.make_async_copy(
            dqkv.at[pl.ds(spot.me * rows, rows), pl.ds(part * LANES, LANES)],
            own_dqkv_ref.at[part, :, columns],
            trade_own.at[part],
        )
        copy.start()
        trades.append(copy)

    feed.begin_far()

    quarter = width // 4

    @pl.loop(0, 4)
    def _(index):
        block = dot_rows(
            normed_ref[:, pl.ds(pl.multiple_of(index * quarter, quarter), quarter)], dqkv[...]
        )
        for part in range(3):
            packed[index, part * quarter : (part + 1) * quarter] = block[
                :, part * LANES : (part + 1) * LANES
            ]

    slim = inner // 4
    for tile in range(width // LANES):
        terms = jnp.zeros((inner, LANES), F32)
        for source in range(count):
            terms = terms + dot_rows(
                mixed_ref[pl.ds(source * rows, rows)],
                branch[source, :, tile * LANES : (tile + 1) * LANES],
            )
        for index in range(4):
            base = 3 * quarter + tile * slim
            packed[index, base : base + slim] = terms[index * slim : (index + 1) * slim]
    core, side = spot.dp % 2, spot.dp // 2
    for index in range(2):
        near_out[index] = packed[2 * index + 1 - core].astype(BF)
    near = push(near_out, near_in, pair_s.at[0], pair_r.at[0], spot.twin)
    near.wait_recv()
    far_out[...] = (packed[2 * (1 - side) + core] + near_in[1 - side].astype(F32)).astype(BF)
    far = push(far_out, far_in, pair_s.at[1], pair_r.at[1], spot.far)
    feed.step(0)
    feed.step_far(0)
    far.wait_recv()
    proj_block[...] = (
        packed[2 * side + core] + near_in[side].astype(F32) + far_in[...].astype(F32)
    ).astype(BF)
    proj = MeshGather(spot, proj_block, proj_ref, 57, gather_sems[half_sems:])
    proj.begin()
    proj_copy = pltpu.make_async_copy(proj_block, proj_ref.at[spot.dp, spot.me], copy_sems.at[1])
    proj_copy.start()

    bucket = near_buckets(rows)
    span = bucket.shape[1]
    low = length - rows - LANES
    for head in range(heads):
        middle = strip[head, :, low : low + span]
        before = jnp.sum(strip[head, :, :low], axis=0, keepdims=True)
        after = jnp.sum(strip[head, :, low + span :], axis=0, keepdims=True)
        for level in range(levels):
            part = jnp.sum(jnp.where(bucket == level, middle, 0.0), axis=0, keepdims=True)
            row = part[:, :LANES]
            for tile in range(1, span // LANES):
                row = row + part[:, tile * LANES : (tile + 1) * LANES]
            edge = before if level == 15 else after if level == 31 else None
            if edge is not None:
                for tile in range(edge.shape[1] // LANES):
                    row = row + edge[:, tile * LANES : (tile + 1) * LANES]
            table_ref[head, level : level + 1, :] = row

    for hop in range(1, spot.half):
        feed.step(hop)
        if hop == 1:
            proj.begin_far()
        feed.step_far(hop)
    feed.step_far(spot.half)
    for hop in range(spot.half):
        proj.step(hop)
        proj.step_far(hop)
    proj.step_far(spot.half)
    feed_copy.wait()
    proj_copy.wait()
    near.wait_send()
    far.wait_send()
    for copy in trades:
        copy.wait()
    ring.finish()
    total.finish()
    feed.finish()
    proj.finish()


def tail(branch, wide, tall, own_out, qkv, weights, normed, mixed, count, heads, depth, levels):
    rows, width = branch.shape
    length = qkv.shape[0]
    inner = heads * depth
    half = count // 2
    wide_rows, span = wide.shape[1:]
    tall_rows = tall.shape[0]
    feed_rows = wide_rows * (span // LANES) + tall_rows
    proj_rows = 3 * (width // 4) + inner // 4 * (width // LANES)
    dma = pltpu.SemaphoreType.DMA
    return pl.pallas_call(
        functools.partial(tail_body, count, heads, depth, levels),
        name="tail",
        out_shape=(
            jax.ShapeDtypeStruct((4, count, feed_rows, LANES), BF),
            jax.ShapeDtypeStruct((4, count, proj_rows, LANES), BF),
            jax.ShapeDtypeStruct((3, rows, width), BF),
            jax.ShapeDtypeStruct((heads, levels, LANES), F32),
        ),
        in_specs=[VMEM] * 8,
        out_specs=(ANY, ANY, ANY, VMEM),
        scratch_shapes=[
            pltpu.VMEM((count, rows, width), BF),
            pltpu.VMEM((length, 3 * inner), BF),
            pltpu.VMEM((heads, rows, 2 * length - rows), F32),
            pltpu.VMEM((length, inner), F32),
            pltpu.VMEM((length, inner), F32),
            pltpu.VMEM((2, half, 2, wide_rows // 2, span), BF),
            pltpu.VMEM((2, half, 2, tall_rows // 2, LANES), BF),
            pltpu.VMEM((feed_rows, LANES), BF),
            pltpu.VMEM((4, proj_rows, LANES), F32),
            pltpu.VMEM((2, proj_rows, LANES), BF),
            pltpu.VMEM((2, proj_rows, LANES), BF),
            pltpu.VMEM((proj_rows, LANES), BF),
            pltpu.VMEM((proj_rows, LANES), BF),
            pltpu.VMEM((proj_rows, LANES), BF),
            *ring_sems(count),
            dma((2, half, 2, 2)),
            dma((2, half, 2, 2)),
            dma((3,)),
            dma((count - 1, 3)),
            dma((count - 1, 3)),
            dma((2,)),
            dma((2,)),
            dma((2,)),
            *mesh_sems(count),
            *mesh_sems(count),
        ],
        compiler_params=comm_params(3, 56 << 20),
    )(branch, wide, tall, own_out, qkv, weights, normed, mixed)


def widen_pair_body(part, x_ref, gate_ref, up_ref):
    outs = (gate_ref, up_ref)
    for dp in range(x_ref.shape[0]):
        for tile in range(x_ref.shape[2] // LANES):
            block = x_ref[dp, 0, tile * LANES : (tile + 1) * LANES].astype(F32)
            start = tile * LANES
            while start < (tile + 1) * LANES:
                which = start // part
                stop = min((tile + 1) * LANES, (which + 1) * part)
                base = dp * part + start - which * part
                outs[which][:, base : base + stop - start] = block[
                    :, start - tile * LANES : stop - tile * LANES
                ]
                start = stop


def widen_pair(gathered, rows, part):
    dps, count = gathered.shape[:2]
    size = rows * 2 * part // LANES
    shape = jax.ShapeDtypeStruct((count * rows, dps * part), F32)
    spec = pl.BlockSpec((rows, dps * part), lambda i: (i, 0))
    return pl.pallas_call(
        functools.partial(widen_pair_body, part),
        name="widen_pair",
        grid=(count,),
        out_shape=(shape, shape),
        in_specs=[pl.BlockSpec((dps, 1, size, LANES), lambda i: (0, i, 0, 0))],
        out_specs=(spec, spec),
        compiler_params=pltpu.CompilerParams(vmem_limit_bytes=48 << 20),
    )(gathered)


def widen_columns_body(x_ref, *o_refs):
    rows = o_refs[0].shape[0]
    for index, o_ref in enumerate(o_refs):
        for source in range(x_ref.shape[1]):
            o_ref[:, source * LANES : (source + 1) * LANES] = x_ref[
                0, source, index * rows : (index + 1) * rows
            ].astype(F32)


def widen_columns(gathered, first, rows, outs, pieces):
    dps, count = gathered.shape[:2]
    size = rows // pieces
    shape = jax.ShapeDtypeStruct((dps * rows, count * LANES), F32)
    spec = pl.BlockSpec((size, count * LANES), lambda i, k: (i * pieces + k, 0))
    base = first // (size * outs)
    return pl.pallas_call(
        widen_columns_body,
        name="widen_columns",
        grid=(dps, pieces),
        out_shape=(shape,) * outs,
        in_specs=[
            pl.BlockSpec((1, count, size * outs, LANES), lambda i, k: (i, 0, base + k, 0))
        ],
        out_specs=(spec,) * outs,
        compiler_params=pltpu.CompilerParams(vmem_limit_bytes=48 << 20),
    )(gathered)


def widen_rows_body(x_ref, o_ref):
    dps, _, size, _ = x_ref.shape
    tiles = o_ref.shape[1] // LANES
    rows = size // tiles
    for dp in range(dps):
        for tile in range(tiles):
            o_ref[dp * rows : (dp + 1) * rows, tile * LANES : (tile + 1) * LANES] = x_ref[
                dp, 0, tile * rows : (tile + 1) * rows
            ].astype(F32)


def widen_rows(gathered, first, rows, width):
    dps, count = gathered.shape[:2]
    size = rows * (width // LANES)
    base = first // size
    return pl.pallas_call(
        widen_rows_body,
        name="widen_rows",
        grid=(count,),
        out_shape=jax.ShapeDtypeStruct((count * dps * rows, width), F32),
        in_specs=[pl.BlockSpec((dps, 1, size, LANES), lambda i: (0, i, base, 0))],
        out_specs=pl.BlockSpec((dps * rows, width), lambda i: (i, 0)),
    )(gathered)


def split_shards(
    hidden,
    group_ids,
    norm1_gain,
    query_weight,
    key_weight,
    value_weight,
    out_weight,
    relative_bias,
    norm2_gain,
    gate_weight,
    up_weight,
    down_projection_weight,
    out_grad,
    *,
    count,
):
    tokens, width = hidden.shape[1:]
    levels, head_count = relative_bias.shape
    depth = query_weight.shape[1] // head_count
    heads = head_count // count
    inner = heads * depth
    length = group_ids.shape[1]
    ff = gate_weight.shape[1] // 4
    me = lax.axis_index("seq")
    dp = lax.axis_index("dp")
    gain_one = norm1_gain.astype(F32)
    gain_two = norm2_gain.astype(F32)

    def over_core(value):
        return lax.ppermute(value, "dp", [(i, i ^ 1) for i in range(4)])

    def over_x(value):
        return lax.ppermute(value, "dp", [(i, i ^ 2) for i in range(4)])

    def gather_dp(value):
        near = over_core(value)
        far = over_x(value)
        cross = over_core(far)
        return jnp.concatenate([value, near, far, cross])

    def sum_dp(value):
        parts = value.reshape(4, tokens, width)
        kept = parts[0::2] + over_core(parts[1::2].astype(BF)).astype(F32)
        return kept[0] + over_x(kept[1].astype(BF)).astype(F32)

    row = ring_gather(hidden[0], count, 0, "gather_row").reshape(length, width)
    row_f = row.astype(F32)
    row_scale = lax.rsqrt(jnp.mean(row_f * row_f, axis=-1, keepdims=True) + EPSILON)
    normed = (row_f * row_scale * gain_one).astype(BF)
    own_columns = lambda w: lax.dynamic_slice_in_dim(w, me * inner, inner, axis=1)
    qkv_weight = jnp.concatenate(
        [own_columns(w) for w in (query_weight, key_weight, value_weight)], axis=1
    )
    qkv = dot(normed, qkv_weight).astype(BF)
    groups = group_ids[0]
    table = lax.dynamic_slice_in_dim(relative_bias, me * heads, heads, axis=1).T.astype(F32)
    weights, mixed_heads = attend(qkv, groups, table, heads, depth)
    mixed = exchange(mixed_heads, count, 1, "mixed_exchange")[0]

    inputs = hidden[0].astype(F32)
    middle = inputs + dot(mixed, out_weight)
    scale_two = lax.rsqrt(jnp.mean(middle * middle, axis=-1, keepdims=True) + EPSILON)
    normed_two = (middle * scale_two * gain_two).astype(BF)
    cotangents = gather_dp(out_grad[0])
    tokens_two = gather_dp(normed_two)
    pair_weight = jnp.concatenate(
        [
            lax.dynamic_slice_in_dim(gate_weight, dp * ff, ff, axis=1),
            lax.dynamic_slice_in_dim(up_weight, dp * ff, ff, axis=1),
        ],
        axis=1,
    )
    down_weight = lax.dynamic_slice_in_dim(down_projection_weight, dp * ff, ff, axis=0)
    pair = dot(tokens_two, pair_weight)
    gate, up = pair[:, :ff], pair[:, ff:]
    root = 0.7978845608028654
    squared = gate * gate
    bend = jnp.tanh(root * (gate + 0.044715 * gate * squared))
    half = 0.5 * (1.0 + bend)
    gelu = gate * half
    slope = half + 0.5 * gate * (1.0 - bend * bend) * root * (1.0 + 3 * 0.044715 * squared)
    activated = (gelu * up).astype(BF)
    act_grad = dot_cols(cotangents, down_weight)
    pair_grad = jnp.concatenate(
        [(act_grad * up * slope).astype(BF), (act_grad * gelu).astype(BF)], axis=1
    )
    normed_two_grad = sum_dp(dot_cols(pair_grad, pair_weight))
    block_out = (middle + sum_dp(dot(activated, down_weight))).astype(BF)
    pair_terms = dot_rows(tokens_two, pair_grad).astype(BF).reshape(count, width // count, 2 * ff)
    down_terms = dot_rows(activated, cotangents).astype(BF)
    cotangent = out_grad[0].astype(F32)
    lifted = gain_two * normed_two_grad
    middle_grad = (
        cotangent
        + scale_two * lifted
        - middle * scale_two**3 * jnp.mean(middle * lifted, axis=-1, keepdims=True)
    )
    gain_two_grad = jnp.sum(normed_two_grad * middle * scale_two, axis=0)

    own_out = lax.dynamic_slice_in_dim(out_weight, me * inner, inner, axis=0)
    feed, proj, own_dqkv, table_part = tail(
        middle_grad.astype(BF), pair_terms, down_terms, own_out, qkv, weights, normed, mixed_heads,
        count, heads, depth, levels,
    )
    normed_grad = (
        dot_cols(own_dqkv[0], query_weight)
        + dot_cols(own_dqkv[1], key_weight)
        + dot_cols(own_dqkv[2], value_weight)
    )
    scale_one = lax.rsqrt(jnp.mean(inputs * inputs, axis=-1, keepdims=True) + EPSILON)
    raised = gain_one * normed_grad
    hidden_grad = (
        middle_grad
        + scale_one * raised
        - inputs * scale_one**3 * jnp.mean(inputs * raised, axis=-1, keepdims=True)
    )
    gain_one_grad = jnp.sum(normed_grad * inputs * scale_one, axis=0)
    table_grad = lax.dynamic_update_slice_in_dim(
        jnp.zeros((levels, head_count), F32), jnp.sum(table_part, axis=-1).T, me * heads, axis=1
    )

    small = jnp.concatenate([gain_one_grad, gain_two_grad, table_grad.reshape(-1)])
    small = small.reshape(-1, LANES)
    small = small + over_core(small)
    small = small + over_x(small)
    step = 1
    while step < count:
        small = small + lax.ppermute(small, "seq", [(i, i ^ step) for i in range(count)])
        step *= 2
    small = small.reshape(-1)
    quarter, slim = width // 4, inner // 4
    gate_grad, up_grad = widen_pair(feed, width // count, ff)
    (down_grad,) = widen_columns(feed, 2 * ff * width // count // LANES, ff, 1, 2)
    query_grad, key_grad, value_grad = widen_columns(proj, 0, quarter, 3, 1)
    out_weight_grad = widen_rows(proj, 3 * quarter, slim, width)
    return (
        block_out[None],
        hidden_grad[None],
        small[:width],
        query_grad,
        key_grad,
        value_grad,
        out_weight_grad,
        small[2 * width :].reshape(levels, head_count),
        small[width : 2 * width],
        gate_grad,
        up_grad,
        down_grad,
    )


def rms_norm(vector, norm_gain):
    return (
        vector * lax.rsqrt(jnp.mean(vector * vector, axis=-1, keepdims=True) + EPSILON) * norm_gain
    )


def activate(gate_proj, up_proj):
    return jax.nn.gelu(gate_proj, approximate=True) * up_proj


def scores_of(
    query_part, key_part, query_places, key_places, query_groups, key_groups, bias_lookup
):
    bucket = bucket_of(key_places[None, :] - query_places[:, None])
    levels = jnp.arange(bias_lookup.shape[0], dtype=jnp.int32)
    one_hot_mask = (bucket[None] == levels[:, None, None]).astype(jnp.bfloat16)
    bias_patch_block = jnp.einsum(
        "ctf,cx->xtf", one_hot_mask, bias_lookup, preferred_element_type=jnp.float32
    )
    raw_scores = (
        jnp.einsum("qhd,khd->hqk", query_part, key_part, preferred_element_type=jnp.float32)
        + bias_patch_block
    )
    same_group = query_groups[:, None] == key_groups[None, :]
    return (one_hot_mask, jnp.where(same_group[None], raw_scores, MASKED))


def shards(
    hidden,
    group_ids,
    norm1_gain,
    query_weight,
    key_weight,
    value_weight,
    out_weight,
    relative_bias,
    norm2_gain,
    gate_weight,
    up_weight,
    down_projection_weight,
    out_grad,
):
    tok_rows = hidden.shape[1]
    head_count = relative_bias.shape[1]
    inner_width = query_weight.shape[1]
    head_depth = inner_width // head_count
    row_length = group_ids.shape[1]
    row_start = lax.axis_index("seq") * tok_rows
    key_block = min(1024, row_length)
    block_count = row_length // key_block
    row_groups = group_ids[0]
    own_groups = lax.dynamic_slice_in_dim(row_groups, row_start, tok_rows)
    own_places = row_start + jnp.arange(tok_rows, dtype=jnp.int32)
    all_places = jnp.arange(row_length, dtype=jnp.int32)

    def key_blocks(key_rows, value_rows):
        return (
            key_rows.reshape(block_count, key_block, head_count, head_depth),
            value_rows.reshape(block_count, key_block, head_count, head_depth),
            row_groups.reshape(block_count, key_block),
            all_places.reshape(block_count, key_block),
        )

    inputs = hidden[0].astype(jnp.float32)
    normed, norm_pull = jax.vjp(rms_norm, inputs, norm1_gain.astype(jnp.float32))
    normed_low = normed.astype(jnp.bfloat16)
    query_low = jnp.dot(normed_low, query_weight, preferred_element_type=jnp.float32).astype(
        jnp.bfloat16
    )
    key_low = jnp.dot(normed_low, key_weight, preferred_element_type=jnp.float32).astype(
        jnp.bfloat16
    )
    value_low = jnp.dot(normed_low, value_weight, preferred_element_type=jnp.float32).astype(
        jnp.bfloat16
    )
    key_all, value_all = (
        lax.all_gather(key_low, "seq", axis=0, tiled=True),
        lax.all_gather(value_low, "seq", axis=0, tiled=True),
    )
    query_heads = query_low.reshape(tok_rows, head_count, head_depth)

    def gather_stats(carry_state, scanned):
        running_max, running_sum = carry_state
        key_part, value_part, key_groups, key_places = scanned
        one_hot_mask, scores = scores_of(
            query_heads, key_part, own_places, key_places, own_groups, key_groups, relative_bias
        )
        new_max = jnp.maximum(running_max, jnp.max(scores, axis=-1))
        running_sum = running_sum * jnp.exp(running_max - new_max) + jnp.sum(
            jnp.exp(scores - new_max[..., None]), axis=-1
        )
        return ((new_max, running_sum), None)

    stats_init = (
        jnp.full((head_count, tok_rows), MASKED, jnp.float32),
        jnp.zeros((head_count, tok_rows), jnp.float32),
    )
    (running_max, running_sum), _ = lax.scan(
        gather_stats, stats_init, key_blocks(key_all, value_all)
    )
    log_total = running_max + jnp.log(running_sum)

    def gather_values(summed, scanned):
        key_part, value_part, key_groups, key_places = scanned
        one_hot_mask, scores = scores_of(
            query_heads, key_part, own_places, key_places, own_groups, key_groups, relative_bias
        )
        attention_low = jnp.exp(scores - log_total[..., None]).astype(jnp.bfloat16)
        return (
            summed
            + jnp.einsum(
                "hqk,khd->qhd", attention_low, value_part, preferred_element_type=jnp.float32
            ),
            None,
        )

    mixed, _ = lax.scan(
        gather_values,
        jnp.zeros((tok_rows, head_count, head_depth), jnp.float32),
        key_blocks(key_all, value_all),
    )
    mixed_low = mixed.reshape(tok_rows, inner_width).astype(jnp.bfloat16)
    middle = inputs + jnp.dot(mixed_low, out_weight, preferred_element_type=jnp.float32)
    normed_two, norm_two_pull = jax.vjp(rms_norm, middle, norm2_gain.astype(jnp.float32))
    normed_two_low = normed_two.astype(jnp.bfloat16)
    gate_proj = jnp.dot(normed_two_low, gate_weight, preferred_element_type=jnp.float32)
    up_proj = jnp.dot(normed_two_low, up_weight, preferred_element_type=jnp.float32)
    activated, act_pull = jax.vjp(activate, gate_proj, up_proj)
    activated_low = activated.astype(jnp.bfloat16)
    result = middle + jnp.dot(
        activated_low, down_projection_weight, preferred_element_type=jnp.float32
    )
    block_out = result.astype(jnp.bfloat16)[None]
    cotangent_low = out_grad[0]
    grad_down = dot_rows(activated_low, cotangent_low)
    act_grad = dot_cols(cotangent_low, down_projection_weight)
    gate_grad, up_grad = act_pull(act_grad)
    gate_grad_low = gate_grad.astype(jnp.bfloat16)
    up_grad_low = up_grad.astype(jnp.bfloat16)
    grad_gate = dot_rows(normed_two_low, gate_grad_low)
    grad_up = dot_rows(normed_two_low, up_grad_low)
    normed_two_grad = dot_cols(gate_grad_low, gate_weight) + dot_cols(up_grad_low, up_weight)
    middle_norm_grad, grad_gain_two = norm_two_pull(normed_two_grad)
    middle_grad = cotangent_low.astype(jnp.float32) + middle_norm_grad
    branch_grad_low = middle_grad.astype(jnp.bfloat16)
    grad_out = dot_rows(mixed_low, branch_grad_low)
    mixed_grad_low = (
        dot_cols(branch_grad_low, out_weight)
        .astype(jnp.bfloat16)
        .reshape(tok_rows, head_count, head_depth)
    )
    row_dots = jnp.einsum("qhd,qhd->hq", mixed_grad_low.astype(jnp.float32), mixed)
    key_back, value_back = (
        lax.all_gather(key_low, "seq", axis=0, tiled=True),
        lax.all_gather(value_low, "seq", axis=0, tiled=True),
    )
    grads_init = (
        jnp.zeros((tok_rows, head_count, head_depth), jnp.float32),
        jnp.zeros(relative_bias.shape, jnp.float32),
    )

    def backward_block(carry_state, scanned):
        query_grad, table_grad = carry_state
        key_part, value_part, key_groups, key_places = scanned
        one_hot_mask, scores = scores_of(
            query_heads, key_part, own_places, key_places, own_groups, key_groups, relative_bias
        )
        attention = jnp.exp(scores - log_total[..., None])
        grad_weights = jnp.einsum(
            "qhd,khd->hqk", mixed_grad_low, value_part, preferred_element_type=jnp.float32
        )
        score_gradients = (attention * (grad_weights - row_dots[..., None])).astype(jnp.bfloat16)
        query_grad = query_grad + jnp.einsum(
            "hqk,khd->qhd", score_gradients, key_part, preferred_element_type=jnp.float32
        )
        table_grad = table_grad + jnp.einsum(
            "oei,cei->oc", one_hot_mask, score_gradients, preferred_element_type=jnp.float32
        )
        key_grad = jnp.einsum(
            "hqk,qhd->khd", score_gradients, query_heads, preferred_element_type=jnp.float32
        )
        value_grad = jnp.einsum(
            "hqk,qhd->khd",
            attention.astype(jnp.bfloat16),
            mixed_grad_low,
            preferred_element_type=jnp.float32,
        )
        return ((query_grad, table_grad), (key_grad, value_grad))

    (query_grad, table_grad), (key_terms, value_terms) = lax.scan(
        backward_block, grads_init, key_blocks(key_back, value_back)
    )
    key_grad, value_grad = (
        lax.psum_scatter(
            key_terms.reshape(row_length, inner_width), "seq", scatter_dimension=0, tiled=True
        ),
        lax.psum_scatter(
            value_terms.reshape(row_length, inner_width), "seq", scatter_dimension=0, tiled=True
        ),
    )
    query_grad_low = query_grad.reshape(tok_rows, inner_width).astype(jnp.bfloat16)
    key_grad_low = key_grad.astype(jnp.bfloat16)
    value_grad_low = value_grad.astype(jnp.bfloat16)
    grad_query = dot_rows(normed_low, query_grad_low)
    grad_key = dot_rows(normed_low, key_grad_low)
    grad_value = dot_rows(normed_low, value_grad_low)
    normed_grad = (
        dot_cols(query_grad_low, query_weight)
        + dot_cols(key_grad_low, key_weight)
        + dot_cols(value_grad_low, value_weight)
    )
    input_norm_grad, grad_gain_one = norm_pull(normed_grad)
    hidden_grad = (middle_grad + input_norm_grad)[None]
    local_grads = (
        grad_gain_one,
        grad_query,
        grad_key,
        grad_value,
        grad_out,
        table_grad.reshape(-1),
        grad_gain_two,
        grad_gate,
        grad_up,
        grad_down,
    )
    shared = (
        lax.psum_scatter(local_grads[0], "seq", scatter_dimension=0, tiled=True),
        lax.psum_scatter(local_grads[1], "seq", scatter_dimension=0, tiled=True),
        lax.psum_scatter(local_grads[2], "seq", scatter_dimension=0, tiled=True),
        lax.psum_scatter(local_grads[3], "seq", scatter_dimension=0, tiled=True),
        lax.psum_scatter(local_grads[4], "seq", scatter_dimension=0, tiled=True),
        lax.psum_scatter(local_grads[5], "seq", scatter_dimension=0, tiled=True),
        lax.psum_scatter(local_grads[6], "seq", scatter_dimension=0, tiled=True),
        lax.psum_scatter(local_grads[7], "seq", scatter_dimension=0, tiled=True),
        lax.psum_scatter(local_grads[8], "seq", scatter_dimension=0, tiled=True),
        lax.psum_scatter(local_grads[9], "seq", scatter_dimension=0, tiled=True),
    )
    shared = (
        lax.psum(shared[0].astype(jnp.bfloat16), "dp").astype(jnp.float32),
        lax.psum(shared[1].astype(jnp.bfloat16), "dp").astype(jnp.float32),
        lax.psum(shared[2].astype(jnp.bfloat16), "dp").astype(jnp.float32),
        lax.psum(shared[3].astype(jnp.bfloat16), "dp").astype(jnp.float32),
        lax.psum(shared[4].astype(jnp.bfloat16), "dp").astype(jnp.float32),
        lax.psum(shared[5].astype(jnp.bfloat16), "dp").astype(jnp.float32),
        lax.psum(shared[6].astype(jnp.bfloat16), "dp").astype(jnp.float32),
        lax.psum(shared[7].astype(jnp.bfloat16), "dp").astype(jnp.float32),
        lax.psum(shared[8].astype(jnp.bfloat16), "dp").astype(jnp.float32),
        lax.psum(shared[9].astype(jnp.bfloat16), "dp").astype(jnp.float32),
    )
    summed = (
        lax.all_gather(shared[0].astype(jnp.bfloat16), "seq", axis=0, tiled=True).astype(
            jnp.float32
        ),
        lax.all_gather(shared[1].astype(jnp.bfloat16), "seq", axis=0, tiled=True).astype(
            jnp.float32
        ),
        lax.all_gather(shared[2].astype(jnp.bfloat16), "seq", axis=0, tiled=True).astype(
            jnp.float32
        ),
        lax.all_gather(shared[3].astype(jnp.bfloat16), "seq", axis=0, tiled=True).astype(
            jnp.float32
        ),
        lax.all_gather(shared[4].astype(jnp.bfloat16), "seq", axis=0, tiled=True).astype(
            jnp.float32
        ),
        lax.all_gather(shared[5].astype(jnp.bfloat16), "seq", axis=0, tiled=True).astype(
            jnp.float32
        ),
        lax.all_gather(shared[6].astype(jnp.bfloat16), "seq", axis=0, tiled=True).astype(
            jnp.float32
        ),
        lax.all_gather(shared[7].astype(jnp.bfloat16), "seq", axis=0, tiled=True).astype(
            jnp.float32
        ),
        lax.all_gather(shared[8].astype(jnp.bfloat16), "seq", axis=0, tiled=True).astype(
            jnp.float32
        ),
        lax.all_gather(shared[9].astype(jnp.bfloat16), "seq", axis=0, tiled=True).astype(
            jnp.float32
        ),
    )
    return (
        block_out,
        hidden_grad,
        summed[0],
        summed[1],
        summed[2],
        summed[3],
        summed[4],
        summed[5].reshape(relative_bias.shape),
        summed[6],
        summed[7],
        summed[8],
        summed[9],
    )


def solution(mesh):
    placed = (P("dp", "seq", None), P("dp", None)) + (P(),) * 10 + (P("dp", "seq", None),)
    out_specs = (P("dp", "seq", None),) * 2 + (P(),) * 10
    count = mesh.shape["seq"]

    def run(*args):
        hidden, query_weight, relative_bias = args[0], args[3], args[7]
        head_count = relative_bias.shape[1]
        inner = query_weight.shape[1] // count
        fits = (
            mesh.shape["dp"] == 4
            and count % 2 == 0
            and head_count % count == 0
            and inner == LANES
            and hidden.shape[2] == count * LANES
            and hidden.shape[1] == count * LANES
        )
        body = functools.partial(split_shards, count=count) if fits else shards
        return jax.shard_map(
            body, mesh=mesh, in_specs=placed, out_specs=out_specs, check_vma=False
        )(*args)

    return run
```

```python
import functools
import types

import jax
import jax.numpy as jnp
from jax import lax
from jax.experimental import pallas as pl
from jax.experimental.pallas import tpu as pltpu
from jax.sharding import PartitionSpec as P

EPSILON = 1e-06
MASKED = -1e30
THRESHOLDS = (12, 16, 23, 32, 46, 64, 91)
MESH = pl.DeviceIdType.MESH
BF = jnp.bfloat16
F32 = jnp.float32
LANES = 128
ANY = pl.BlockSpec(memory_space=pl.ANY)
VMEM = pl.BlockSpec(memory_space=pltpu.VMEM)
SMEM = pl.BlockSpec(memory_space=pltpu.SMEM)


def bucket_of(relative):
    distance = jnp.abs(relative)
    bucket_level = jnp.full(relative.shape, 8, jnp.int32)
    for boundary in THRESHOLDS:
        bucket_level = bucket_level + (distance >= boundary).astype(jnp.int32)
    near_bucket = jnp.where(distance < 8, distance, bucket_level)
    return near_bucket + 16 * (relative > 0).astype(jnp.int32)


def dot(left_mat, right_mat):
    return jnp.dot(left_mat, right_mat, preferred_element_type=F32)


def dot_rows(left_mat, right_mat):
    return lax.dot_general(
        left_mat, right_mat, (((0,), (0,)), ((), ())), preferred_element_type=F32
    )


def dot_cols(left_mat, right_mat):
    return lax.dot_general(
        left_mat, right_mat, (((1,), (1,)), ((), ())), preferred_element_type=F32
    )


def ring_place(index, count):
    odd = index % 2
    return (1 - odd) * (index // 2) + odd * ((2 * count - 1 - index) // 2)


def ring_index(place, count):
    late = place // (count // 2)
    return (1 - late) * 2 * place + late * (2 * count - 1 - 2 * place)


def greet(targets):
    barrier = pltpu.get_barrier_semaphore()
    for target in targets:
        pl.semaphore_signal(barrier, inc=1, device_id=target, device_id_type=MESH)
    pl.semaphore_wait(barrier, len(targets))


def comm_params(collective_id, vmem=None):
    return pltpu.CompilerParams(
        collective_id=collective_id, has_side_effects=True, vmem_limit_bytes=vmem
    )


class Spot:
    def __init__(self, count):
        self.count = count
        self.half = count // 2
        self.me = lax.axis_index("seq")
        self.dp = lax.axis_index("dp")
        self.place = ring_place(self.me, count)
        self.nexts = tuple((self.dp, self.at(step)) for step in (1, -1))
        self.far_dp = (self.dp + 2) % 4
        self.twin_dp = self.dp + 1 - 2 * (self.dp % 2)
        self.far = (self.far_dp, self.me)
        self.twin = (self.twin_dp, self.me)
        self.others = tuple((self.dp, (self.me + step) % count) for step in range(1, count))

    def at(self, step):
        return ring_index((self.place + (step + self.count) % self.count) % self.count, self.count)

    def back(self, way, hop):
        return self.at(-hop if way == 0 else hop)


def push(source, target, send_sem, recv_sem, device):
    copy = pltpu.make_async_remote_copy(
        src_ref=source,
        dst_ref=target,
        send_sem=send_sem,
        recv_sem=recv_sem,
        device_id=device,
        device_id_type=MESH,
    )
    copy.start()
    return copy


class RingGather:
    def __init__(self, spot, own, into, send_sems, recv_sems):
        self.spot, self.own, self.into = spot, own, into
        self.send_sems, self.recv_sems = send_sems, recv_sems
        self.copies = {}

    def pieces(self, way, hop):
        return (0, 1) if hop < self.spot.half - 1 else (way,)

    def forward(self, hop, way, piece):
        spot = self.spot
        if hop >= spot.half or piece not in self.pieces(way, hop):
            return
        origin = spot.back(way, hop)
        target = self.into(origin, piece)
        self.copies[hop, way, piece] = push(
            self.own(piece) if hop == 0 else target,
            target,
            self.send_sems.at[way, hop, piece],
            self.recv_sems.at[way, hop, piece],
            spot.nexts[way],
        )

    def begin(self):
        for piece in range(2):
            for way in range(2):
                self.forward(0, way, piece)

    def step(self, hop):
        for piece in range(2):
            for way in range(2):
                if (hop, way, piece) in self.copies:
                    self.copies[hop, way, piece].wait_recv()
                    self.forward(hop + 1, way, piece)

    def finish(self):
        for copy in self.copies.values():
            copy.wait_send()


class RingSum:
    def __init__(self, spot, terms, buf, send_sems, recv_sems):
        self.spot, self.terms, self.buf = spot, terms, buf
        self.send_sems, self.recv_sems = send_sems, recv_sems
        self.rows = terms.shape[1] // 2
        self.copies = {}

    def term(self, block, piece):
        return self.terms.at[block, pl.ds(piece * self.rows, self.rows)]

    def send(self, hop, way, piece, source):
        self.copies[hop, way, piece] = push(
            source,
            self.buf.at[way, hop, piece],
            self.send_sems.at[way, hop, piece],
            self.recv_sems.at[way, hop, piece],
            self.spot.nexts[way],
        )

    def block(self, way, hop):
        step = self.spot.half - hop
        return self.spot.at(step if way == 0 else -step)

    def begin(self):
        for way in range(2):
            self.send(0, way, way, self.term(self.block(way, 0), way))
        for way in range(2):
            self.send(1, way, 1 - way, self.term(self.block(way, 1), 1 - way))

    def step(self, hop):
        for piece in range(2):
            for way in range(2):
                if (hop, way, piece) not in self.copies or hop + 1 >= self.spot.half:
                    continue
                self.copies[hop, way, piece].wait_recv()
                term = self.term(self.block(way, hop + 1), piece)
                self.buf[way, hop, piece] = (
                    self.buf[way, hop, piece].astype(F32) + term[...].astype(F32)
                ).astype(BF)
                self.send(hop + 1, way, piece, self.buf.at[way, hop, piece])

    def total(self, out):
        last = self.spot.half - 1
        for piece in range(2):
            value = self.term(self.spot.me, piece)[...].astype(F32)
            for way in range(2):
                self.copies[last, way, piece].wait_recv()
                value = value + self.buf[way, last, piece].astype(F32)
            out[pl.ds(piece * self.rows, self.rows)] = value.astype(BF)

    def finish(self):
        for copy in self.copies.values():
            copy.wait_send()


class PairGather:
    def __init__(self, spot, own_ref, buf, send_sems, recv_sems):
        self.spot, self.buf = spot, buf
        self.send_sems, self.recv_sems = send_sems, recv_sems
        rows = own_ref.shape[0]
        self.low, self.high = pl.ds(0, rows), pl.ds(rows, rows)
        self.far = self.push(1, own_ref, buf.at[1, self.low], spot.far)
        self.near = self.push(0, own_ref, buf.at[0, self.high], spot.twin)

    def push(self, index, source, target, device):
        return push(source, target, self.send_sems.at[index], self.recv_sems.at[index], device)

    def relay(self):
        self.far.wait_recv()
        self.cross = self.push(
            2, self.buf.at[1, self.low], self.buf.at[1, self.high], self.spot.twin
        )

    def finish(self):
        for copy in (self.near, self.far, self.cross):
            copy.wait_send()


class PairSum:
    def __init__(self, spot, kept, outs, ins, far_out, far_in, send_sems, recv_sems):
        self.spot, self.kept, self.outs, self.ins = spot, kept, outs, ins
        self.far_out, self.far_in = far_out, far_in
        self.send_sems, self.recv_sems = send_sems, recv_sems
        self.copies = []

    def near(self, half):
        self.copies.append(
            push(
                self.outs.at[half], self.ins.at[half],
                self.send_sems.at[half], self.recv_sems.at[half], self.spot.twin,
            )
        )

    def over(self):
        self.copies[1].wait_recv()
        self.far_out[...] = (self.kept[1] + self.ins[1].astype(F32)).astype(BF)
        self.copies.append(
            push(
                self.far_out, self.far_in, self.send_sems.at[2], self.recv_sems.at[2], self.spot.far
            )
        )

    def total(self):
        self.copies[0].wait_recv()
        self.copies[2].wait_recv()
        return self.kept[0] + self.ins[0].astype(F32) + self.far_in[...].astype(F32)

    def finish(self):
        for copy in self.copies:
            copy.wait_send()


class MeshGather:
    def __init__(self, spot, x_ref, o_ref, share, sems):
        self.spot, self.x_ref, self.o_ref = spot, x_ref, o_ref
        self.ring_s, self.ring_r, self.x_s, self.x_r, self.core_s, self.core_r = sems
        rows = x_ref.shape[0]
        first = rows * share // 100 // 32 * 32
        cuts = (0, first // 2, first, first + (rows - first) // 2 // 16 * 16, rows)
        self.windows = [
            [pl.ds(cuts[2 * part + piece], cuts[2 * part + piece + 1] - cuts[2 * part + piece]) for piece in range(2)]
            for part in range(2)
        ]
        self.ring, self.x, self.core = {}, {}, {}

    def into(self, dp, origin, part, piece):
        return self.o_ref.at[dp, origin, self.windows[part][piece]]

    def pieces(self, way, hop):
        return (0, 1) if hop < self.spot.half - 1 else (way,)

    def pass_on(self, part, lane, hop, way, piece, source):
        spot = self.spot
        dp = spot.far_dp if lane else spot.dp
        origin = spot.me if way is None else spot.back(way, hop)
        target = self.into(dp, origin, part, piece)
        source = target if source is None else source
        slot = 0 if way is None else 2 * hop - 1 + way
        for onward in (0, 1) if way is None else (way,):
            if hop < spot.half and piece in self.pieces(onward, hop):
                index = (2 * part if lane == 0 else 4) + onward
                self.ring[part, lane, hop, onward, piece] = push(
                    source, target,
                    self.ring_s.at[index, hop, piece], self.ring_r.at[index, hop, piece],
                    spot.nexts[onward],
                )
        if part == 0 and lane == 0:
            self.x[part, slot, piece] = push(
                source, target,
                self.x_s.at[part, slot, piece], self.x_r.at[part, slot, piece], spot.far,
            )
        index = 2 * part + lane
        self.core[part, lane, slot, piece] = push(
            source, target,
            self.core_s.at[index, slot, piece], self.core_r.at[index, slot, piece], spot.twin,
        )

    def begin(self):
        spot = self.spot
        for piece in range(2):
            self.x[1, 0, piece] = push(
                self.x_ref.at[self.windows[1][piece]],
                self.into(spot.dp, spot.me, 1, piece),
                self.x_s.at[1, 0, piece], self.x_r.at[1, 0, piece], spot.far,
            )
        for part in range(2):
            for piece in range(2):
                self.pass_on(part, 0, 0, None, piece, self.x_ref.at[self.windows[part][piece]])

    def begin_far(self):
        for piece in range(2):
            self.x[1, 0, piece].wait_recv()
            self.pass_on(1, 1, 0, None, piece, None)

    def step(self, hop):
        for piece in range(2):
            for part, lane in ((0, 0), (1, 0), (1, 1)):
                for way in range(2):
                    key = (part, lane, hop, way, piece)
                    if key in self.ring:
                        self.ring[key].wait_recv()
                        self.pass_on(part, lane, hop + 1, way, piece, None)

    def step_far(self, hop):
        spot = self.spot
        for piece in range(2):
            for way in (None,) if hop == 0 else range(2):
                slot = 0 if way is None else 2 * hop - 1 + way
                if (0, slot, piece) in self.x:
                    self.x[0, slot, piece].wait_recv()
                    origin = spot.me if way is None else spot.back(way, hop)
                    target = self.into(spot.far_dp, origin, 0, piece)
                    self.core[0, 1, slot, piece] = push(
                        target, target,
                        self.core_s.at[1, slot, piece], self.core_r.at[1, slot, piece], spot.twin,
                    )

    def finish(self):
        for copy in self.core.values():
            copy.wait_recv()
        for copies in (self.ring, self.x, self.core):
            for copy in copies.values():
                copy.wait_send()


def mesh_sems(count):
    half = count // 2
    return [
        pltpu.SemaphoreType.DMA(shape)
        for shape in ((6, half, 2), (2, 2 * half + 1, 2), (4, 2 * half + 1, 2))
        for _ in range(2)
    ]


def near_buckets(rows):
    shape = (rows, rows + 2 * LANES)
    column = lax.broadcasted_iota(jnp.int32, shape, 1) - LANES
    return bucket_of(column - lax.broadcasted_iota(jnp.int32, shape, 0))


def strip_window(step, rows, length):
    return pl.ds(pl.multiple_of(length - rows - step * rows, LANES), length)


def scale_of(value):
    return lax.rsqrt(jnp.mean(value * value, axis=-1, keepdims=True) + EPSILON)


def row_block(origin, rows):
    return pl.ds(pl.multiple_of(origin * rows, rows), rows)


def exclusive(index, bit):
    return index + bit - 2 * bit * ((index // bit) % 2)


def layer_body(count, heads, depth, ff, names, *refs):
    r = types.SimpleNamespace(**dict(zip(names, refs)))
    spot = Spot(count)
    hidden_ref, grad_ref = r.hidden, r.out_grad
    rows, width = hidden_ref.shape
    length = count * rows
    inner = heads * depth
    span = r.gate_w.shape[1]
    odd = spot.dp % 2
    ff_start = pl.multiple_of(spot.dp * ff - odd * (span - ff), span - ff)
    own_columns = pl.ds(pl.multiple_of(spot.me * LANES, LANES), LANES)
    greet(spot.others + (spot.far, spot.twin))

    loads = {}

    def load(name, source, target):
        copy = pltpu.make_async_copy(source, target, r.load_sems.at[len(loads)])
        copy.start()
        loads[name] = copy

    half_rows = rows // 2
    ring = RingGather(
        spot,
        lambda piece: hidden_ref.at[pl.ds(piece * half_rows, half_rows)],
        lambda origin, piece: r.row.at[origin, pl.ds(piece * half_rows, half_rows)],
        r.row_s,
        r.row_r,
    )
    ring.begin()
    cots = PairGather(spot, grad_ref, r.cot, r.cot_s, r.cot_r)
    sources = (r.query_weight, r.key_weight, r.value_weight)
    for part, source in enumerate(sources):
        load(
            part,
            source.at[:, pl.ds(pl.multiple_of(spot.me * inner, inner), inner)],
            r.qkv_w.at[:, pl.ds(part * inner, inner)],
        )
    load("out", r.out_weight, r.out_w)
    ff_columns = pl.ds(pl.multiple_of(ff_start, LANES), span)
    load("gate", r.gate_weight.at[:, ff_columns], r.gate_w)
    load("up", r.up_weight.at[:, ff_columns], r.up_w)
    load("down", r.down_weight.at[pl.ds(ff_start, span)], r.down_w)
    for part, source in enumerate(sources):
        load(3 + part, source, r.full_w.at[part])

    strip, qkv, normed, weights = r.strip, r.qkv, r.normed, r.weights
    low = length - rows - LANES
    bucket = near_buckets(rows)
    near_span = bucket.shape[1]
    table = r.table
    for head in range(heads):
        value = jnp.zeros(bucket.shape, F32)
        for level in range(table.shape[1]):
            value = jnp.where(bucket == level, table[head, level], value)
        strip[head, :, :low] = jnp.full((rows, low), table[head, 15], F32)
        strip[head, :, low : low + near_span] = value
        after = strip.shape[2] - low - near_span
        strip[head, :, low + near_span :] = jnp.full((rows, after), table[head, 31], F32)
    gain_one, gain_two = r.gain_one[...], r.gain_two[...]

    def project(origin, block):
        value = block.astype(F32)
        low_value = (value * scale_of(value) * gain_one).astype(BF)
        mine = row_block(origin, rows)
        normed[mine] = low_value
        qkv[mine] = dot(low_value, r.qkv_w[...]).astype(BF)

    for part in range(3):
        loads[part].wait()
    project(spot.me, hidden_ref[...])
    for hop in range(spot.half):
        ring.step(hop)
        if hop < spot.half - 1:

            def both(side, carry, hop=hop):
                origin = spot.at((1 - 2 * side) * (hop + 1))
                project(origin, r.row[origin])
                return carry

            lax.fori_loop(0, 2, both, 0)
        else:
            origin = spot.at(spot.half)
            project(origin, r.row[origin])
    cots.relay()
    r.cot[0, :rows] = grad_ref[...]
    mixed_heads, mixed = r.mixed_heads, r.mixed

    def attend(target):
        mine = row_block(target, rows)
        same = r.column_ids[mine] == r.row_ids[...]
        window = strip_window(target, rows, length)
        for head in range(heads):
            columns = slice(head * depth, (head + 1) * depth)
            key = qkv[:, inner + head * depth : inner + (head + 1) * depth]
            value = qkv[:, 2 * inner + head * depth : 2 * inner + (head + 1) * depth]
            scores = dot_cols(qkv[mine, columns], key) + strip[head, :, window]
            scores = jnp.where(same, scores, MASKED)
            top = jnp.max(scores, axis=1, keepdims=True)
            weight = jnp.exp(scores - top)
            weight = weight * (1.0 / jnp.sum(weight, axis=1, keepdims=True))
            weight = weight.astype(BF)
            weights[head, mine] = weight
            mixed_heads[mine, columns] = dot(weight, value).astype(BF)

    def mixed_copy(step):
        target = (spot.me + step) % count
        return pltpu.make_async_remote_copy(
            src_ref=mixed_heads.at[row_block(target, rows)],
            dst_ref=mixed.at[:, own_columns],
            send_sem=r.mixed_s.at[step - 1],
            recv_sem=r.mixed_r.at[step - 1],
            device_id=(spot.dp, target),
            device_id_type=MESH,
        )

    def attend_and_send(step, carry):
        attend((spot.me + step) % count)
        mixed_copy(step).start()
        return carry

    lax.fori_loop(1, count, attend_and_send, 0)
    attend(spot.me)
    mixed[:, own_columns] = mixed_heads[row_block(spot.me, rows)]
    mixed_copies = [mixed_copy(step) for step in range(1, count)]

    loads["out"].wait()
    for copy in mixed_copies:
        copy.wait_recv()
    inputs = hidden_ref[...].astype(F32)
    middle_ref = r.middle
    middle = inputs + dot(mixed[...], r.out_w[...])
    middle_ref[...] = middle
    tok, cot = r.tok, r.cot
    tok[0, :rows] = (middle * scale_of(middle) * gain_two).astype(BF)
    toks = PairGather(spot, tok.at[0, pl.ds(0, rows)], tok, r.tok_s, r.tok_r)
    gate_w, up_w, down_w = r.gate_w, r.up_w, r.down_w
    act, gate_g, up_g = r.act, r.gate_g, r.up_g
    for name in ("gate", "up", "down"):
        loads[name].wait()
    both_rows = 2 * rows
    chunk = 256
    grads = PairSum(
        spot, r.grad_kept, r.grad_outs, r.grad_ins, r.grad_far_out, r.grad_far_in,
        r.grad_s, r.grad_r,
    )
    outs = PairSum(
        spot, r.out_kept, r.out_outs, r.out_ins, r.out_far_out, r.out_far_in,
        r.out_s, r.out_r,
    )

    def activate_half(half):
        mine = pl.ds(half * both_rows, both_rows)

        def tile(index, carry):
            columns = row_block(index, chunk)
            gate = dot(tok[half], gate_w[:, columns])
            up = dot(tok[half], up_w[:, columns])
            act_grad = dot_cols(cot[half], down_w[columns])
            place = index * chunk + lax.broadcasted_iota(jnp.int32, (1, chunk), 1)
            place = place - odd * (span - ff)
            inside = (place >= 0) & (place < ff)
            root = 0.7978845608028654
            squared = gate * gate
            bend = jnp.tanh(root * (gate + 0.044715 * gate * squared))
            share = 0.5 * (1.0 + bend)
            gelu = gate * share
            slope = share + 0.5 * gate * (1.0 - bend * bend) * root * (
                1.0 + 3 * 0.044715 * squared
            )
            act[mine, columns] = jnp.where(inside, gelu * up, 0.0).astype(BF)
            gate_g[mine, columns] = jnp.where(inside, act_grad * up * slope, 0.0).astype(BF)
            up_g[mine, columns] = jnp.where(inside, act_grad * gelu, 0.0).astype(BF)
            return carry

        lax.fori_loop(0, span // chunk, tile, 0)

    def spread(pair_sum, half, product):
        def tile(index, carry):
            columns = row_block(index, chunk)
            value = product(columns)
            pair_sum.kept[half, :, columns] = value[:rows]
            pair_sum.outs[half, :, columns] = value[rows:].astype(BF)
            return carry

        lax.fori_loop(0, width // chunk, tile, 0)
        pair_sum.near(half)

    def back_half(half):
        mine = pl.ds(half * both_rows, both_rows)
        spread(
            grads,
            half,
            lambda columns: dot_cols(gate_g[mine], gate_w[columns])
            + dot_cols(up_g[mine], up_w[columns]),
        )

    def out_half(half):
        mine = pl.ds(half * both_rows, both_rows)
        spread(outs, half, lambda columns: dot(act[mine], down_w[:, columns]))

    cots.near.wait_recv()
    cots.cross.wait_recv()
    toks.near.wait_recv()
    activate_half(0)
    toks.relay()
    back_half(0)
    toks.cross.wait_recv()
    activate_half(1)
    back_half(1)

    down_terms, pair_terms = r.down_terms, r.pair_terms
    spare = span - ff

    def down_tile(index, carry):
        columns = row_block(index, LANES)
        value = dot_rows(act[:both_rows], cot[0, :, columns]) + dot_rows(
            act[both_rows:], cot[1, :, columns]
        )
        down_terms[index] = jnp.where(odd == 1, value[spare:], value[:ff]).astype(BF)
        return carry

    lax.fori_loop(0, count, down_tile, 0)
    down_sum = RingSum(spot, down_terms, r.down_buf, r.down_s, r.down_r)
    down_sum.begin()
    grads.over()
    full = ff // LANES
    lane = lax.broadcasted_iota(jnp.int32, (LANES, LANES), 1)

    def pair_tile(index, carry):
        columns = row_block(index, LANES)
        parts = []
        for source in (gate_g, up_g):
            parts.append(
                dot_rows(tok[0, :, columns], source[:both_rows])
                + dot_rows(tok[1, :, columns], source[both_rows:])
            )
        cut = lambda value, place: value[:, place * LANES : (place + 1) * LANES]
        for part, value in enumerate(parts):
            for place in range(full):
                start = (part * full + place) * LANES
                pair_terms[index, start : start + LANES] = jnp.where(
                    odd == 1, cut(value, place + 1), cut(value, place)
                ).astype(BF)
        edges = [jnp.where(odd == 1, cut(value, 0), cut(value, full)) for value in parts]
        turned = pltpu.roll(edges[1], LANES // 2, 1)
        lower = (lane < LANES // 2).astype(jnp.int32)
        pair_terms[index, 2 * full * LANES :] = jnp.where(lower == odd, turned, edges[0]).astype(BF)
        return carry

    lax.fori_loop(0, count, pair_tile, 0)
    pair_sum = RingSum(spot, pair_terms, r.pair_buf, r.pair_s, r.pair_r)
    pair_sum.begin()
    down_sum.step(0)
    out_half(0)
    out_half(1)

    normed_two_grad = grads.total()
    middle = middle_ref[...]
    scale_two = scale_of(middle)
    lifted = gain_two * normed_two_grad
    middle_grad = (
        grad_ref[...].astype(F32)
        + scale_two * lifted
        - middle * (scale_two * scale_two * scale_two)
        * jnp.mean(middle * lifted, axis=-1, keepdims=True)
    )
    middle_grad_ref = r.middle_grad
    middle_grad_ref[...] = middle_grad
    small = r.small
    small[...] = jnp.zeros_like(small)
    gain_grad = jnp.sum(normed_two_grad * middle * scale_two, axis=0, keepdims=True)
    tiles = width // LANES
    for tile in range(tiles):
        small[tiles + tile : tiles + tile + 1] = gain_grad[:, tile * LANES : (tile + 1) * LANES]
    branch, own_branch = r.branch, r.own_branch
    own_branch[...] = middle_grad.astype(BF)
    branches = RingGather(
        spot,
        lambda piece: own_branch.at[pl.ds(piece * half_rows, half_rows)],
        lambda origin, piece: branch.at[origin, pl.ds(piece * half_rows, half_rows)],
        r.branch_s,
        r.branch_r,
    )
    branches.begin()
    branch[spot.me] = own_branch[...]
    outs.over()

    keys, values, dqkv = r.keys, r.values, r.dqkv
    strip[...] = jnp.zeros_like(strip)
    keys[...] = jnp.zeros_like(keys)
    values[...] = jnp.zeros_like(values)
    own_out = r.out_w.at[row_block(spot.me, inner)]

    def attend_back(origin):
        mine = row_block(origin, rows)
        window = strip_window(origin, rows, length)
        mixed_grad = dot_cols(branch[origin], own_out[...]).astype(BF)
        for head in range(heads):
            columns = slice(head * depth, (head + 1) * depth)
            key = qkv[:, inner + head * depth : inner + (head + 1) * depth]
            value = qkv[:, 2 * inner + head * depth : 2 * inner + (head + 1) * depth]
            grad = mixed_grad[:, columns]
            weight_low = weights[head, mine]
            weight = weight_low.astype(F32)
            scaled = weight * dot_cols(grad, value)
            score_grad = scaled - weight * jnp.sum(scaled, axis=1, keepdims=True)
            strip[head, :, window] += score_grad
            score_low = score_grad.astype(BF)
            dqkv[mine, columns] = dot(score_low, key).astype(BF)
            keys[:, columns] += dot_rows(score_low, qkv[mine, columns])
            values[:, columns] += dot_rows(weight_low, grad)

    down_sum.step(1)
    attend_back(spot.me)
    pair_sum.step(0)
    block_out = middle + outs.total()
    r.block_out[...] = block_out.astype(BF)
    mesh_sets = [r.gather_sems[6 * index : 6 * index + 6] for index in range(3)]
    for hop in range(spot.half):
        branches.step(hop)
        if hop == 0:
            down_sum.step(2)
        if hop == 1:
            down_sum.total(r.down_block)
            down = MeshGather(spot, r.down_block, r.down_all, SHARES[0], mesh_sets[0])
            down.begin()
            load("down_own", r.down_block, r.down_all.at[spot.dp, spot.me])
        if hop:
            pair_sum.step(hop)
        if hop == 2:
            down.begin_far()
        if hop < spot.half - 1:

            def both_back(side, carry, hop=hop):
                attend_back(spot.at((1 - 2 * side) * (hop + 1)))
                return carry

            lax.fori_loop(0, 2, both_back, 0)
        else:
            attend_back(spot.at(spot.half))
        if hop >= 2:
            down.step(hop - 2)
            down.step_far(hop - 2)

    dqkv[:, inner : 2 * inner] = keys[...].astype(BF)
    dqkv[:, 2 * inner :] = values[...].astype(BF)
    own_dqkv = r.own_dqkv
    trades = []
    for index, device in enumerate(spot.others):
        for part in range(3):
            trades.append(
                push(
                    dqkv.at[row_block(device[1], rows), pl.ds(part * LANES, LANES)],
                    own_dqkv.at[part, :, own_columns],
                    r.trade_s.at[index, part],
                    r.trade_r.at[index, part],
                    device,
                )
            )
    for part in range(3):
        own_dqkv[part, :, own_columns] = dqkv[
            row_block(spot.me, rows), part * LANES : (part + 1) * LANES
        ]
    pair_sum.total(r.pair_block)
    pair = MeshGather(spot, r.pair_block, r.pair_all, SHARES[1], mesh_sets[1])
    pair.begin()
    load("pair_own", r.pair_block, r.pair_all.at[spot.dp, spot.me])

    packed = r.packed
    quarter, slim = width // 4, inner // 4

    def quarter_block(index, carry):
        block = dot_rows(normed[:, row_block(index, quarter)], dqkv[...])
        for part in range(3):
            packed[index, part * quarter : (part + 1) * quarter] = block[
                :, part * LANES : (part + 1) * LANES
            ]
        return carry

    lax.fori_loop(0, 4, quarter_block, 0)
    for hop in (2, 3):
        down.step(hop)
        down.step_far(hop)

    def out_tile(tile, carry):
        terms = jnp.zeros((inner, LANES), F32)
        for source in range(count):
            terms = terms + dot_rows(
                mixed_heads[source * rows : (source + 1) * rows],
                branch[source, :, row_block(tile, LANES)],
            )
        for index in range(4):
            base = pl.multiple_of(3 * quarter + tile * slim, slim)
            packed[index, pl.ds(base, slim)] = terms[index * slim : (index + 1) * slim]
        return carry

    lax.fori_loop(0, tiles, out_tile, 0)
    core, side = odd, spot.dp // 2
    for index in range(2):
        r.near_out[index] = packed[2 * index + 1 - core].astype(BF)
    near = push(r.near_out, r.near_in, r.proj_s.at[0], r.proj_r.at[0], spot.twin)
    pair.begin_far()
    down.step_far(spot.half)
    near.wait_recv()
    r.far_out[...] = (
        packed[2 * (1 - side) + core] + r.near_in[1 - side].astype(F32)
    ).astype(BF)
    far = push(r.far_out, r.far_in, r.proj_s.at[1], r.proj_r.at[1], spot.far)
    pair.step(0)
    pair.step_far(0)
    far.wait_recv()
    r.proj_block[...] = (
        packed[2 * side + core] + r.near_in[side].astype(F32) + r.far_in[...].astype(F32)
    ).astype(BF)
    proj = MeshGather(spot, r.proj_block, r.proj_all, SHARES[2], mesh_sets[2])
    proj.begin()
    load("proj_own", r.proj_block, r.proj_all.at[spot.dp, spot.me])

    for head in range(heads):
        middle_part = strip[head, :, low : low + near_span]
        before = jnp.sum(strip[head, :, :low], axis=0, keepdims=True)
        after = jnp.sum(strip[head, :, low + near_span :], axis=0, keepdims=True)
        levels = []
        for level in range(table.shape[1]):
            part = jnp.sum(jnp.where(bucket == level, middle_part, 0.0), axis=0, keepdims=True)
            line = part[:, :LANES]
            for tile in range(1, near_span // LANES):
                line = line + part[:, tile * LANES : (tile + 1) * LANES]
            edge = before if level == 15 else after if level == 31 else None
            if edge is not None:
                for tile in range(edge.shape[1] // LANES):
                    line = line + edge[:, tile * LANES : (tile + 1) * LANES]
            r.levels[level : level + 1] = line
        sums = lax.dot_general(
            jnp.ones((8, LANES), F32),
            r.levels[...],
            (((1,), (1,)), ((), ())),
            precision=lax.Precision.HIGHEST,
            preferred_element_type=F32,
        )
        small[pl.ds(2 * tiles + spot.me * heads + head, 1), : table.shape[1]] = sums[:1]

    pair.step(1)
    proj.begin_far()
    pair.step_far(1)
    for part in range(3):
        loads[3 + part].wait()
    for copy in trades:
        copy.wait_recv()
    normed_grad = dot_cols(own_dqkv[0], r.full_w[0])
    for part in range(1, 3):
        normed_grad = normed_grad + dot_cols(own_dqkv[part], r.full_w[part])
    inputs = hidden_ref[...].astype(F32)
    scale_one = scale_of(inputs)
    raised = gain_one * normed_grad
    r.hidden_grad[...] = (
        middle_grad_ref[...]
        + scale_one * raised
        - inputs * (scale_one * scale_one * scale_one)
        * jnp.mean(inputs * raised, axis=-1, keepdims=True)
    )
    gain_grad = jnp.sum(normed_grad * inputs * scale_one, axis=0, keepdims=True)
    for tile in range(tiles):
        small[tile : tile + 1] = gain_grad[:, tile * LANES : (tile + 1) * LANES]

    partners = [spot.twin, spot.far]
    bit = 1
    while bit < count:
        partners.append((spot.dp, exclusive(spot.me, bit)))
        bit *= 2
    small_out, small_in = r.small_out, r.small_in
    small_copies = []

    def small_send():
        index = len(small_copies)
        if index < len(partners):
            small_out[index] = small[...]
            small_copies.append(
                push(
                    small_out.at[index], small_in.at[index],
                    r.small_s.at[index], r.small_r.at[index], partners[index],
                )
            )

    def small_step():
        if len(small_copies) <= len(partners) and small_copies:
            index = len(small_copies) - 1
            small_copies[index].wait_recv()
            small[...] += small_in[index]
            small_send()

    small_send()
    for hop in range(2, spot.half):
        pair.step(hop)
        pair.step_far(hop)
        small_step()
        proj.step(hop - 2)
        proj.step_far(hop - 2)
    pair.step_far(spot.half)
    small_step()
    for hop in range(spot.half - 2, spot.half):
        proj.step(hop)
        proj.step_far(hop)
        small_step()
    proj.step_far(spot.half)
    r.small_sum[...] = small[...]
    for name in ("down_own", "pair_own", "proj_own"):
        loads[name].wait()
    for copy in mixed_copies + trades + [near, far] + small_copies:
        copy.wait_send()
    for item in (ring, cots, toks, grads, outs, down_sum, pair_sum, branches, down, pair, proj):
        item.finish()


SHARES = (80, 70, 57)


def layer(arrays, count, heads, depth, ff):
    rows, width = arrays["hidden"].shape
    length = count * rows
    inner = heads * depth
    half = count // 2
    span = (ff + LANES - 1) // LANES * LANES
    pair_rows = 2 * ff // LANES * rows
    proj_rows = 3 * (width // 4) + inner // 4 * (width // LANES)
    small_rows = 2 * (width // LANES) + count * heads
    steps = 2 + (count - 1).bit_length()
    dma = pltpu.SemaphoreType.DMA
    specs = dict(
        hidden=VMEM,
        out_grad=VMEM,
        gain_one=VMEM,
        gain_two=VMEM,
        column_ids=VMEM,
        row_ids=VMEM,
        table=SMEM,
    )
    shape = jax.ShapeDtypeStruct
    results = dict(
        block_out=(shape((rows, width), BF), VMEM),
        hidden_grad=(shape((rows, width), F32), VMEM),
        small_sum=(shape((small_rows, LANES), F32), VMEM),
        down_all=(shape((4, count, ff, LANES), BF), ANY),
        pair_all=(shape((4, count, pair_rows, LANES), BF), ANY),
        proj_all=(shape((4, count, proj_rows, LANES), BF), ANY),
    )
    vm = pltpu.VMEM
    ring_buf = lambda n: vm((2, half, 2, n // 2, LANES), BF)
    pairs = {}
    for name in ("grad", "out"):
        pairs[name + "_kept"] = vm((2, rows, width), F32)
        pairs[name + "_outs"] = vm((2, rows, width), BF)
        pairs[name + "_ins"] = vm((2, rows, width), BF)
        pairs[name + "_far_out"] = vm((rows, width), BF)
        pairs[name + "_far_in"] = vm((rows, width), BF)
        pairs[name + "_s"] = dma((3,))
        pairs[name + "_r"] = dma((3,))
    for name in ("cot", "tok"):
        pairs[name] = vm((2, 2 * rows, width), BF)
        pairs[name + "_s"] = dma((3,))
        pairs[name + "_r"] = dma((3,))
    for name in ("row", "branch"):
        pairs[name] = vm((count, rows, width), BF)
        pairs[name + "_s"] = dma((2, half, 2))
        pairs[name + "_r"] = dma((2, half, 2))
    for name, size in (("down", ff), ("pair", pair_rows)):
        pairs[name + "_terms"] = vm((count, size, LANES), BF)
        pairs[name + "_buf"] = ring_buf(size)
        pairs[name + "_block"] = vm((size, LANES), BF)
        pairs[name + "_s"] = dma((2, half, 2))
        pairs[name + "_r"] = dma((2, half, 2))
    scratch = dict(
        **pairs,
        strip=vm((heads, rows, 2 * length - rows), F32),
        normed=vm((length, width), BF),
        qkv=vm((length, 3 * inner), BF),
        weights=vm((heads, length, length), BF),
        mixed_heads=vm((length, inner), BF),
        mixed=vm((rows, width), BF),
        qkv_w=vm((width, 3 * inner), BF),
        full_w=vm((3, width, width), BF),
        out_w=vm((width, width), BF),
        gate_w=vm((width, span), BF),
        up_w=vm((width, span), BF),
        down_w=vm((span, width), BF),
        middle=vm((rows, width), F32),
        middle_grad=vm((rows, width), F32),
        act=vm((4 * rows, span), BF),
        gate_g=vm((4 * rows, span), BF),
        up_g=vm((4 * rows, span), BF),
        own_branch=vm((rows, width), BF),
        keys=vm((length, inner), F32),
        values=vm((length, inner), F32),
        dqkv=vm((length, 3 * inner), BF),
        own_dqkv=vm((3, rows, width), BF),
        packed=vm((4, proj_rows, LANES), F32),
        near_out=vm((2, proj_rows, LANES), BF),
        near_in=vm((2, proj_rows, LANES), BF),
        far_out=vm((proj_rows, LANES), BF),
        far_in=vm((proj_rows, LANES), BF),
        proj_block=vm((proj_rows, LANES), BF),
        levels=vm((arrays["table"].shape[1], LANES), F32),
        small=vm((small_rows, LANES), F32),
        small_out=vm((steps, small_rows, LANES), F32),
        small_in=vm((steps, small_rows, LANES), F32),
        load_sems=dma((16,)),
        mixed_s=dma((count - 1,)),
        mixed_r=dma((count - 1,)),
        trade_s=dma((count - 1, 3)),
        trade_r=dma((count - 1, 3)),
        proj_s=dma((2,)),
        proj_r=dma((2,)),
        small_s=dma((steps,)),
        small_r=dma((steps,)),
    )
    names = tuple(arrays) + tuple(results) + tuple(scratch)

    def body(*refs):
        plain = refs[: len(names)]
        layer_body(
            count, heads, depth, ff, names + ("gather_sems",), *plain, refs[len(names) :]
        )

    outs = pl.pallas_call(
        body,
        name="layer",
        out_shape=tuple(value[0] for value in results.values()),
        in_specs=[specs.get(name, ANY) for name in arrays],
        out_specs=tuple(value[1] for value in results.values()),
        scratch_shapes=list(scratch.values()) + mesh_sems(count) * 3,
        compiler_params=comm_params(0, 60 << 20),
    )(*arrays.values())
    return types.SimpleNamespace(**dict(zip(results, outs)))


def widen_pair_body(part, x_ref, gate_ref, up_ref):
    rows = gate_ref.shape[0]
    full, half = part // LANES, LANES // 2
    for dp in range(x_ref.shape[0]):
        base = dp * part
        shift = half if dp % 2 else 0
        for which, o_ref in enumerate((gate_ref, up_ref)):
            for tile in range(full):
                start = (which * full + tile) * rows
                column = base + shift + tile * LANES
                o_ref[:, column : column + LANES] = x_ref[dp, 0, start : start + rows].astype(F32)
        edge = x_ref[dp, 0, 2 * full * rows :].astype(F32)
        column = base if dp % 2 else base + full * LANES
        gate_half = slice(half, LANES) if dp % 2 else slice(0, half)
        up_half = slice(0, half) if dp % 2 else slice(half, LANES)
        gate_ref[:, column : column + half] = edge[:, gate_half]
        up_ref[:, column : column + half] = edge[:, up_half]


def widen_pair(gathered, rows, part):
    dps, count, size = gathered.shape[:3]
    shape = jax.ShapeDtypeStruct((count * rows, dps * part), F32)
    spec = pl.BlockSpec((rows, dps * part), lambda i: (i, 0))
    return pl.pallas_call(
        functools.partial(widen_pair_body, part),
        name="widen_pair",
        grid=(count,),
        out_shape=(shape, shape),
        in_specs=[pl.BlockSpec((dps, 1, size, LANES), lambda i: (0, i, 0, 0))],
        out_specs=(spec, spec),
        compiler_params=pltpu.CompilerParams(vmem_limit_bytes=48 << 20),
    )(gathered)


def widen_columns_body(x_ref, *o_refs):
    rows = o_refs[0].shape[0]
    for index, o_ref in enumerate(o_refs):
        for source in range(x_ref.shape[1]):
            o_ref[:, source * LANES : (source + 1) * LANES] = x_ref[
                0, source, index * rows : (index + 1) * rows
            ].astype(F32)


def widen_columns(gathered, first, rows, outs, pieces):
    dps, count = gathered.shape[:2]
    size = rows // pieces
    shape = jax.ShapeDtypeStruct((dps * rows, count * LANES), F32)
    spec = pl.BlockSpec((size, count * LANES), lambda i, k: (i * pieces + k, 0))
    base = first // (size * outs)
    return pl.pallas_call(
        widen_columns_body,
        name="widen_columns",
        grid=(dps, pieces),
        out_shape=(shape,) * outs,
        in_specs=[
            pl.BlockSpec((1, count, size * outs, LANES), lambda i, k: (i, 0, base + k, 0))
        ],
        out_specs=(spec,) * outs,
        compiler_params=pltpu.CompilerParams(vmem_limit_bytes=48 << 20),
    )(gathered)


def widen_rows_body(x_ref, o_ref):
    dps, _, size, _ = x_ref.shape
    tiles = o_ref.shape[1] // LANES
    rows = size // tiles
    for dp in range(dps):
        for tile in range(tiles):
            o_ref[dp * rows : (dp + 1) * rows, tile * LANES : (tile + 1) * LANES] = x_ref[
                dp, 0, tile * rows : (tile + 1) * rows
            ].astype(F32)


def widen_rows(gathered, first, rows, width):
    dps, count = gathered.shape[:2]
    size = rows * (width // LANES)
    base = first // size
    return pl.pallas_call(
        widen_rows_body,
        name="widen_rows",
        grid=(count,),
        out_shape=jax.ShapeDtypeStruct((count * dps * rows, width), F32),
        in_specs=[pl.BlockSpec((dps, 1, size, LANES), lambda i: (0, i, base, 0))],
        out_specs=pl.BlockSpec((dps * rows, width), lambda i: (i, 0)),
    )(gathered)


def split_shards(
    hidden,
    group_ids,
    norm1_gain,
    query_weight,
    key_weight,
    value_weight,
    out_weight,
    relative_bias,
    norm2_gain,
    gate_weight,
    up_weight,
    down_projection_weight,
    out_grad,
    *,
    count,
):
    width = hidden.shape[2]
    levels, head_count = relative_bias.shape
    depth = query_weight.shape[1] // head_count
    heads = head_count // count
    ff = gate_weight.shape[1] // 4
    me = lax.axis_index("seq")
    table = lax.dynamic_slice_in_dim(relative_bias, me * heads, heads, axis=1).T.astype(F32)
    arrays = dict(
        hidden=hidden[0],
        out_grad=out_grad[0],
        gain_one=norm1_gain.astype(F32)[None],
        gain_two=norm2_gain.astype(F32)[None],
        column_ids=group_ids[0][:, None],
        row_ids=group_ids,
        table=table,
        query_weight=query_weight,
        key_weight=key_weight,
        value_weight=value_weight,
        out_weight=out_weight,
        gate_weight=gate_weight,
        up_weight=up_weight,
        down_weight=down_projection_weight,
    )
    out = layer(arrays, count, heads, depth, ff)
    quarter, slim = width // 4, heads * depth // 4
    gate_grad, up_grad = widen_pair(out.pair_all, width // count, ff)
    (down_grad,) = widen_columns(out.down_all, 0, ff, 1, 2)
    query_grad, key_grad, value_grad = widen_columns(out.proj_all, 0, quarter, 3, 1)
    out_weight_grad = widen_rows(out.proj_all, 3 * quarter, slim, width)
    small = out.small_sum
    tiles = width // LANES
    return (
        out.block_out[None],
        out.hidden_grad[None],
        small[:tiles].reshape(-1),
        query_grad,
        key_grad,
        value_grad,
        out_weight_grad,
        small[2 * tiles :, :levels].T,
        small[tiles : 2 * tiles].reshape(-1),
        gate_grad,
        up_grad,
        down_grad,
    )


def rms_norm(vector, norm_gain):
    return (
        vector * lax.rsqrt(jnp.mean(vector * vector, axis=-1, keepdims=True) + EPSILON) * norm_gain
    )


def activate(gate_proj, up_proj):
    return jax.nn.gelu(gate_proj, approximate=True) * up_proj


def scores_of(
    query_part, key_part, query_places, key_places, query_groups, key_groups, bias_lookup
):
    bucket = bucket_of(key_places[None, :] - query_places[:, None])
    levels = jnp.arange(bias_lookup.shape[0], dtype=jnp.int32)
    one_hot_mask = (bucket[None] == levels[:, None, None]).astype(jnp.bfloat16)
    bias_patch_block = jnp.einsum(
        "ctf,cx->xtf", one_hot_mask, bias_lookup, preferred_element_type=jnp.float32
    )
    raw_scores = (
        jnp.einsum("qhd,khd->hqk", query_part, key_part, preferred_element_type=jnp.float32)
        + bias_patch_block
    )
    same_group = query_groups[:, None] == key_groups[None, :]
    return (one_hot_mask, jnp.where(same_group[None], raw_scores, MASKED))


def shards(
    hidden,
    group_ids,
    norm1_gain,
    query_weight,
    key_weight,
    value_weight,
    out_weight,
    relative_bias,
    norm2_gain,
    gate_weight,
    up_weight,
    down_projection_weight,
    out_grad,
):
    tok_rows = hidden.shape[1]
    head_count = relative_bias.shape[1]
    inner_width = query_weight.shape[1]
    head_depth = inner_width // head_count
    row_length = group_ids.shape[1]
    row_start = lax.axis_index("seq") * tok_rows
    key_block = min(1024, row_length)
    block_count = row_length // key_block
    row_groups = group_ids[0]
    own_groups = lax.dynamic_slice_in_dim(row_groups, row_start, tok_rows)
    own_places = row_start + jnp.arange(tok_rows, dtype=jnp.int32)
    all_places = jnp.arange(row_length, dtype=jnp.int32)

    def key_blocks(key_rows, value_rows):
        return (
            key_rows.reshape(block_count, key_block, head_count, head_depth),
            value_rows.reshape(block_count, key_block, head_count, head_depth),
            row_groups.reshape(block_count, key_block),
            all_places.reshape(block_count, key_block),
        )

    inputs = hidden[0].astype(jnp.float32)
    normed, norm_pull = jax.vjp(rms_norm, inputs, norm1_gain.astype(jnp.float32))
    normed_low = normed.astype(jnp.bfloat16)
    query_low = jnp.dot(normed_low, query_weight, preferred_element_type=jnp.float32).astype(
        jnp.bfloat16
    )
    key_low = jnp.dot(normed_low, key_weight, preferred_element_type=jnp.float32).astype(
        jnp.bfloat16
    )
    value_low = jnp.dot(normed_low, value_weight, preferred_element_type=jnp.float32).astype(
        jnp.bfloat16
    )
    key_all, value_all = (
        lax.all_gather(key_low, "seq", axis=0, tiled=True),
        lax.all_gather(value_low, "seq", axis=0, tiled=True),
    )
    query_heads = query_low.reshape(tok_rows, head_count, head_depth)

    def gather_stats(carry_state, scanned):
        running_max, running_sum = carry_state
        key_part, value_part, key_groups, key_places = scanned
        one_hot_mask, scores = scores_of(
            query_heads, key_part, own_places, key_places, own_groups, key_groups, relative_bias
        )
        new_max = jnp.maximum(running_max, jnp.max(scores, axis=-1))
        running_sum = running_sum * jnp.exp(running_max - new_max) + jnp.sum(
            jnp.exp(scores - new_max[..., None]), axis=-1
        )
        return ((new_max, running_sum), None)

    stats_init = (
        jnp.full((head_count, tok_rows), MASKED, jnp.float32),
        jnp.zeros((head_count, tok_rows), jnp.float32),
    )
    (running_max, running_sum), _ = lax.scan(
        gather_stats, stats_init, key_blocks(key_all, value_all)
    )
    log_total = running_max + jnp.log(running_sum)

    def gather_values(summed, scanned):
        key_part, value_part, key_groups, key_places = scanned
        one_hot_mask, scores = scores_of(
            query_heads, key_part, own_places, key_places, own_groups, key_groups, relative_bias
        )
        attention_low = jnp.exp(scores - log_total[..., None]).astype(jnp.bfloat16)
        return (
            summed
            + jnp.einsum(
                "hqk,khd->qhd", attention_low, value_part, preferred_element_type=jnp.float32
            ),
            None,
        )

    mixed, _ = lax.scan(
        gather_values,
        jnp.zeros((tok_rows, head_count, head_depth), jnp.float32),
        key_blocks(key_all, value_all),
    )
    mixed_low = mixed.reshape(tok_rows, inner_width).astype(jnp.bfloat16)
    middle = inputs + jnp.dot(mixed_low, out_weight, preferred_element_type=jnp.float32)
    normed_two, norm_two_pull = jax.vjp(rms_norm, middle, norm2_gain.astype(jnp.float32))
    normed_two_low = normed_two.astype(jnp.bfloat16)
    gate_proj = jnp.dot(normed_two_low, gate_weight, preferred_element_type=jnp.float32)
    up_proj = jnp.dot(normed_two_low, up_weight, preferred_element_type=jnp.float32)
    activated, act_pull = jax.vjp(activate, gate_proj, up_proj)
    activated_low = activated.astype(jnp.bfloat16)
    result = middle + jnp.dot(
        activated_low, down_projection_weight, preferred_element_type=jnp.float32
    )
    block_out = result.astype(jnp.bfloat16)[None]
    cotangent_low = out_grad[0]
    grad_down = dot_rows(activated_low, cotangent_low)
    act_grad = dot_cols(cotangent_low, down_projection_weight)
    gate_grad, up_grad = act_pull(act_grad)
    gate_grad_low = gate_grad.astype(jnp.bfloat16)
    up_grad_low = up_grad.astype(jnp.bfloat16)
    grad_gate = dot_rows(normed_two_low, gate_grad_low)
    grad_up = dot_rows(normed_two_low, up_grad_low)
    normed_two_grad = dot_cols(gate_grad_low, gate_weight) + dot_cols(up_grad_low, up_weight)
    middle_norm_grad, grad_gain_two = norm_two_pull(normed_two_grad)
    middle_grad = cotangent_low.astype(jnp.float32) + middle_norm_grad
    branch_grad_low = middle_grad.astype(jnp.bfloat16)
    grad_out = dot_rows(mixed_low, branch_grad_low)
    mixed_grad_low = (
        dot_cols(branch_grad_low, out_weight)
        .astype(jnp.bfloat16)
        .reshape(tok_rows, head_count, head_depth)
    )
    row_dots = jnp.einsum("qhd,qhd->hq", mixed_grad_low.astype(jnp.float32), mixed)
    key_back, value_back = (
        lax.all_gather(key_low, "seq", axis=0, tiled=True),
        lax.all_gather(value_low, "seq", axis=0, tiled=True),
    )
    grads_init = (
        jnp.zeros((tok_rows, head_count, head_depth), jnp.float32),
        jnp.zeros(relative_bias.shape, jnp.float32),
    )

    def backward_block(carry_state, scanned):
        query_grad, table_grad = carry_state
        key_part, value_part, key_groups, key_places = scanned
        one_hot_mask, scores = scores_of(
            query_heads, key_part, own_places, key_places, own_groups, key_groups, relative_bias
        )
        attention = jnp.exp(scores - log_total[..., None])
        grad_weights = jnp.einsum(
            "qhd,khd->hqk", mixed_grad_low, value_part, preferred_element_type=jnp.float32
        )
        score_gradients = (attention * (grad_weights - row_dots[..., None])).astype(jnp.bfloat16)
        query_grad = query_grad + jnp.einsum(
            "hqk,khd->qhd", score_gradients, key_part, preferred_element_type=jnp.float32
        )
        table_grad = table_grad + jnp.einsum(
            "oei,cei->oc", one_hot_mask, score_gradients, preferred_element_type=jnp.float32
        )
        key_grad = jnp.einsum(
            "hqk,qhd->khd", score_gradients, query_heads, preferred_element_type=jnp.float32
        )
        value_grad = jnp.einsum(
            "hqk,qhd->khd",
            attention.astype(jnp.bfloat16),
            mixed_grad_low,
            preferred_element_type=jnp.float32,
        )
        return ((query_grad, table_grad), (key_grad, value_grad))

    (query_grad, table_grad), (key_terms, value_terms) = lax.scan(
        backward_block, grads_init, key_blocks(key_back, value_back)
    )
    key_grad, value_grad = (
        lax.psum_scatter(
            key_terms.reshape(row_length, inner_width), "seq", scatter_dimension=0, tiled=True
        ),
        lax.psum_scatter(
            value_terms.reshape(row_length, inner_width), "seq", scatter_dimension=0, tiled=True
        ),
    )
    query_grad_low = query_grad.reshape(tok_rows, inner_width).astype(jnp.bfloat16)
    key_grad_low = key_grad.astype(jnp.bfloat16)
    value_grad_low = value_grad.astype(jnp.bfloat16)
    grad_query = dot_rows(normed_low, query_grad_low)
    grad_key = dot_rows(normed_low, key_grad_low)
    grad_value = dot_rows(normed_low, value_grad_low)
    normed_grad = (
        dot_cols(query_grad_low, query_weight)
        + dot_cols(key_grad_low, key_weight)
        + dot_cols(value_grad_low, value_weight)
    )
    input_norm_grad, grad_gain_one = norm_pull(normed_grad)
    hidden_grad = (middle_grad + input_norm_grad)[None]
    local_grads = (
        grad_gain_one,
        grad_query,
        grad_key,
        grad_value,
        grad_out,
        table_grad.reshape(-1),
        grad_gain_two,
        grad_gate,
        grad_up,
        grad_down,
    )
    shared = (
        lax.psum_scatter(local_grads[0], "seq", scatter_dimension=0, tiled=True),
        lax.psum_scatter(local_grads[1], "seq", scatter_dimension=0, tiled=True),
        lax.psum_scatter(local_grads[2], "seq", scatter_dimension=0, tiled=True),
        lax.psum_scatter(local_grads[3], "seq", scatter_dimension=0, tiled=True),
        lax.psum_scatter(local_grads[4], "seq", scatter_dimension=0, tiled=True),
        lax.psum_scatter(local_grads[5], "seq", scatter_dimension=0, tiled=True),
        lax.psum_scatter(local_grads[6], "seq", scatter_dimension=0, tiled=True),
        lax.psum_scatter(local_grads[7], "seq", scatter_dimension=0, tiled=True),
        lax.psum_scatter(local_grads[8], "seq", scatter_dimension=0, tiled=True),
        lax.psum_scatter(local_grads[9], "seq", scatter_dimension=0, tiled=True),
    )
    shared = (
        lax.psum(shared[0].astype(jnp.bfloat16), "dp").astype(jnp.float32),
        lax.psum(shared[1].astype(jnp.bfloat16), "dp").astype(jnp.float32),
        lax.psum(shared[2].astype(jnp.bfloat16), "dp").astype(jnp.float32),
        lax.psum(shared[3].astype(jnp.bfloat16), "dp").astype(jnp.float32),
        lax.psum(shared[4].astype(jnp.bfloat16), "dp").astype(jnp.float32),
        lax.psum(shared[5].astype(jnp.bfloat16), "dp").astype(jnp.float32),
        lax.psum(shared[6].astype(jnp.bfloat16), "dp").astype(jnp.float32),
        lax.psum(shared[7].astype(jnp.bfloat16), "dp").astype(jnp.float32),
        lax.psum(shared[8].astype(jnp.bfloat16), "dp").astype(jnp.float32),
        lax.psum(shared[9].astype(jnp.bfloat16), "dp").astype(jnp.float32),
    )
    summed = (
        lax.all_gather(shared[0].astype(jnp.bfloat16), "seq", axis=0, tiled=True).astype(
            jnp.float32
        ),
        lax.all_gather(shared[1].astype(jnp.bfloat16), "seq", axis=0, tiled=True).astype(
            jnp.float32
        ),
        lax.all_gather(shared[2].astype(jnp.bfloat16), "seq", axis=0, tiled=True).astype(
            jnp.float32
        ),
        lax.all_gather(shared[3].astype(jnp.bfloat16), "seq", axis=0, tiled=True).astype(
            jnp.float32
        ),
        lax.all_gather(shared[4].astype(jnp.bfloat16), "seq", axis=0, tiled=True).astype(
            jnp.float32
        ),
        lax.all_gather(shared[5].astype(jnp.bfloat16), "seq", axis=0, tiled=True).astype(
            jnp.float32
        ),
        lax.all_gather(shared[6].astype(jnp.bfloat16), "seq", axis=0, tiled=True).astype(
            jnp.float32
        ),
        lax.all_gather(shared[7].astype(jnp.bfloat16), "seq", axis=0, tiled=True).astype(
            jnp.float32
        ),
        lax.all_gather(shared[8].astype(jnp.bfloat16), "seq", axis=0, tiled=True).astype(
            jnp.float32
        ),
        lax.all_gather(shared[9].astype(jnp.bfloat16), "seq", axis=0, tiled=True).astype(
            jnp.float32
        ),
    )
    return (
        block_out,
        hidden_grad,
        summed[0],
        summed[1],
        summed[2],
        summed[3],
        summed[4],
        summed[5].reshape(relative_bias.shape),
        summed[6],
        summed[7],
        summed[8],
        summed[9],
    )


def solution(mesh):
    placed = (P("dp", "seq", None), P("dp", None)) + (P(),) * 10 + (P("dp", "seq", None),)
    out_specs = (P("dp", "seq", None),) * 2 + (P(),) * 10
    count = mesh.shape["seq"]

    def run(*args):
        hidden, query_weight, relative_bias = args[0], args[3], args[7]
        head_count = relative_bias.shape[1]
        inner = query_weight.shape[1] // count
        fits = (
            mesh.shape["dp"] == 4
            and count % 2 == 0
            and head_count % count == 0
            and inner == LANES
            and hidden.shape[2] == count * LANES
            and hidden.shape[1] == count * LANES
            and args[9].shape[1] % (4 * LANES) == 2 * LANES
        )
        body = functools.partial(split_shards, count=count) if fits else shards
        return jax.shard_map(
            body, mesh=mesh, in_specs=placed, out_specs=out_specs, check_vma=False
        )(*args)

    return run
```

```python
import functools
import types

import jax
import jax.numpy as jnp
from jax import lax
from jax.experimental import pallas as pl
from jax.experimental.pallas import tpu as pltpu
from jax.sharding import PartitionSpec as P

EPSILON = 1e-06
MASKED = -1e30
THRESHOLDS = (12, 16, 23, 32, 46, 64, 91)
MESH = pl.DeviceIdType.MESH
BF = jnp.bfloat16
F32 = jnp.float32
LANES = 128
ANY = pl.BlockSpec(memory_space=pl.ANY)
VMEM = pl.BlockSpec(memory_space=pltpu.VMEM)


def bucket_of(relative):
    distance = jnp.abs(relative)
    bucket_level = jnp.full(relative.shape, 8, jnp.int32)
    for boundary in THRESHOLDS:
        bucket_level = bucket_level + (distance >= boundary).astype(jnp.int32)
    near_bucket = jnp.where(distance < 8, distance, bucket_level)
    return near_bucket + 16 * (relative > 0).astype(jnp.int32)


def dot(left_mat, right_mat):
    return jnp.dot(left_mat, right_mat, preferred_element_type=F32)


def dot_rows(left_mat, right_mat):
    return lax.dot_general(
        left_mat, right_mat, (((0,), (0,)), ((), ())), preferred_element_type=F32
    )


def dot_cols(left_mat, right_mat):
    return lax.dot_general(
        left_mat, right_mat, (((1,), (1,)), ((), ())), preferred_element_type=F32
    )


def ring_place(index, count):
    odd = index % 2
    return (1 - odd) * (index // 2) + odd * ((2 * count - 1 - index) // 2)


def ring_index(place, count):
    late = place // (count // 2)
    return (1 - late) * 2 * place + late * (2 * count - 1 - 2 * place)


def greet(targets):
    barrier = pltpu.get_barrier_semaphore()
    for target in targets:
        pl.semaphore_signal(barrier, inc=1, device_id=target, device_id_type=MESH)
    pl.semaphore_wait(barrier, len(targets))


def comm_params(collective_id, vmem=None):
    return pltpu.CompilerParams(
        collective_id=collective_id, has_side_effects=True, vmem_limit_bytes=vmem
    )


class Spot:
    def __init__(self, count):
        self.count = count
        self.half = count // 2
        self.me = lax.axis_index("seq")
        self.dp = lax.axis_index("dp")
        self.place = ring_place(self.me, count)
        self.nexts = tuple((self.dp, self.at(step)) for step in (1, -1))
        self.far_dp = (self.dp + 2) % 4
        self.twin_dp = self.dp + 1 - 2 * (self.dp % 2)
        self.far = (self.far_dp, self.me)
        self.twin = (self.twin_dp, self.me)
        self.others = tuple((self.dp, (self.me + step) % count) for step in range(1, count))

    def at(self, step):
        return ring_index((self.place + (step + self.count) % self.count) % self.count, self.count)

    def back(self, way, hop):
        return self.at(-hop if way == 0 else hop)


def push(source, target, send_sem, recv_sem, device):
    copy = pltpu.make_async_remote_copy(
        src_ref=source,
        dst_ref=target,
        send_sem=send_sem,
        recv_sem=recv_sem,
        device_id=device,
        device_id_type=MESH,
    )
    copy.start()
    return copy


def wait_all(like, sem):
    pltpu.make_async_copy(like, like, sem).wait()


class RingGather:
    def __init__(self, spot, own, blocks, send_sem, recv_sems):
        self.spot, self.own, self.blocks = spot, own, blocks
        self.send_sem, self.recv_sems = send_sem, recv_sems
        self.rows = blocks.shape[1] // 2
        self.copies = {}

    def into(self, origin, piece):
        return self.blocks.at[origin, pl.ds(piece * self.rows, self.rows)]

    def pieces(self, way, hop):
        return (0, 1) if hop < self.spot.half - 1 else (way,)

    def forward(self, hop, way, piece):
        spot = self.spot
        if hop >= spot.half or piece not in self.pieces(way, hop):
            return
        origin = spot.back(way, hop)
        target = self.into(origin, piece)
        self.copies[hop, way, piece] = push(
            self.own.at[pl.ds(piece * self.rows, self.rows)] if hop == 0 else target,
            target,
            self.send_sem,
            self.recv_sems.at[way, hop, piece],
            spot.nexts[way],
        )

    def begin(self, piece):
        for way in range(2):
            self.forward(0, way, piece)

    def step(self, hop):
        for piece in range(2):
            for way in range(2):
                if (hop, way, piece) in self.copies:
                    self.copies[hop, way, piece].wait_recv()
                    self.forward(hop + 1, way, piece)

    def finish(self):
        wait_all(self.blocks.at[pl.ds(0, self.spot.count - 1)], self.send_sem)


class RingSum:
    def __init__(self, spot, terms, buf, send_sem, recv_sems):
        self.spot, self.terms, self.buf = spot, terms, buf
        self.send_sem, self.recv_sems = send_sem, recv_sems
        self.rows = terms.shape[1] // 2
        self.copies = {}

    def term(self, block, piece):
        return self.terms.at[block, pl.ds(piece * self.rows, self.rows)]

    def send(self, hop, way, piece, source):
        self.copies[hop, way, piece] = push(
            source,
            self.buf.at[way, hop, piece],
            self.send_sem,
            self.recv_sems.at[way, hop, piece],
            self.spot.nexts[way],
        )

    def block(self, way, hop):
        step = self.spot.half - hop
        return self.spot.at(step if way == 0 else -step)

    def begin(self):
        for way in range(2):
            self.send(0, way, way, self.term(self.block(way, 0), way))
        for way in range(2):
            self.send(1, way, 1 - way, self.term(self.block(way, 1), 1 - way))

    def step(self, hop):
        for piece in range(2):
            for way in range(2):
                if (hop, way, piece) not in self.copies or hop + 1 >= self.spot.half:
                    continue
                self.copies[hop, way, piece].wait_recv()
                term = self.term(self.block(way, hop + 1), piece)
                self.buf[way, hop, piece] = (
                    self.buf[way, hop, piece].astype(F32) + term[...].astype(F32)
                ).astype(BF)
                self.send(hop + 1, way, piece, self.buf.at[way, hop, piece])

    def total(self, out):
        last = self.spot.half - 1
        for piece in range(2):
            value = self.term(self.spot.me, piece)[...].astype(F32)
            for way in range(2):
                self.copies[last, way, piece].wait_recv()
                value = value + self.buf[way, last, piece].astype(F32)
            out[pl.ds(piece * self.rows, self.rows)] = value.astype(BF)

    def finish(self):
        wait_all(self.terms.at[pl.ds(0, self.spot.count - 1)], self.send_sem)


class PairGather:
    def __init__(self, spot, own_ref, buf, send_sems, recv_sems):
        self.spot, self.buf = spot, buf
        self.send_sems, self.recv_sems = send_sems, recv_sems
        rows = own_ref.shape[0]
        self.low, self.high = pl.ds(0, rows), pl.ds(rows, rows)
        self.far = self.push(1, own_ref, buf.at[1, self.low], spot.far)
        self.near = self.push(0, own_ref, buf.at[0, self.high], spot.twin)

    def push(self, index, source, target, device):
        return push(source, target, self.send_sems.at[index], self.recv_sems.at[index], device)

    def relay(self):
        self.far.wait_recv()
        self.cross = self.push(
            2, self.buf.at[1, self.low], self.buf.at[1, self.high], self.spot.twin
        )

    def finish(self):
        for copy in (self.near, self.far, self.cross):
            copy.wait_send()


class PairSum:
    def __init__(self, spot, kept, outs, ins, far_out, far_in, send_sems, recv_sems):
        self.spot, self.kept, self.outs, self.ins = spot, kept, outs, ins
        self.far_out, self.far_in = far_out, far_in
        self.send_sems, self.recv_sems = send_sems, recv_sems
        self.copies = []

    def near(self, half):
        self.copies.append(
            push(
                self.outs.at[half], self.ins.at[half],
                self.send_sems.at[half], self.recv_sems.at[half], self.spot.twin,
            )
        )

    def over(self):
        self.copies[1].wait_recv()
        self.far_out[...] = (self.kept[1] + self.ins[1].astype(F32)).astype(BF)
        self.copies.append(
            push(
                self.far_out, self.far_in, self.send_sems.at[2], self.recv_sems.at[2], self.spot.far
            )
        )

    def total(self):
        self.copies[0].wait_recv()
        self.copies[2].wait_recv()
        return self.kept[0] + self.ins[0].astype(F32) + self.far_in[...].astype(F32)

    def finish(self):
        for copy in self.copies:
            copy.wait_send()


class MeshGather:
    def __init__(self, spot, x_ref, o_ref, share, sems):
        self.spot, self.x_ref, self.o_ref = spot, x_ref, o_ref
        self.ring_s, self.ring_r, self.x_s, self.far_r, self.own_r, self.core_s, self.core_r = sems
        rows = x_ref.shape[0]
        first = rows * share // 100 // 32 * 32
        cuts = (0, first // 2, first, first + (rows - first) // 2 // 16 * 16, rows)
        self.parts = (pl.ds(0, first), pl.ds(first, rows - first))
        self.windows = [
            [pl.ds(cuts[2 * part + piece], cuts[2 * part + piece + 1] - cuts[2 * part + piece]) for piece in range(2)]
            for part in range(2)
        ]
        self.ring, self.x = {}, {}

    def into(self, dp, origin, part, piece):
        return self.o_ref.at[dp, origin, self.windows[part][piece]]

    def pieces(self, way, hop):
        return (0, 1) if hop < self.spot.half - 1 else (way,)

    def to_core(self, source, target):
        push(source, target, self.core_s, self.core_r, self.spot.twin)

    def pass_on(self, part, lane, hop, way, piece, source):
        spot = self.spot
        dp = spot.far_dp if lane else spot.dp
        origin = spot.me if way is None else spot.back(way, hop)
        target = self.into(dp, origin, part, piece)
        source = target if source is None else source
        slot = 0 if way is None else 2 * hop - 1 + way
        for onward in (0, 1) if way is None else (way,):
            if hop < spot.half and piece in self.pieces(onward, hop):
                self.ring[part, lane, hop, onward, piece] = push(
                    source, target,
                    self.ring_s.at[part + lane],
                    self.ring_r.at[2 * (part + lane) + onward, hop, piece],
                    spot.nexts[onward],
                )
        if part == 0:
            self.x[part, slot, piece] = push(
                source, target, self.x_s.at[0], self.far_r.at[slot, piece], spot.far
            )
        self.to_core(source, target)

    def begin(self):
        spot = self.spot
        for piece in range(2):
            self.x[1, 0, piece] = push(
                self.x_ref.at[self.windows[1][piece]],
                self.into(spot.dp, spot.me, 1, piece),
                self.x_s.at[1], self.own_r.at[piece], spot.far,
            )
        for part in range(2):
            for piece in range(2):
                self.pass_on(part, 0, 0, None, piece, self.x_ref.at[self.windows[part][piece]])

    def begin_far(self):
        for piece in range(2):
            self.x[1, 0, piece].wait_recv()
            self.pass_on(1, 1, 0, None, piece, None)

    def step(self, hop):
        for piece in range(2):
            for part, lane in ((0, 0), (1, 0), (1, 1)):
                for way in range(2):
                    key = (part, lane, hop, way, piece)
                    if key in self.ring:
                        self.ring[key].wait_recv()
                        self.pass_on(part, lane, hop + 1, way, piece, None)

    def step_far(self, hop):
        spot = self.spot
        for piece in range(2):
            for way in (None,) if hop == 0 else range(2):
                slot = 0 if way is None else 2 * hop - 1 + way
                if (0, slot, piece) in self.x:
                    self.x[0, slot, piece].wait_recv()
                    origin = spot.me if way is None else spot.back(way, hop)
                    target = self.into(spot.far_dp, origin, 0, piece)
                    self.to_core(target, target)

    def finish(self):
        o_ref, count = self.o_ref, self.spot.count
        wait_all(o_ref.at[pl.ds(0, 2)], self.core_r)
        wait_all(o_ref.at[pl.ds(0, 2)], self.core_s)
        for index in range(3):
            wait_all(o_ref.at[0, pl.ds(0, count - 1), self.parts[min(index, 1)]], self.ring_s.at[index])
        wait_all(o_ref.at[0, :, self.parts[0]], self.x_s.at[0])
        wait_all(self.x_ref.at[self.parts[1]], self.x_s.at[1])


def mesh_sems(count):
    half = count // 2
    dma = pltpu.SemaphoreType.DMA
    return [
        dma((3,)), dma((6, half, 2)), dma((2,)), dma((2 * half + 1, 2)), dma((2,)), dma(()), dma(())
    ]


def near_buckets(rows):
    shape = (rows, rows + 2 * LANES)
    column = lax.broadcasted_iota(jnp.int32, shape, 1) - LANES
    return bucket_of(column - lax.broadcasted_iota(jnp.int32, shape, 0))


def strip_window(step, rows, length):
    return pl.ds(pl.multiple_of(length - rows - step * rows, LANES), length)


def scale_of(value):
    return lax.rsqrt(jnp.mean(value * value, axis=-1, keepdims=True) + EPSILON)


def row_block(origin, rows):
    return pl.ds(pl.multiple_of(origin * rows, rows), rows)


def exclusive(index, bit):
    return index + bit - 2 * bit * ((index // bit) % 2)


def layer_body(count, heads, depth, ff, names, *refs):
    r = types.SimpleNamespace(**dict(zip(names, refs)))
    spot = Spot(count)
    hidden_ref, grad_ref = r.hidden, r.out_grad
    rows, width = hidden_ref.shape
    length = count * rows
    inner = heads * depth
    span = r.gate_w.shape[1]
    odd = spot.dp % 2
    ff_start = pl.multiple_of(spot.dp * ff - odd * (span - ff), span - ff)
    own_columns = pl.ds(pl.multiple_of(spot.me * LANES, LANES), LANES)
    greet(spot.nexts + (spot.far, spot.twin))

    loads = {}

    def load(name, source, target):
        copy = pltpu.make_async_copy(source, target, r.load_sems.at[len(loads)])
        copy.start()
        loads[name] = copy

    ring = RingGather(
        spot,
        hidden_ref,
        r.row,
        r.row_s,
        r.row_r,
    )
    ring.begin(0)
    sources = (r.query_weight, r.key_weight, r.value_weight)
    for part, source in enumerate(sources):
        load(
            part,
            source.at[:, pl.ds(pl.multiple_of(spot.me * inner, inner), inner)],
            r.qkv_w.at[:, pl.ds(part * inner, inner)],
        )
    load("out", r.out_weight, r.out_w)
    ff_columns = pl.ds(pl.multiple_of(ff_start, LANES), span)
    load("gate", r.gate_weight.at[:, ff_columns], r.gate_w)
    load("up", r.up_weight.at[:, ff_columns], r.up_w)
    load("down", r.down_weight.at[pl.ds(ff_start, span)], r.down_w)
    for part, source in enumerate(sources):
        load(3 + part, source, r.full_w.at[part])

    strip, qkv, normed, weights = r.strip, r.qkv, r.normed, r.weights
    low = length - rows - LANES
    bucket = near_buckets(rows)
    near_span = bucket.shape[1]
    level_count, head_count = r.table.shape
    chosen = lax.broadcasted_iota(jnp.int32, (head_count, LANES), 0) == (
        spot.me * heads + lax.broadcasted_iota(jnp.int32, (head_count, LANES), 1)
    )
    table = dot(r.table[...], chosen.astype(BF))
    for head in range(heads):
        entry = lambda level: table[level : level + 1, head : head + 1]
        value = jnp.zeros(bucket.shape, F32)
        for level in range(level_count):
            value = jnp.where(bucket == level, entry(level), value)
        strip[head, :, :low] = jnp.broadcast_to(entry(15), (rows, low))
        strip[head, :, low : low + near_span] = value
        after = strip.shape[2] - low - near_span
        strip[head, :, low + near_span :] = jnp.broadcast_to(entry(31), (rows, after))
    ring.begin(1)
    cots = PairGather(spot, grad_ref, r.cot, r.cot_s, r.cot_r)
    gain_one = r.gain_one[...].astype(F32)
    gain_two = r.gain_two[...].astype(F32)

    def project(origin, block):
        value = block.astype(F32)
        low_value = (value * scale_of(value) * gain_one).astype(BF)
        mine = row_block(origin, rows)
        normed[mine] = low_value
        qkv[mine] = dot(low_value, r.qkv_w[...]).astype(BF)

    for part in range(3):
        loads[part].wait()
    project(spot.me, hidden_ref[...])
    for hop in range(spot.half):
        ring.step(hop)
        if hop < spot.half - 1:

            def both(side, carry, hop=hop):
                origin = spot.at((1 - 2 * side) * (hop + 1))
                project(origin, r.row[origin])
                return carry

            lax.fori_loop(0, 2, both, 0)
        else:
            origin = spot.at(spot.half)
            project(origin, r.row[origin])
    cots.relay()
    r.cot[0, :rows] = grad_ref[...]
    mixed_heads, mixed = r.mixed_heads, r.mixed

    def attend(target):
        mine = row_block(target, rows)
        turned_ids = jnp.broadcast_to(r.row_ids[:, mine], (LANES, rows)).T
        same = turned_ids[:, :1] == r.row_ids[...]
        window = strip_window(target, rows, length)
        for head in range(heads):
            columns = slice(head * depth, (head + 1) * depth)
            key = qkv[:, inner + head * depth : inner + (head + 1) * depth]
            value = qkv[:, 2 * inner + head * depth : 2 * inner + (head + 1) * depth]
            scores = dot_cols(qkv[mine, columns], key) + strip[head, :, window]
            scores = jnp.where(same, scores, MASKED)
            top = jnp.max(scores, axis=1, keepdims=True)
            weight = jnp.exp(scores - top)
            weight = weight * (1.0 / jnp.sum(weight, axis=1, keepdims=True))
            weight = weight.astype(BF)
            weights[head, mine] = weight
            mixed_heads[mine, columns] = dot(weight, value).astype(BF)

    def mixed_copy(step):
        target = (spot.me + step) % count
        return pltpu.make_async_remote_copy(
            src_ref=mixed_heads.at[row_block(target, rows)],
            dst_ref=mixed.at[:, own_columns],
            send_sem=r.mixed_s,
            recv_sem=r.mixed_r,
            device_id=(spot.dp, target),
            device_id_type=MESH,
        )

    def attend_and_send(step, carry):
        attend((spot.me + step) % count)
        mixed_copy(step).start()
        return carry

    lax.fori_loop(1, count, attend_and_send, 0)
    attend(spot.me)
    mixed[:, own_columns] = mixed_heads[row_block(spot.me, rows)]

    loads["out"].wait()
    wait_all(mixed.at[:, pl.ds(0, width - LANES)], r.mixed_r)
    inputs = hidden_ref[...].astype(F32)
    middle_ref = r.middle
    middle = inputs + dot(mixed[...], r.out_w[...])
    middle_ref[...] = middle
    tok, cot = r.tok, r.cot
    tok[0, :rows] = (middle * scale_of(middle) * gain_two).astype(BF)
    toks = PairGather(spot, tok.at[0, pl.ds(0, rows)], tok, r.tok_s, r.tok_r)
    gate_w, up_w, down_w = r.gate_w, r.up_w, r.down_w
    act, gate_g, up_g = r.act, r.gate_g, r.up_g
    for name in ("gate", "up", "down"):
        loads[name].wait()
    both_rows = 2 * rows
    chunk = 256
    grads = PairSum(
        spot, r.grad_kept, r.grad_outs, r.grad_ins, r.grad_far_out, r.grad_far_in,
        r.grad_s, r.grad_r,
    )
    outs = PairSum(
        spot, r.out_kept, r.out_outs, r.out_ins, r.out_far_out, r.out_far_in,
        r.out_s, r.out_r,
    )

    def activate_half(half):
        mine = pl.ds(half * both_rows, both_rows)

        def tile(index, carry):
            columns = row_block(index, chunk)
            gate = dot(tok[half], gate_w[:, columns])
            up = dot(tok[half], up_w[:, columns])
            act_grad = dot_cols(cot[half], down_w[columns])
            place = index * chunk + lax.broadcasted_iota(jnp.int32, (1, chunk), 1)
            place = place - odd * (span - ff)
            inside = (place >= 0) & (place < ff)
            root = 0.7978845608028654
            squared = gate * gate
            bend = jnp.tanh(root * (gate + 0.044715 * gate * squared))
            share = 0.5 * (1.0 + bend)
            gelu = gate * share
            slope = share + 0.5 * gate * (1.0 - bend * bend) * root * (
                1.0 + 3 * 0.044715 * squared
            )
            act[mine, columns] = jnp.where(inside, gelu * up, 0.0).astype(BF)
            gate_g[mine, columns] = jnp.where(inside, act_grad * up * slope, 0.0).astype(BF)
            up_g[mine, columns] = jnp.where(inside, act_grad * gelu, 0.0).astype(BF)
            return carry

        lax.fori_loop(0, span // chunk, tile, 0)

    def spread(pair_sum, half, product):
        def tile(index, carry):
            columns = row_block(index, chunk)
            value = product(columns)
            pair_sum.kept[half, :, columns] = value[:rows]
            pair_sum.outs[half, :, columns] = value[rows:].astype(BF)
            return carry

        lax.fori_loop(0, width // chunk, tile, 0)
        pair_sum.near(half)

    def back_half(half):
        mine = pl.ds(half * both_rows, both_rows)
        spread(
            grads,
            half,
            lambda columns: dot_cols(gate_g[mine], gate_w[columns])
            + dot_cols(up_g[mine], up_w[columns]),
        )

    def out_half(half):
        mine = pl.ds(half * both_rows, both_rows)
        spread(outs, half, lambda columns: dot(act[mine], down_w[:, columns]))

    cots.near.wait_recv()
    cots.cross.wait_recv()
    toks.near.wait_recv()
    activate_half(0)
    toks.relay()
    back_half(0)
    toks.cross.wait_recv()
    activate_half(1)
    back_half(1)

    down_terms, pair_terms = r.down_terms, r.pair_terms
    spare = span - ff

    def down_tile(index, carry):
        columns = row_block(index, LANES)
        value = dot_rows(act[:both_rows], cot[0, :, columns]) + dot_rows(
            act[both_rows:], cot[1, :, columns]
        )
        down_terms[index] = jnp.where(odd == 1, value[spare:], value[:ff]).astype(BF)
        return carry

    lax.fori_loop(0, count, down_tile, 0)
    down_sum = RingSum(spot, down_terms, r.down_buf, r.down_s, r.down_r)
    down_sum.begin()
    grads.over()
    full = ff // LANES
    lane = lax.broadcasted_iota(jnp.int32, (LANES, LANES), 1)

    def pair_tile(index, carry):
        columns = row_block(index, LANES)
        parts = []
        for source in (gate_g, up_g):
            parts.append(
                dot_rows(tok[0, :, columns], source[:both_rows])
                + dot_rows(tok[1, :, columns], source[both_rows:])
            )
        cut = lambda value, place: value[:, place * LANES : (place + 1) * LANES]
        for part, value in enumerate(parts):
            for place in range(full):
                start = (part * full + place) * LANES
                pair_terms[index, start : start + LANES] = jnp.where(
                    odd == 1, cut(value, place + 1), cut(value, place)
                ).astype(BF)
        edges = [jnp.where(odd == 1, cut(value, 0), cut(value, full)) for value in parts]
        turned = pltpu.roll(edges[1], LANES // 2, 1)
        lower = (lane < LANES // 2).astype(jnp.int32)
        pair_terms[index, 2 * full * LANES :] = jnp.where(lower == odd, turned, edges[0]).astype(BF)
        return carry

    lax.fori_loop(0, count, pair_tile, 0)
    pair_sum = RingSum(spot, pair_terms, r.pair_buf, r.pair_s, r.pair_r)
    down_sum.step(0)
    out_half(0)
    out_half(1)

    normed_two_grad = grads.total()
    middle = middle_ref[...]
    scale_two = scale_of(middle)
    lifted = gain_two * normed_two_grad
    middle_grad = (
        grad_ref[...].astype(F32)
        + scale_two * lifted
        - middle * (scale_two * scale_two * scale_two)
        * jnp.mean(middle * lifted, axis=-1, keepdims=True)
    )
    middle_grad_ref = r.middle_grad
    middle_grad_ref[...] = middle_grad
    small = r.small
    small[...] = jnp.zeros_like(small)
    gain_grad = jnp.sum(normed_two_grad * middle * scale_two, axis=0, keepdims=True)
    tiles = width // LANES
    for tile in range(tiles):
        small[tiles + tile : tiles + tile + 1] = gain_grad[:, tile * LANES : (tile + 1) * LANES]
    branch, own_branch = r.branch, r.own_branch
    own_branch[...] = middle_grad.astype(BF)
    branches = RingGather(
        spot,
        own_branch,
        branch,
        r.branch_s,
        r.branch_r,
    )
    branches.begin(0)
    branch[spot.me] = own_branch[...]
    outs.over()
    keys, values, dqkv, packed = r.keys, r.values, r.dqkv, r.packed
    strip[...] = jnp.zeros_like(strip)
    keys[...] = jnp.zeros_like(keys)
    values[...] = jnp.zeros_like(values)
    branches.begin(1)
    packed[...] = jnp.zeros_like(packed)

    own_out = r.out_w.at[row_block(spot.me, inner)]
    quarter, slim = width // 4, inner // 4

    def attend_back(origin):
        mine = row_block(origin, rows)
        window = strip_window(origin, rows, length)
        mixed_grad = dot_cols(branch[origin], own_out[...]).astype(BF)
        for head in range(heads):
            columns = slice(head * depth, (head + 1) * depth)
            key = qkv[:, inner + head * depth : inner + (head + 1) * depth]
            value = qkv[:, 2 * inner + head * depth : 2 * inner + (head + 1) * depth]
            grad = mixed_grad[:, columns]
            weight_low = weights[head, mine]
            weight = weight_low.astype(F32)
            scaled = weight * dot_cols(grad, value)
            score_grad = scaled - weight * jnp.sum(scaled, axis=1, keepdims=True)
            strip[head, :, window] += score_grad
            score_low = score_grad.astype(BF)
            dqkv[mine, columns] = dot(score_low, key).astype(BF)
            keys[:, columns] += dot_rows(score_low, qkv[mine, columns])
            values[:, columns] += dot_rows(weight_low, grad)
        terms = dot_rows(mixed_heads[mine], branch[origin])
        for tile in range(tiles):
            for index in range(4):
                base = 3 * quarter + tile * slim
                packed[index, base : base + slim] += terms[
                    index * slim : (index + 1) * slim, tile * LANES : (tile + 1) * LANES
                ]
        terms = dot_rows(normed[mine], dqkv[mine, :inner])
        for index in range(4):
            packed[index, :quarter] += terms[index * quarter : (index + 1) * quarter]

    mesh_sets = [r.gather_sems[7 * index : 7 * index + 7] for index in range(3)]
    attend_back(spot.me)
    down_sum.step(1)
    r.block_out[...] = (middle + outs.total()).astype(BF)
    for hop in range(spot.half):
        branches.step(hop)
        if hop == 0:
            down_sum.step(2)
        if hop == spot.half - 2:
            pair_sum.begin()
            down_sum.total(r.down_block)
            down = MeshGather(spot, r.down_block, r.down_all, SHARES[0], mesh_sets[0])
            down.begin()
            load("down_own", r.down_block, r.down_all.at[spot.dp, spot.me])
        if hop < spot.half - 1:

            def both_back(side, carry, hop=hop):
                attend_back(spot.at((1 - 2 * side) * (hop + 1)))
                return carry

            lax.fori_loop(0, 2, both_back, 0)
        else:
            attend_back(spot.at(spot.half))

    dqkv[:, inner : 2 * inner] = keys[...].astype(BF)
    dqkv[:, 2 * inner :] = values[...].astype(BF)

    def quarter_block(index, carry):
        block = dot_rows(normed[:, row_block(index, quarter)], dqkv[:, inner:])
        for part in range(2):
            packed[index, (part + 1) * quarter : (part + 2) * quarter] = block[
                :, part * LANES : (part + 1) * LANES
            ]
        return carry

    lax.fori_loop(0, 4, quarter_block, 0)
    core, side = odd, spot.dp // 2
    for index in range(2):
        r.near_out[index] = packed[2 * index + 1 - core].astype(BF)
    near = push(r.near_out, r.near_in, r.proj_s.at[0], r.proj_r.at[0], spot.twin)
    pair_sum.step(0)
    near.wait_recv()
    r.far_out[...] = (
        packed[2 * (1 - side) + core] + r.near_in[1 - side].astype(F32)
    ).astype(BF)
    far = push(r.far_out, r.far_in, r.proj_s.at[1], r.proj_r.at[1], spot.far)

    own_dqkv = r.own_dqkv
    for device in spot.others:
        for part in range(3):
            push(
                dqkv.at[row_block(device[1], rows), pl.ds(part * LANES, LANES)],
                own_dqkv.at[part, :, own_columns],
                r.trade_s,
                r.trade_r,
                device,
            )
    for part in range(3):
        own_dqkv[part, :, own_columns] = dqkv[
            row_block(spot.me, rows), part * LANES : (part + 1) * LANES
        ]
    down.begin_far()
    down.step(0)
    down.step_far(0)
    pair_sum.step(1)
    far.wait_recv()
    r.proj_block[...] = (
        packed[2 * side + core] + r.near_in[side].astype(F32) + r.far_in[...].astype(F32)
    ).astype(BF)
    proj = MeshGather(spot, r.proj_block, r.proj_all, SHARES[2], mesh_sets[2])
    proj.begin()
    load("proj_own", r.proj_block, r.proj_all.at[spot.dp, spot.me])
    down.step(1)
    down.step_far(1)
    pair_sum.step(2)

    for head in range(heads):
        middle_part = strip[head, :, low : low + near_span]
        before = jnp.sum(strip[head, :, :low], axis=0, keepdims=True)
        after = jnp.sum(strip[head, :, low + near_span :], axis=0, keepdims=True)
        levels = []
        for level in range(level_count):
            part = jnp.sum(jnp.where(bucket == level, middle_part, 0.0), axis=0, keepdims=True)
            line = part[:, :LANES]
            for tile in range(1, near_span // LANES):
                line = line + part[:, tile * LANES : (tile + 1) * LANES]
            edge = before if level == 15 else after if level == 31 else None
            if edge is not None:
                for tile in range(edge.shape[1] // LANES):
                    line = line + edge[:, tile * LANES : (tile + 1) * LANES]
            r.levels[level : level + 1] = line
        sums = lax.dot_general(
            jnp.ones((8, LANES), F32),
            r.levels[...],
            (((1,), (1,)), ((), ())),
            precision=lax.Precision.HIGHEST,
            preferred_element_type=F32,
        )
        small[pl.ds(2 * tiles + spot.me * heads + head, 1), : level_count] = sums[:1]

    pair_sum.total(r.pair_block)
    pair = MeshGather(spot, r.pair_block, r.pair_all, SHARES[1], mesh_sets[1])
    pair.begin()
    load("pair_own", r.pair_block, r.pair_all.at[spot.dp, spot.me])
    proj.begin_far()
    for hop in (2, 3):
        down.step(hop)
        down.step_far(hop)
    down.step_far(spot.half)
    proj.step(0)
    proj.step_far(0)
    pair.begin_far()

    for part in range(3):
        loads[3 + part].wait()
    wait_all(own_dqkv.at[:, :, pl.ds(0, width - LANES)], r.trade_r)
    normed_grad = dot_cols(own_dqkv[0], r.full_w[0])
    for part in range(1, 3):
        normed_grad = normed_grad + dot_cols(own_dqkv[part], r.full_w[part])
    inputs = hidden_ref[...].astype(F32)
    scale_one = scale_of(inputs)
    raised = gain_one * normed_grad
    r.hidden_grad[...] = (
        middle_grad_ref[...]
        + scale_one * raised
        - inputs * (scale_one * scale_one * scale_one)
        * jnp.mean(inputs * raised, axis=-1, keepdims=True)
    )
    gain_grad = jnp.sum(normed_grad * inputs * scale_one, axis=0, keepdims=True)
    for tile in range(tiles):
        small[tile : tile + 1] = gain_grad[:, tile * LANES : (tile + 1) * LANES]

    partners = [spot.twin, spot.far]
    bit = 1
    while bit < count:
        partners.append((spot.dp, exclusive(spot.me, bit)))
        bit *= 2
    small_out, small_in = r.small_out, r.small_in
    small_copies = []

    def small_send():
        index = len(small_copies)
        if index < len(partners):
            small_out[index] = small[...]
            small_copies.append(
                push(
                    small_out.at[index], small_in.at[index],
                    r.small_s.at[index], r.small_r.at[index], partners[index],
                )
            )

    def small_step():
        if len(small_copies) <= len(partners) and small_copies:
            index = len(small_copies) - 1
            small_copies[index].wait_recv()
            small[...] += small_in[index]
            small_send()

    small_send()
    for hop in range(spot.half):
        pair.step(hop)
        pair.step_far(hop)
        small_step()
        if hop < spot.half - 1:
            proj.step(hop + 1)
            proj.step_far(hop + 1)
        else:
            proj.step_far(spot.half)
    pair.step_far(spot.half)
    small_step()
    r.small_sum[...] = small[...]
    for name in ("down_own", "pair_own", "proj_own"):
        loads[name].wait()
    wait_all(mixed_heads.at[pl.ds(0, length - rows)], r.mixed_s)
    wait_all(dqkv.at[pl.ds(0, length - rows)], r.trade_s)
    for copy in [near, far] + small_copies:
        copy.wait_send()
    for item in (ring, cots, toks, grads, outs, down_sum, pair_sum, branches, down, pair, proj):
        item.finish()


SHARES = (70, 57, 57)


def layer(arrays, count, heads, depth, ff):
    rows, width = arrays["hidden"].shape
    length = count * rows
    inner = heads * depth
    half = count // 2
    span = (ff + LANES - 1) // LANES * LANES
    pair_rows = 2 * ff // LANES * rows
    proj_rows = 3 * (width // 4) + inner // 4 * (width // LANES)
    small_rows = 2 * (width // LANES) + count * heads
    steps = 2 + (count - 1).bit_length()
    dma = pltpu.SemaphoreType.DMA
    specs = dict(
        hidden=VMEM,
        out_grad=VMEM,
        gain_one=VMEM,
        gain_two=VMEM,
        row_ids=VMEM,
        table=VMEM,
    )
    shape = jax.ShapeDtypeStruct
    results = dict(
        block_out=(shape((rows, width), BF), VMEM),
        hidden_grad=(shape((rows, width), F32), VMEM),
        small_sum=(shape((small_rows, LANES), F32), VMEM),
        down_all=(shape((4, count, ff, LANES), BF), ANY),
        pair_all=(shape((4, count, pair_rows, LANES), BF), ANY),
        proj_all=(shape((4, count, proj_rows, LANES), BF), ANY),
    )
    vm = pltpu.VMEM
    ring_buf = lambda n: vm((2, half, 2, n // 2, LANES), BF)
    pairs = {}
    for name in ("grad", "out"):
        pairs[name + "_kept"] = vm((2, rows, width), F32)
        pairs[name + "_outs"] = vm((2, rows, width), BF)
        pairs[name + "_ins"] = vm((2, rows, width), BF)
        pairs[name + "_far_out"] = vm((rows, width), BF)
        pairs[name + "_far_in"] = vm((rows, width), BF)
        pairs[name + "_s"] = dma((3,))
        pairs[name + "_r"] = dma((3,))
    for name in ("cot", "tok"):
        pairs[name] = vm((2, 2 * rows, width), BF)
        pairs[name + "_s"] = dma((3,))
        pairs[name + "_r"] = dma((3,))
    for name in ("row", "branch"):
        pairs[name] = vm((count, rows, width), BF)
        pairs[name + "_s"] = dma(())
        pairs[name + "_r"] = dma((2, half, 2))
    for name, size in (("down", ff), ("pair", pair_rows)):
        pairs[name + "_terms"] = vm((count, size, LANES), BF)
        pairs[name + "_buf"] = ring_buf(size)
        pairs[name + "_block"] = vm((size, LANES), BF)
        pairs[name + "_s"] = dma(())
        pairs[name + "_r"] = dma((2, half, 2))
    scratch = dict(
        **pairs,
        strip=vm((heads, rows, 2 * length - rows), F32),
        normed=vm((length, width), BF),
        qkv=vm((length, 3 * inner), BF),
        weights=vm((heads, length, length), BF),
        mixed_heads=vm((length, inner), BF),
        mixed=vm((rows, width), BF),
        qkv_w=vm((width, 3 * inner), BF),
        full_w=vm((3, width, width), BF),
        out_w=vm((width, width), BF),
        gate_w=vm((width, span), BF),
        up_w=vm((width, span), BF),
        down_w=vm((span, width), BF),
        middle=vm((rows, width), F32),
        middle_grad=vm((rows, width), F32),
        act=vm((4 * rows, span), BF),
        gate_g=vm((4 * rows, span), BF),
        up_g=vm((4 * rows, span), BF),
        own_branch=vm((rows, width), BF),
        keys=vm((length, inner), F32),
        values=vm((length, inner), F32),
        dqkv=vm((length, 3 * inner), BF),
        own_dqkv=vm((3, rows, width), BF),
        packed=vm((4, proj_rows, LANES), F32),
        near_out=vm((2, proj_rows, LANES), BF),
        near_in=vm((2, proj_rows, LANES), BF),
        far_out=vm((proj_rows, LANES), BF),
        far_in=vm((proj_rows, LANES), BF),
        proj_block=vm((proj_rows, LANES), BF),
        levels=vm((arrays["table"].shape[0], LANES), F32),
        small=vm((small_rows, LANES), F32),
        small_out=vm((steps, small_rows, LANES), F32),
        small_in=vm((steps, small_rows, LANES), F32),
        load_sems=dma((16,)),
        mixed_s=dma(()),
        mixed_r=dma(()),
        trade_s=dma(()),
        trade_r=dma(()),
        proj_s=dma((2,)),
        proj_r=dma((2,)),
        small_s=dma((steps,)),
        small_r=dma((steps,)),
    )
    names = tuple(arrays) + tuple(results) + tuple(scratch)

    def body(*refs):
        plain = refs[: len(names)]
        layer_body(
            count, heads, depth, ff, names + ("gather_sems",), *plain, refs[len(names) :]
        )

    outs = pl.pallas_call(
        body,
        name="layer",
        out_shape=tuple(value[0] for value in results.values()),
        in_specs=[specs.get(name, ANY) for name in arrays],
        out_specs=tuple(value[1] for value in results.values()),
        scratch_shapes=list(scratch.values()) + mesh_sems(count) * 3,
        compiler_params=comm_params(0, 60 << 20),
    )(*arrays.values())
    return types.SimpleNamespace(**dict(zip(results, outs)))


def widen_body(
    part, down_ref, pair_ref, proj_ref, block_ref, hidden_ref, small_ref,
    down_out, gate_out, up_out, query_out, key_out, value_out, out_out,
    block_out, hidden_out, one_out, two_out, bias_out,
):
    full, half = part // LANES, LANES // 2
    down_out[...] = down_ref[:, 0].astype(F32)
    for dp in range(pair_ref.shape[0]):
        base = dp * part
        shift = half if dp % 2 else 0
        for which, o_ref in enumerate((gate_out, up_out)):
            for tile in range(full):
                column = base + shift + tile * LANES
                o_ref[:, column : column + LANES] = pair_ref[dp, 0, which * full + tile].astype(F32)
        edge = pair_ref[dp, 0, 2 * full].astype(F32)
        column = base if dp % 2 else base + full * LANES
        gate_half = slice(half, LANES) if dp % 2 else slice(0, half)
        up_half = slice(0, half) if dp % 2 else slice(half, LANES)
        gate_out[:, column : column + half] = edge[:, gate_half]
        up_out[:, column : column + half] = edge[:, up_half]
        slim = out_out.shape[0] // pair_ref.shape[0]
        for tile in range(out_out.shape[1] // LANES):
            out_out[dp * slim : (dp + 1) * slim, tile * LANES : (tile + 1) * LANES] = proj_ref[
                dp, 0, 3, tile * slim : (tile + 1) * slim
            ].astype(F32)
    for index, o_ref in enumerate((query_out, key_out, value_out)):
        o_ref[...] = proj_ref[:, 0, index].astype(F32)

    @pl.when((pl.program_id(0) == 0) & (pl.program_id(1) == 0))
    def _():
        block_out[...] = block_ref[...]
        hidden_out[...] = hidden_ref[...]
        tiles = one_out.shape[0]
        one_out[...] = small_ref[:tiles]
        two_out[...] = small_ref[tiles : 2 * tiles]
        bias_out[...] = small_ref[2 * tiles :].T[: bias_out.shape[0]]


def widen(out, levels, ff):
    rows, width = out.hidden_grad.shape
    dps, count = out.down_all.shape[:2]
    quarter = width // dps
    small_rows = out.small_sum.shape[0]
    tiles = width // LANES
    heads = small_rows - 2 * tiles
    pair = out.pair_all.reshape(dps, count, -1, rows, LANES)
    proj = out.proj_all.reshape(dps, count, 4, quarter, LANES)
    shape = lambda *dims: jax.ShapeDtypeStruct(dims, F32)
    spec = pl.BlockSpec
    whole = lambda *dims: spec(dims, lambda i, h: (0,) * len(dims))
    wide = spec((rows // 2, dps * ff), lambda i, h: (2 * i + h, 0))
    tall = lambda size: spec((dps, size // 2, LANES), lambda i, h: (0, h, i))
    results = pl.pallas_call(
        functools.partial(widen_body, ff),
        name="widen",
        grid=(count, 2),
        out_shape=(
            shape(dps, ff, width),
            shape(width, dps * ff),
            shape(width, dps * ff),
            *[shape(dps, quarter, width)] * 3,
            shape(width, width),
            jax.ShapeDtypeStruct((rows, width), BF),
            shape(rows, width),
            shape(tiles, LANES),
            shape(tiles, LANES),
            shape(levels, heads),
        ),
        in_specs=[
            spec((dps, 1, ff // 2, LANES), lambda i, h: (0, i, h, 0)),
            spec((dps, 1, pair.shape[2], rows // 2, LANES), lambda i, h: (0, i, 0, h, 0)),
            spec((dps, 1, 4, quarter // 2, LANES), lambda i, h: (0, i, 0, h, 0)),
            whole(rows, width),
            whole(rows, width),
            whole(small_rows, LANES),
        ],
        out_specs=(
            tall(ff), wide, wide, tall(quarter), tall(quarter), tall(quarter),
            spec((width // count, width // 2), lambda i, h: (i, h)),
            whole(rows, width), whole(rows, width), whole(tiles, LANES), whole(tiles, LANES),
            whole(levels, heads),
        ),
        compiler_params=pltpu.CompilerParams(vmem_limit_bytes=48 << 20),
    )(out.down_all, pair, proj, out.block_out, out.hidden_grad, out.small_sum)
    return results


def split_shards(
    hidden,
    group_ids,
    norm1_gain,
    query_weight,
    key_weight,
    value_weight,
    out_weight,
    relative_bias,
    norm2_gain,
    gate_weight,
    up_weight,
    down_projection_weight,
    out_grad,
    *,
    count,
):
    width = hidden.shape[2]
    levels, head_count = relative_bias.shape
    depth = query_weight.shape[1] // head_count
    heads = head_count // count
    ff = gate_weight.shape[1] // 4
    arrays = dict(
        hidden=hidden[0],
        out_grad=out_grad[0],
        gain_one=norm1_gain[None],
        gain_two=norm2_gain[None],
        row_ids=group_ids,
        table=relative_bias,
        query_weight=query_weight,
        key_weight=key_weight,
        value_weight=value_weight,
        out_weight=out_weight,
        gate_weight=gate_weight,
        up_weight=up_weight,
        down_weight=down_projection_weight,
    )
    out = layer(arrays, count, heads, depth, ff)
    down, gate, up, query, key, value, projected, block, grad, one, two, bias = widen(
        out, levels, ff
    )
    square = lambda v: v.reshape(-1, width)
    return (
        block[None], grad[None], one.reshape(-1), square(query), square(key), square(value),
        projected, bias, two.reshape(-1), gate, up, square(down),
    )


def rms_norm(vector, norm_gain):
    return (
        vector * lax.rsqrt(jnp.mean(vector * vector, axis=-1, keepdims=True) + EPSILON) * norm_gain
    )


def activate(gate_proj, up_proj):
    return jax.nn.gelu(gate_proj, approximate=True) * up_proj


def scores_of(
    query_part, key_part, query_places, key_places, query_groups, key_groups, bias_lookup
):
    bucket = bucket_of(key_places[None, :] - query_places[:, None])
    levels = jnp.arange(bias_lookup.shape[0], dtype=jnp.int32)
    one_hot_mask = (bucket[None] == levels[:, None, None]).astype(jnp.bfloat16)
    bias_patch_block = jnp.einsum(
        "ctf,cx->xtf", one_hot_mask, bias_lookup, preferred_element_type=jnp.float32
    )
    raw_scores = (
        jnp.einsum("qhd,khd->hqk", query_part, key_part, preferred_element_type=jnp.float32)
        + bias_patch_block
    )
    same_group = query_groups[:, None] == key_groups[None, :]
    return (one_hot_mask, jnp.where(same_group[None], raw_scores, MASKED))


def shards(
    hidden,
    group_ids,
    norm1_gain,
    query_weight,
    key_weight,
    value_weight,
    out_weight,
    relative_bias,
    norm2_gain,
    gate_weight,
    up_weight,
    down_projection_weight,
    out_grad,
):
    tok_rows = hidden.shape[1]
    head_count = relative_bias.shape[1]
    inner_width = query_weight.shape[1]
    head_depth = inner_width // head_count
    row_length = group_ids.shape[1]
    row_start = lax.axis_index("seq") * tok_rows
    key_block = min(1024, row_length)
    block_count = row_length // key_block
    row_groups = group_ids[0]
    own_groups = lax.dynamic_slice_in_dim(row_groups, row_start, tok_rows)
    own_places = row_start + jnp.arange(tok_rows, dtype=jnp.int32)
    all_places = jnp.arange(row_length, dtype=jnp.int32)

    def key_blocks(key_rows, value_rows):
        return (
            key_rows.reshape(block_count, key_block, head_count, head_depth),
            value_rows.reshape(block_count, key_block, head_count, head_depth),
            row_groups.reshape(block_count, key_block),
            all_places.reshape(block_count, key_block),
        )

    inputs = hidden[0].astype(jnp.float32)
    normed, norm_pull = jax.vjp(rms_norm, inputs, norm1_gain.astype(jnp.float32))
    normed_low = normed.astype(jnp.bfloat16)
    query_low = jnp.dot(normed_low, query_weight, preferred_element_type=jnp.float32).astype(
        jnp.bfloat16
    )
    key_low = jnp.dot(normed_low, key_weight, preferred_element_type=jnp.float32).astype(
        jnp.bfloat16
    )
    value_low = jnp.dot(normed_low, value_weight, preferred_element_type=jnp.float32).astype(
        jnp.bfloat16
    )
    key_all, value_all = (
        lax.all_gather(key_low, "seq", axis=0, tiled=True),
        lax.all_gather(value_low, "seq", axis=0, tiled=True),
    )
    query_heads = query_low.reshape(tok_rows, head_count, head_depth)

    def gather_stats(carry_state, scanned):
        running_max, running_sum = carry_state
        key_part, value_part, key_groups, key_places = scanned
        one_hot_mask, scores = scores_of(
            query_heads, key_part, own_places, key_places, own_groups, key_groups, relative_bias
        )
        new_max = jnp.maximum(running_max, jnp.max(scores, axis=-1))
        running_sum = running_sum * jnp.exp(running_max - new_max) + jnp.sum(
            jnp.exp(scores - new_max[..., None]), axis=-1
        )
        return ((new_max, running_sum), None)

    stats_init = (
        jnp.full((head_count, tok_rows), MASKED, jnp.float32),
        jnp.zeros((head_count, tok_rows), jnp.float32),
    )
    (running_max, running_sum), _ = lax.scan(
        gather_stats, stats_init, key_blocks(key_all, value_all)
    )
    log_total = running_max + jnp.log(running_sum)

    def gather_values(summed, scanned):
        key_part, value_part, key_groups, key_places = scanned
        one_hot_mask, scores = scores_of(
            query_heads, key_part, own_places, key_places, own_groups, key_groups, relative_bias
        )
        attention_low = jnp.exp(scores - log_total[..., None]).astype(jnp.bfloat16)
        return (
            summed
            + jnp.einsum(
                "hqk,khd->qhd", attention_low, value_part, preferred_element_type=jnp.float32
            ),
            None,
        )

    mixed, _ = lax.scan(
        gather_values,
        jnp.zeros((tok_rows, head_count, head_depth), jnp.float32),
        key_blocks(key_all, value_all),
    )
    mixed_low = mixed.reshape(tok_rows, inner_width).astype(jnp.bfloat16)
    middle = inputs + jnp.dot(mixed_low, out_weight, preferred_element_type=jnp.float32)
    normed_two, norm_two_pull = jax.vjp(rms_norm, middle, norm2_gain.astype(jnp.float32))
    normed_two_low = normed_two.astype(jnp.bfloat16)
    gate_proj = jnp.dot(normed_two_low, gate_weight, preferred_element_type=jnp.float32)
    up_proj = jnp.dot(normed_two_low, up_weight, preferred_element_type=jnp.float32)
    activated, act_pull = jax.vjp(activate, gate_proj, up_proj)
    activated_low = activated.astype(jnp.bfloat16)
    result = middle + jnp.dot(
        activated_low, down_projection_weight, preferred_element_type=jnp.float32
    )
    block_out = result.astype(jnp.bfloat16)[None]
    cotangent_low = out_grad[0]
    grad_down = dot_rows(activated_low, cotangent_low)
    act_grad = dot_cols(cotangent_low, down_projection_weight)
    gate_grad, up_grad = act_pull(act_grad)
    gate_grad_low = gate_grad.astype(jnp.bfloat16)
    up_grad_low = up_grad.astype(jnp.bfloat16)
    grad_gate = dot_rows(normed_two_low, gate_grad_low)
    grad_up = dot_rows(normed_two_low, up_grad_low)
    normed_two_grad = dot_cols(gate_grad_low, gate_weight) + dot_cols(up_grad_low, up_weight)
    middle_norm_grad, grad_gain_two = norm_two_pull(normed_two_grad)
    middle_grad = cotangent_low.astype(jnp.float32) + middle_norm_grad
    branch_grad_low = middle_grad.astype(jnp.bfloat16)
    grad_out = dot_rows(mixed_low, branch_grad_low)
    mixed_grad_low = (
        dot_cols(branch_grad_low, out_weight)
        .astype(jnp.bfloat16)
        .reshape(tok_rows, head_count, head_depth)
    )
    row_dots = jnp.einsum("qhd,qhd->hq", mixed_grad_low.astype(jnp.float32), mixed)
    key_back, value_back = (
        lax.all_gather(key_low, "seq", axis=0, tiled=True),
        lax.all_gather(value_low, "seq", axis=0, tiled=True),
    )
    grads_init = (
        jnp.zeros((tok_rows, head_count, head_depth), jnp.float32),
        jnp.zeros(relative_bias.shape, jnp.float32),
    )

    def backward_block(carry_state, scanned):
        query_grad, table_grad = carry_state
        key_part, value_part, key_groups, key_places = scanned
        one_hot_mask, scores = scores_of(
            query_heads, key_part, own_places, key_places, own_groups, key_groups, relative_bias
        )
        attention = jnp.exp(scores - log_total[..., None])
        grad_weights = jnp.einsum(
            "qhd,khd->hqk", mixed_grad_low, value_part, preferred_element_type=jnp.float32
        )
        score_gradients = (attention * (grad_weights - row_dots[..., None])).astype(jnp.bfloat16)
        query_grad = query_grad + jnp.einsum(
            "hqk,khd->qhd", score_gradients, key_part, preferred_element_type=jnp.float32
        )
        table_grad = table_grad + jnp.einsum(
            "oei,cei->oc", one_hot_mask, score_gradients, preferred_element_type=jnp.float32
        )
        key_grad = jnp.einsum(
            "hqk,qhd->khd", score_gradients, query_heads, preferred_element_type=jnp.float32
        )
        value_grad = jnp.einsum(
            "hqk,qhd->khd",
            attention.astype(jnp.bfloat16),
            mixed_grad_low,
            preferred_element_type=jnp.float32,
        )
        return ((query_grad, table_grad), (key_grad, value_grad))

    (query_grad, table_grad), (key_terms, value_terms) = lax.scan(
        backward_block, grads_init, key_blocks(key_back, value_back)
    )
    key_grad, value_grad = (
        lax.psum_scatter(
            key_terms.reshape(row_length, inner_width), "seq", scatter_dimension=0, tiled=True
        ),
        lax.psum_scatter(
            value_terms.reshape(row_length, inner_width), "seq", scatter_dimension=0, tiled=True
        ),
    )
    query_grad_low = query_grad.reshape(tok_rows, inner_width).astype(jnp.bfloat16)
    key_grad_low = key_grad.astype(jnp.bfloat16)
    value_grad_low = value_grad.astype(jnp.bfloat16)
    grad_query = dot_rows(normed_low, query_grad_low)
    grad_key = dot_rows(normed_low, key_grad_low)
    grad_value = dot_rows(normed_low, value_grad_low)
    normed_grad = (
        dot_cols(query_grad_low, query_weight)
        + dot_cols(key_grad_low, key_weight)
        + dot_cols(value_grad_low, value_weight)
    )
    input_norm_grad, grad_gain_one = norm_pull(normed_grad)
    hidden_grad = (middle_grad + input_norm_grad)[None]
    local_grads = (
        grad_gain_one,
        grad_query,
        grad_key,
        grad_value,
        grad_out,
        table_grad.reshape(-1),
        grad_gain_two,
        grad_gate,
        grad_up,
        grad_down,
    )
    shared = (
        lax.psum_scatter(local_grads[0], "seq", scatter_dimension=0, tiled=True),
        lax.psum_scatter(local_grads[1], "seq", scatter_dimension=0, tiled=True),
        lax.psum_scatter(local_grads[2], "seq", scatter_dimension=0, tiled=True),
        lax.psum_scatter(local_grads[3], "seq", scatter_dimension=0, tiled=True),
        lax.psum_scatter(local_grads[4], "seq", scatter_dimension=0, tiled=True),
        lax.psum_scatter(local_grads[5], "seq", scatter_dimension=0, tiled=True),
        lax.psum_scatter(local_grads[6], "seq", scatter_dimension=0, tiled=True),
        lax.psum_scatter(local_grads[7], "seq", scatter_dimension=0, tiled=True),
        lax.psum_scatter(local_grads[8], "seq", scatter_dimension=0, tiled=True),
        lax.psum_scatter(local_grads[9], "seq", scatter_dimension=0, tiled=True),
    )
    shared = (
        lax.psum(shared[0].astype(jnp.bfloat16), "dp").astype(jnp.float32),
        lax.psum(shared[1].astype(jnp.bfloat16), "dp").astype(jnp.float32),
        lax.psum(shared[2].astype(jnp.bfloat16), "dp").astype(jnp.float32),
        lax.psum(shared[3].astype(jnp.bfloat16), "dp").astype(jnp.float32),
        lax.psum(shared[4].astype(jnp.bfloat16), "dp").astype(jnp.float32),
        lax.psum(shared[5].astype(jnp.bfloat16), "dp").astype(jnp.float32),
        lax.psum(shared[6].astype(jnp.bfloat16), "dp").astype(jnp.float32),
        lax.psum(shared[7].astype(jnp.bfloat16), "dp").astype(jnp.float32),
        lax.psum(shared[8].astype(jnp.bfloat16), "dp").astype(jnp.float32),
        lax.psum(shared[9].astype(jnp.bfloat16), "dp").astype(jnp.float32),
    )
    summed = (
        lax.all_gather(shared[0].astype(jnp.bfloat16), "seq", axis=0, tiled=True).astype(
            jnp.float32
        ),
        lax.all_gather(shared[1].astype(jnp.bfloat16), "seq", axis=0, tiled=True).astype(
            jnp.float32
        ),
        lax.all_gather(shared[2].astype(jnp.bfloat16), "seq", axis=0, tiled=True).astype(
            jnp.float32
        ),
        lax.all_gather(shared[3].astype(jnp.bfloat16), "seq", axis=0, tiled=True).astype(
            jnp.float32
        ),
        lax.all_gather(shared[4].astype(jnp.bfloat16), "seq", axis=0, tiled=True).astype(
            jnp.float32
        ),
        lax.all_gather(shared[5].astype(jnp.bfloat16), "seq", axis=0, tiled=True).astype(
            jnp.float32
        ),
        lax.all_gather(shared[6].astype(jnp.bfloat16), "seq", axis=0, tiled=True).astype(
            jnp.float32
        ),
        lax.all_gather(shared[7].astype(jnp.bfloat16), "seq", axis=0, tiled=True).astype(
            jnp.float32
        ),
        lax.all_gather(shared[8].astype(jnp.bfloat16), "seq", axis=0, tiled=True).astype(
            jnp.float32
        ),
        lax.all_gather(shared[9].astype(jnp.bfloat16), "seq", axis=0, tiled=True).astype(
            jnp.float32
        ),
    )
    return (
        block_out,
        hidden_grad,
        summed[0],
        summed[1],
        summed[2],
        summed[3],
        summed[4],
        summed[5].reshape(relative_bias.shape),
        summed[6],
        summed[7],
        summed[8],
        summed[9],
    )


def solution(mesh):
    placed = (P("dp", "seq", None), P("dp", None)) + (P(),) * 10 + (P("dp", "seq", None),)
    out_specs = (P("dp", "seq", None),) * 2 + (P(),) * 10
    count = mesh.shape["seq"]

    def run(*args):
        hidden, query_weight, relative_bias = args[0], args[3], args[7]
        head_count = relative_bias.shape[1]
        inner = query_weight.shape[1] // count
        fits = (
            mesh.shape["dp"] == 4
            and count % 2 == 0
            and head_count % count == 0
            and inner == LANES
            and hidden.shape[2] == count * LANES
            and hidden.shape[1] == count * LANES
            and args[9].shape[1] % (4 * LANES) == 2 * LANES
        )
        body = functools.partial(split_shards, count=count) if fits else shards
        return jax.shard_map(
            body, mesh=mesh, in_specs=placed, out_specs=out_specs, check_vma=False
        )(*args)

    return run
```

```python
import functools
import types

import jax
import jax.numpy as jnp
from jax import lax
from jax.experimental import pallas as pl
from jax.experimental.pallas import tpu as pltpu
from jax.sharding import PartitionSpec as P

EPSILON = 1e-06
MASKED = -1e30
THRESHOLDS = (12, 16, 23, 32, 46, 64, 91)
MESH = pl.DeviceIdType.MESH
BF = jnp.bfloat16
F32 = jnp.float32
LANES = 128
ANY = pl.BlockSpec(memory_space=pl.ANY)
VMEM = pl.BlockSpec(memory_space=pltpu.VMEM)


def bucket_of(relative):
    distance = jnp.abs(relative)
    bucket_level = jnp.full(relative.shape, 8, jnp.int32)
    for boundary in THRESHOLDS:
        bucket_level = bucket_level + (distance >= boundary).astype(jnp.int32)
    near_bucket = jnp.where(distance < 8, distance, bucket_level)
    return near_bucket + 16 * (relative > 0).astype(jnp.int32)


def dot(left_mat, right_mat):
    return jnp.dot(left_mat, right_mat, preferred_element_type=F32)


def dot_rows(left_mat, right_mat):
    return lax.dot_general(
        left_mat, right_mat, (((0,), (0,)), ((), ())), preferred_element_type=F32
    )


def dot_cols(left_mat, right_mat):
    return lax.dot_general(
        left_mat, right_mat, (((1,), (1,)), ((), ())), preferred_element_type=F32
    )


def ring_place(index, count):
    odd = index % 2
    return (1 - odd) * (index // 2) + odd * ((2 * count - 1 - index) // 2)


def ring_index(place, count):
    late = place // (count // 2)
    return (1 - late) * 2 * place + late * (2 * count - 1 - 2 * place)


def greet(targets):
    barrier = pltpu.get_barrier_semaphore()
    for target in targets:
        pl.semaphore_signal(barrier, inc=1, device_id=target, device_id_type=MESH)
    pl.semaphore_wait(barrier, len(targets))


def comm_params(collective_id, vmem=None):
    return pltpu.CompilerParams(
        collective_id=collective_id, has_side_effects=True, vmem_limit_bytes=vmem
    )


class Spot:
    def __init__(self, count):
        self.count = count
        self.half = count // 2
        self.me = lax.axis_index("seq")
        self.dp = lax.axis_index("dp")
        self.place = ring_place(self.me, count)
        self.nexts = tuple((self.dp, self.at(step)) for step in (1, -1))
        self.far_dp = (self.dp + 2) % 4
        self.twin_dp = self.dp + 1 - 2 * (self.dp % 2)
        self.far = (self.far_dp, self.me)
        self.twin = (self.twin_dp, self.me)
        self.others = tuple((self.dp, (self.me + step) % count) for step in range(1, count))

    def at(self, step):
        return ring_index((self.place + (step + self.count) % self.count) % self.count, self.count)

    def back(self, way, hop):
        return self.at(-hop if way == 0 else hop)


def push(source, target, send_sem, recv_sem, device, split=1):
    def copy_of(source, target):
        return pltpu.make_async_remote_copy(
            src_ref=source,
            dst_ref=target,
            send_sem=send_sem,
            recv_sem=recv_sem,
            device_id=device,
            device_id_type=MESH,
        )

    whole = copy_of(source, target)
    if split == 1:
        whole.start()
        return whole
    rows = source.shape[0] // split
    for index in range(split):
        window = pl.ds(index * rows, rows)
        copy_of(source.at[window], target.at[window]).start()
    return whole


def wait_all(like, sem):
    pltpu.make_async_copy(like, like, sem).wait()


class RingGather:
    def __init__(self, spot, own, blocks, send_sem, recv_sems, split=1):
        self.spot, self.own, self.blocks, self.split = spot, own, blocks, split
        self.send_sem, self.recv_sems = send_sem, recv_sems
        self.rows = blocks.shape[1] // 2
        self.copies = {}

    def into(self, origin, piece):
        return self.blocks.at[origin, pl.ds(piece * self.rows, self.rows)]

    def pieces(self, way, hop):
        return (0, 1) if hop < self.spot.half - 1 else (way,)

    def forward(self, hop, way, piece):
        spot = self.spot
        if hop >= spot.half or piece not in self.pieces(way, hop):
            return
        origin = spot.back(way, hop)
        target = self.into(origin, piece)
        self.copies[hop, way, piece] = push(
            self.own.at[pl.ds(piece * self.rows, self.rows)] if hop == 0 else target,
            target,
            self.send_sem,
            self.recv_sems.at[way, hop, piece],
            spot.nexts[way],
            self.split,
        )

    def begin(self, piece):
        for way in range(2):
            self.forward(0, way, piece)

    def step(self, hop):
        for piece in range(2):
            for way in range(2):
                if (hop, way, piece) in self.copies:
                    self.copies[hop, way, piece].wait_recv()
                    self.forward(hop + 1, way, piece)

    def finish(self):
        wait_all(self.blocks.at[pl.ds(0, self.spot.count - 1)], self.send_sem)


class RingSum:
    def __init__(self, spot, terms, buf, send_sem, recv_sems):
        self.spot, self.terms, self.buf = spot, terms, buf
        self.send_sem, self.recv_sems = send_sem, recv_sems
        self.rows = terms.shape[1] // 2
        self.copies = {}

    def term(self, block, piece):
        return self.terms.at[block, pl.ds(piece * self.rows, self.rows)]

    def send(self, hop, way, piece, source):
        self.copies[hop, way, piece] = push(
            source,
            self.buf.at[way, hop, piece],
            self.send_sem,
            self.recv_sems.at[way, hop, piece],
            self.spot.nexts[way],
        )

    def block(self, way, hop):
        step = self.spot.half - hop
        return self.spot.at(step if way == 0 else -step)

    def begin(self):
        for way in range(2):
            self.send(0, way, way, self.term(self.block(way, 0), way))
        for way in range(2):
            self.send(1, way, 1 - way, self.term(self.block(way, 1), 1 - way))

    def step(self, hop):
        for piece in range(2):
            for way in range(2):
                if (hop, way, piece) not in self.copies or hop + 1 >= self.spot.half:
                    continue
                self.copies[hop, way, piece].wait_recv()
                term = self.term(self.block(way, hop + 1), piece)
                self.buf[way, hop, piece] = (
                    self.buf[way, hop, piece].astype(F32) + term[...].astype(F32)
                ).astype(BF)
                self.send(hop + 1, way, piece, self.buf.at[way, hop, piece])

    def total(self, out):
        last = self.spot.half - 1
        for piece in range(2):
            value = self.term(self.spot.me, piece)[...].astype(F32)
            for way in range(2):
                self.copies[last, way, piece].wait_recv()
                value = value + self.buf[way, last, piece].astype(F32)
            out[pl.ds(piece * self.rows, self.rows)] = value.astype(BF)

    def finish(self):
        wait_all(self.terms.at[pl.ds(0, self.spot.count - 1)], self.send_sem)


class PairGather:
    def __init__(self, spot, own_ref, buf, send_sems, recv_sems):
        self.spot, self.buf = spot, buf
        self.send_sems, self.recv_sems = send_sems, recv_sems
        rows = own_ref.shape[0]
        self.low, self.high = pl.ds(0, rows), pl.ds(rows, rows)
        self.far = self.push(1, own_ref, buf.at[1, self.low], spot.far)
        self.near = self.push(0, own_ref, buf.at[0, self.high], spot.twin)

    def push(self, index, source, target, device):
        return push(source, target, self.send_sems.at[index], self.recv_sems.at[index], device)

    def relay(self):
        self.far.wait_recv()
        self.cross = self.push(
            2, self.buf.at[1, self.low], self.buf.at[1, self.high], self.spot.twin
        )

    def finish(self):
        for copy in (self.near, self.far, self.cross):
            copy.wait_send()


class PairSum:
    def __init__(self, spot, kept, outs, ins, far_out, far_in, send_sems, recv_sems):
        self.spot, self.kept, self.outs, self.ins = spot, kept, outs, ins
        self.far_out, self.far_in = far_out, far_in
        self.send_sems, self.recv_sems = send_sems, recv_sems
        self.copies = []

    def near(self, half):
        self.copies.append(
            push(
                self.outs.at[half], self.ins.at[half],
                self.send_sems.at[half], self.recv_sems.at[half], self.spot.twin,
            )
        )

    def over(self):
        self.copies[1].wait_recv()
        self.far_out[...] = (self.kept[1] + self.ins[1].astype(F32)).astype(BF)
        self.copies.append(
            push(
                self.far_out, self.far_in, self.send_sems.at[2], self.recv_sems.at[2], self.spot.far
            )
        )

    def total(self):
        self.copies[0].wait_recv()
        self.copies[2].wait_recv()
        return self.kept[0] + self.ins[0].astype(F32) + self.far_in[...].astype(F32)

    def finish(self):
        for copy in self.copies:
            copy.wait_send()


class MeshGather:
    def __init__(self, spot, x_ref, o_ref, share, sems):
        self.spot, self.x_ref, self.o_ref = spot, x_ref, o_ref
        self.ring_s, self.ring_r, self.x_s, self.far_r, self.own_r, self.core_s, self.core_r = sems
        rows = x_ref.shape[0]
        first = rows * share // 100 // 32 * 32
        cuts = (0, first // 2, first, first + (rows - first) // 2 // 16 * 16, rows)
        self.parts = (pl.ds(0, first), pl.ds(first, rows - first))
        self.windows = [
            [pl.ds(cuts[2 * part + piece], cuts[2 * part + piece + 1] - cuts[2 * part + piece]) for piece in range(2)]
            for part in range(2)
        ]
        self.ring, self.x = {}, {}

    def into(self, dp, origin, part, piece):
        return self.o_ref.at[dp, origin, self.windows[part][piece]]

    def pieces(self, way, hop):
        return (0, 1) if hop < self.spot.half - 1 else (way,)

    def to_core(self, source, target):
        push(source, target, self.core_s, self.core_r, self.spot.twin)

    def pass_on(self, part, lane, hop, way, piece, source):
        spot = self.spot
        dp = spot.far_dp if lane else spot.dp
        origin = spot.me if way is None else spot.back(way, hop)
        target = self.into(dp, origin, part, piece)
        source = target if source is None else source
        slot = 0 if way is None else 2 * hop - 1 + way
        for onward in (0, 1) if way is None else (way,):
            if hop < spot.half and piece in self.pieces(onward, hop):
                self.ring[part, lane, hop, onward, piece] = push(
                    source, target,
                    self.ring_s.at[part + lane],
                    self.ring_r.at[2 * (part + lane) + onward, hop, piece],
                    spot.nexts[onward],
                )
        if part == 0:
            self.x[part, slot, piece] = push(
                source, target, self.x_s.at[0], self.far_r.at[slot, piece], spot.far
            )
        self.to_core(source, target)

    def begin(self):
        spot = self.spot
        for piece in range(2):
            self.x[1, 0, piece] = push(
                self.x_ref.at[self.windows[1][piece]],
                self.into(spot.dp, spot.me, 1, piece),
                self.x_s.at[1], self.own_r.at[piece], spot.far,
            )
        for part in range(2):
            for piece in range(2):
                self.pass_on(part, 0, 0, None, piece, self.x_ref.at[self.windows[part][piece]])

    def begin_far(self):
        for piece in range(2):
            self.x[1, 0, piece].wait_recv()
            self.pass_on(1, 1, 0, None, piece, None)

    def step(self, hop):
        for piece in range(2):
            for part, lane in ((0, 0), (1, 0), (1, 1)):
                for way in range(2):
                    key = (part, lane, hop, way, piece)
                    if key in self.ring:
                        self.ring[key].wait_recv()
                        self.pass_on(part, lane, hop + 1, way, piece, None)

    def step_far(self, hop):
        spot = self.spot
        for piece in range(2):
            for way in (None,) if hop == 0 else range(2):
                slot = 0 if way is None else 2 * hop - 1 + way
                if (0, slot, piece) in self.x:
                    self.x[0, slot, piece].wait_recv()
                    origin = spot.me if way is None else spot.back(way, hop)
                    target = self.into(spot.far_dp, origin, 0, piece)
                    self.to_core(target, target)

    def finish(self):
        o_ref, count = self.o_ref, self.spot.count
        wait_all(o_ref.at[pl.ds(0, 2)], self.core_r)
        wait_all(o_ref.at[pl.ds(0, 2)], self.core_s)
        for index in range(3):
            wait_all(o_ref.at[0, pl.ds(0, count - 1), self.parts[min(index, 1)]], self.ring_s.at[index])
        wait_all(o_ref.at[0, :, self.parts[0]], self.x_s.at[0])
        wait_all(self.x_ref.at[self.parts[1]], self.x_s.at[1])


def mesh_sems(count):
    half = count // 2
    dma = pltpu.SemaphoreType.DMA
    return [
        dma((3,)), dma((6, half, 2)), dma((2,)), dma((2 * half + 1, 2)), dma((2,)), dma(()), dma(())
    ]


def near_buckets(rows):
    shape = (rows, rows + 2 * LANES)
    column = lax.broadcasted_iota(jnp.int32, shape, 1) - LANES
    return bucket_of(column - lax.broadcasted_iota(jnp.int32, shape, 0))


def strip_window(step, rows, length):
    return pl.ds(pl.multiple_of(length - rows - step * rows, LANES), length)


def scale_of(value):
    return lax.rsqrt(jnp.mean(value * value, axis=-1, keepdims=True) + EPSILON)


def row_block(origin, rows):
    return pl.ds(pl.multiple_of(origin * rows, rows), rows)


def exclusive(index, bit):
    return index + bit - 2 * bit * ((index // bit) % 2)


def layer_body(count, heads, depth, ff, names, *refs):
    r = types.SimpleNamespace(**dict(zip(names, refs)))
    spot = Spot(count)
    hidden_ref, grad_ref = r.hidden, r.out_grad
    rows, width = hidden_ref.shape
    length = count * rows
    inner = heads * depth
    span = r.gate_w.shape[1]
    odd = spot.dp % 2
    ff_start = pl.multiple_of(spot.dp * ff - odd * (span - ff), span - ff)
    own_columns = pl.ds(pl.multiple_of(spot.me * LANES, LANES), LANES)
    greet(spot.nexts + (spot.far, spot.twin))

    loads = {}

    def load(name, source, target):
        copy = pltpu.make_async_copy(source, target, r.load_sems.at[len(loads)])
        copy.start()
        loads[name] = copy

    ring = RingGather(
        spot,
        hidden_ref,
        r.row,
        r.row_s,
        r.row_r,
    )
    ring.begin(0)
    sources = (r.query_weight, r.key_weight, r.value_weight)
    for part, source in enumerate(sources):
        load(
            part,
            source.at[:, pl.ds(pl.multiple_of(spot.me * inner, inner), inner)],
            r.qkv_w.at[:, pl.ds(part * inner, inner)],
        )
    load("out", r.out_weight, r.out_w)
    ff_columns = pl.ds(pl.multiple_of(ff_start, LANES), span)
    load("gate", r.gate_weight.at[:, ff_columns], r.gate_w)
    load("up", r.up_weight.at[:, ff_columns], r.up_w)
    load("down", r.down_weight.at[pl.ds(ff_start, span)], r.down_w)
    for part, source in enumerate(sources):
        load(3 + part, source, r.full_w.at[part])

    qkv, normed, weights = r.qkv, r.normed, r.weights
    both_rows = 2 * rows
    low = length - rows - LANES
    bucket = near_buckets(rows)
    near_span = bucket.shape[1]
    score_strip = r.score_strip
    strip = score_strip.at[:, pl.ds(0, rows)]
    score_low = length - both_rows - LANES
    score_bucket = near_buckets(both_rows)
    score_span = score_bucket.shape[1]
    head_count, level_count = r.table.shape
    chosen = lax.broadcasted_iota(jnp.int32, (8, head_count), 1) == (
        spot.me * heads + lax.broadcasted_iota(jnp.int32, (8, head_count), 0)
    )
    table = dot(chosen.astype(BF), r.table[...])
    for head in range(heads):
        entry = lambda level: table[head : head + 1, level : level + 1]
        value = jnp.zeros(score_bucket.shape, F32)
        for level in range(level_count):
            value = jnp.where(score_bucket == level, entry(level), value)
        after = score_strip.shape[2] - score_low - score_span
        score_strip[head, :, :score_low] = jnp.broadcast_to(entry(15), (both_rows, score_low))
        score_strip[head, :, score_low : score_low + score_span] = value
        score_strip[head, :, score_low + score_span :] = jnp.broadcast_to(
            entry(31), (both_rows, after)
        )
    ring.begin(1)
    cots = PairGather(spot, grad_ref, r.cot, r.cot_s, r.cot_r)
    gain_one = r.gain_one[...].astype(F32).reshape(1, width)
    gain_two = r.gain_two[...].astype(F32).reshape(1, width)

    def project(origin, block):
        value = block.astype(F32)
        low_value = (value * scale_of(value) * gain_one).astype(BF)
        mine = row_block(origin, rows)
        normed[mine] = low_value
        qkv[mine] = dot(low_value, r.qkv_w[...]).astype(BF)

    for part in range(3):
        loads[part].wait()
    project(spot.me, hidden_ref[...])
    for hop in range(spot.half):
        ring.step(hop)
        if hop < spot.half - 1:

            def both(side, carry, hop=hop):
                origin = spot.at((1 - 2 * side) * (hop + 1))
                project(origin, r.row[origin])
                return carry

            lax.fori_loop(0, 2, both, 0)
        else:
            origin = spot.at(spot.half)
            project(origin, r.row[origin])
    ring.finish()
    cots.relay()
    r.cot[0, :rows] = grad_ref[...]
    mixed_heads, mixed = r.mixed_heads, r.mixed

    def attend(block):
        mine = row_block(block, both_rows)
        turned_ids = jnp.broadcast_to(r.row_ids[:, mine], (LANES, both_rows)).T
        same = turned_ids[:, :1] == r.row_ids[...]
        window = strip_window(block, both_rows, length)
        for head in range(heads):
            columns = slice(head * depth, (head + 1) * depth)
            key = qkv[:, inner + head * depth : inner + (head + 1) * depth]
            value = qkv[:, 2 * inner + head * depth : 2 * inner + (head + 1) * depth]
            scores = dot_cols(qkv[mine, columns], key) + score_strip[head, :, window]
            scores = jnp.where(same, scores, MASKED)
            top = jnp.max(scores, axis=1, keepdims=True)
            weight = jnp.exp(scores - top)
            weight = weight * (1.0 / jnp.sum(weight, axis=1, keepdims=True))
            weight = weight.astype(BF)
            weights[head, mine] = weight
            mixed_heads[mine, columns] = dot(weight, value).astype(BF)

    def mixed_send(target):
        push(
            mixed_heads.at[row_block(target, rows)],
            mixed.at[:, own_columns],
            r.mixed_s,
            r.mixed_r,
            (spot.dp, target),
        )

    def attend_and_send(step, carry):
        block = (spot.me // 2 + step) % (count // 2)
        attend(block)
        for index in range(2):
            mixed_send(2 * block + index)
        return carry

    lax.fori_loop(1, count // 2, attend_and_send, 0)
    attend(spot.me // 2)
    mixed_send(exclusive(spot.me, 1))
    mixed[:, own_columns] = mixed_heads[row_block(spot.me, rows)]

    loads["out"].wait()
    wait_all(mixed.at[:, pl.ds(0, width - LANES)], r.mixed_r)
    inputs = hidden_ref[...].astype(F32)
    middle_ref = r.middle
    middle = inputs + dot(mixed[...], r.out_w[...])
    middle_ref[...] = middle
    tok, cot = r.tok, r.cot
    tok[0, :rows] = (middle * scale_of(middle) * gain_two).astype(BF)
    toks = PairGather(spot, tok.at[0, pl.ds(0, rows)], tok, r.tok_s, r.tok_r)
    gate_w, up_w, down_w = r.gate_w, r.up_w, r.down_w
    act, gate_g, up_g = r.act, r.gate_g, r.up_g
    for name in ("gate", "up", "down"):
        loads[name].wait()
    chunk = 256
    grads = PairSum(
        spot, r.grad_kept, r.grad_outs, r.grad_ins, r.grad_far_out, r.grad_far_in,
        r.grad_s, r.grad_r,
    )
    outs = PairSum(
        spot, r.out_kept, r.out_outs, r.out_ins, r.out_far_out, r.out_far_in,
        r.out_s, r.out_r,
    )

    def activate_half(half):
        mine = pl.ds(half * both_rows, both_rows)

        def tile(index, carry):
            columns = row_block(index, chunk)
            gate = dot(tok[half], gate_w[:, columns])
            up = dot(tok[half], up_w[:, columns])
            act_grad = dot_cols(cot[half], down_w[columns])
            place = index * chunk + lax.broadcasted_iota(jnp.int32, (1, chunk), 1)
            place = place - odd * (span - ff)
            inside = (place >= 0) & (place < ff)
            root = 0.7978845608028654
            squared = gate * gate
            bend = jnp.tanh(root * (gate + 0.044715 * gate * squared))
            share = 0.5 * (1.0 + bend)
            gelu = gate * share
            slope = share + 0.5 * gate * (1.0 - bend * bend) * root * (
                1.0 + 3 * 0.044715 * squared
            )
            act[mine, columns] = jnp.where(inside, gelu * up, 0.0).astype(BF)
            gate_g[mine, columns] = jnp.where(inside, act_grad * up * slope, 0.0).astype(BF)
            up_g[mine, columns] = jnp.where(inside, act_grad * gelu, 0.0).astype(BF)
            return carry

        lax.fori_loop(0, span // chunk, tile, 0)

    def spread(pair_sum, half, product):
        def tile(index, carry):
            columns = row_block(index, chunk)
            value = product(columns)
            pair_sum.kept[half, :, columns] = value[:rows]
            pair_sum.outs[half, :, columns] = value[rows:].astype(BF)
            return carry

        lax.fori_loop(0, width // chunk, tile, 0)
        pair_sum.near(half)

    def back_half(half):
        mine = pl.ds(half * both_rows, both_rows)
        spread(
            grads,
            half,
            lambda columns: dot_cols(gate_g[mine], gate_w[columns])
            + dot_cols(up_g[mine], up_w[columns]),
        )

    def out_half(half):
        mine = pl.ds(half * both_rows, both_rows)
        spread(outs, half, lambda columns: dot(act[mine], down_w[:, columns]))

    cots.near.wait_recv()
    cots.cross.wait_recv()
    toks.near.wait_recv()
    activate_half(0)
    toks.relay()
    back_half(0)
    toks.cross.wait_recv()
    activate_half(1)
    back_half(1)

    down_terms, pair_terms = r.down_terms, r.pair_terms
    spare = span - ff

    def down_tile(index, carry):
        columns = row_block(index, LANES)
        value = dot_rows(act[:both_rows], cot[0, :, columns]) + dot_rows(
            act[both_rows:], cot[1, :, columns]
        )
        down_terms[index] = jnp.where(odd == 1, value[spare:], value[:ff]).astype(BF)
        return carry

    lax.fori_loop(0, count, down_tile, 0)
    down_sum = RingSum(spot, down_terms, r.down_buf, r.down_s, r.down_r)
    down_sum.begin()
    grads.over()
    full = ff // LANES
    lane = lax.broadcasted_iota(jnp.int32, (LANES, LANES), 1)

    def pair_tile(index, carry):
        columns = row_block(index, LANES)
        parts = []
        for source in (gate_g, up_g):
            parts.append(
                dot_rows(tok[0, :, columns], source[:both_rows])
                + dot_rows(tok[1, :, columns], source[both_rows:])
            )
        cut = lambda value, place: value[:, place * LANES : (place + 1) * LANES]
        for part, value in enumerate(parts):
            for place in range(full):
                start = (part * full + place) * LANES
                pair_terms[index, start : start + LANES] = jnp.where(
                    odd == 1, cut(value, place + 1), cut(value, place)
                ).astype(BF)
        edges = [jnp.where(odd == 1, cut(value, 0), cut(value, full)) for value in parts]
        turned = pltpu.roll(edges[1], LANES // 2, 1)
        lower = (lane < LANES // 2).astype(jnp.int32)
        pair_terms[index, 2 * full * LANES :] = jnp.where(lower == odd, turned, edges[0]).astype(BF)
        return carry

    lax.fori_loop(0, count, pair_tile, 0)
    pair_sum = RingSum(spot, pair_terms, r.pair_buf, r.pair_s, r.pair_r)
    pair_sum.begin()
    down_sum.step(0)
    out_half(0)
    out_half(1)

    normed_two_grad = grads.total()
    middle = middle_ref[...]
    scale_two = scale_of(middle)
    lifted = gain_two * normed_two_grad
    middle_grad = (
        grad_ref[...].astype(F32)
        + scale_two * lifted
        - middle * (scale_two * scale_two * scale_two)
        * jnp.mean(middle * lifted, axis=-1, keepdims=True)
    )
    middle_grad_ref = r.middle_grad
    middle_grad_ref[...] = middle_grad
    small = r.small
    small[...] = jnp.zeros_like(small)
    gain_grad = jnp.sum(normed_two_grad * middle * scale_two, axis=0, keepdims=True)
    tiles = width // LANES
    for tile in range(tiles):
        small[tiles + tile : tiles + tile + 1] = gain_grad[:, tile * LANES : (tile + 1) * LANES]
    branch, own_branch = r.row, r.own_branch
    own_branch[...] = middle_grad.astype(BF)
    branches = RingGather(
        spot,
        own_branch,
        branch,
        r.branch_s,
        r.branch_r,
        SPLITS[0],
    )
    keys, values, dqkv, packed = r.keys, r.values, r.dqkv, r.packed

    own_out = r.out_w.at[row_block(spot.me, inner)]
    quarter, slim = width // 4, inner // 4

    def attend_back(origin):
        mine = row_block(origin, rows)
        window = strip_window(origin, rows, length)
        mixed_grad = dot_cols(branch[origin], own_out[...]).astype(BF)
        for head in range(heads):
            columns = slice(head * depth, (head + 1) * depth)
            key = qkv[:, inner + head * depth : inner + (head + 1) * depth]
            value = qkv[:, 2 * inner + head * depth : 2 * inner + (head + 1) * depth]
            grad = mixed_grad[:, columns]
            weight_low = weights[head, mine]
            weight = weight_low.astype(F32)
            scaled = weight * dot_cols(grad, value)
            score_grad = scaled - weight * jnp.sum(scaled, axis=1, keepdims=True)
            strip[head, :, window] += score_grad
            score_low = score_grad.astype(BF)
            dqkv[mine, columns] = dot(score_low, key).astype(BF)
            keys[:, columns] += dot_rows(score_low, qkv[mine, columns])
            values[:, columns] += dot_rows(weight_low, grad)
        terms = dot_rows(mixed_heads[mine], branch[origin])
        for tile in range(tiles):
            for index in range(4):
                base = 3 * quarter + tile * slim
                packed[index, base : base + slim] += terms[
                    index * slim : (index + 1) * slim, tile * LANES : (tile + 1) * LANES
                ]
        terms = dot_rows(normed[mine], dqkv[mine, :inner])
        for index in range(4):
            packed[index, :quarter] += terms[index * quarter : (index + 1) * quarter]

    mesh_sets = [r.gather_sems[7 * index : 7 * index + 7] for index in range(3)]
    down = MeshGather(spot, r.down_block, r.down_all, SHARES[0], mesh_sets[0])
    pair = MeshGather(spot, r.pair_block, r.pair_all, SHARES[1], mesh_sets[1])
    proj = MeshGather(spot, r.proj_block, r.proj_all, SHARES[2], mesh_sets[2])
    core, side = odd, spot.dp // 2
    own_dqkv = r.own_dqkv

    def branch_start():
        branches.begin(0)
        branch[spot.me] = own_branch[...]
        strip[...] = jnp.zeros_like(strip)
        keys[...] = jnp.zeros_like(keys)
        values[...] = jnp.zeros_like(values)
        branches.begin(1)
        packed[...] = jnp.zeros_like(packed)
        attend_back(spot.me)

    def finish_down():
        down_sum.total(r.down_block)
        down.begin()
        load("down_own", r.down_block, r.down_all.at[spot.dp, spot.me])

    def finish_pair():
        pair_sum.total(r.pair_block)
        pair.begin()
        load("pair_own", r.pair_block, r.pair_all.at[spot.dp, spot.me])

    def attend_pair(hop):
        def both_back(index, carry):
            attend_back(spot.at((1 - 2 * index) * (hop + 1)))
            return carry

        lax.fori_loop(0, 2, both_back, 0)

    def finish_heads():
        dqkv[:, inner : 2 * inner] = keys[...].astype(BF)
        dqkv[:, 2 * inner :] = values[...].astype(BF)

        def quarter_block(index, carry):
            block = dot_rows(normed[:, row_block(index, quarter)], dqkv[:, inner:])
            for part in range(2):
                packed[index, (part + 1) * quarter : (part + 2) * quarter] = block[
                    :, part * LANES : (part + 1) * LANES
                ]
            return carry

        lax.fori_loop(0, 4, quarter_block, 0)
        for index in range(2):
            r.near_out[index] = packed[2 * index + 1 - core].astype(BF)
        return push(r.near_out, r.near_in, r.proj_s.at[0], r.proj_r.at[0], spot.twin)

    def heads_over():
        near.wait_recv()
        r.far_out[...] = (
            packed[2 * (1 - side) + core] + r.near_in[1 - side].astype(F32)
        ).astype(BF)
        return push(r.far_out, r.far_in, r.proj_s.at[1], r.proj_r.at[1], spot.far, SPLITS[1])

    def finish_proj():
        far.wait_recv()
        r.proj_block[...] = (
            packed[2 * side + core] + r.near_in[side].astype(F32) + r.far_in[...].astype(F32)
        ).astype(BF)
        proj.begin()
        load("proj_own", r.proj_block, r.proj_all.at[spot.dp, spot.me])

    def trade():
        for device in spot.others:
            for part in range(3):
                push(
                    dqkv.at[row_block(device[1], rows), pl.ds(part * LANES, LANES)],
                    own_dqkv.at[part, :, own_columns],
                    r.trade_s,
                    r.trade_r,
                    device,
                )
        for part in range(3):
            own_dqkv[part, :, own_columns] = dqkv[
                row_block(spot.me, rows), part * LANES : (part + 1) * LANES
            ]

    def finish_table():
        for head in range(heads):
            middle_part = strip[head, :, low : low + near_span]
            before = jnp.sum(strip[head, :, :low], axis=0, keepdims=True)
            after = jnp.sum(strip[head, :, low + near_span :], axis=0, keepdims=True)
            levels = []
            for level in range(level_count):
                part = jnp.sum(jnp.where(bucket == level, middle_part, 0.0), axis=0, keepdims=True)
                line = part[:, :LANES]
                for tile in range(1, near_span // LANES):
                    line = line + part[:, tile * LANES : (tile + 1) * LANES]
                edge = before if level == 15 else after if level == 31 else None
                if edge is not None:
                    for tile in range(edge.shape[1] // LANES):
                        line = line + edge[:, tile * LANES : (tile + 1) * LANES]
                r.levels[level : level + 1] = line
            sums = lax.dot_general(
                jnp.ones((8, LANES), F32),
                r.levels[...],
                (((1,), (1,)), ((), ())),
                precision=lax.Precision.HIGHEST,
                preferred_element_type=F32,
            )
            small[pl.ds(2 * tiles + spot.me * heads + head, 1), : level_count] = sums[:1]

    def finish_input():
        for part in range(3):
            loads[3 + part].wait()
        wait_all(own_dqkv.at[:, :, pl.ds(0, width - LANES)], r.trade_r)
        normed_grad = dot_cols(own_dqkv[0], r.full_w[0])
        for part in range(1, 3):
            normed_grad = normed_grad + dot_cols(own_dqkv[part], r.full_w[part])
        inputs = hidden_ref[...].astype(F32)
        scale_one = scale_of(inputs)
        raised = gain_one * normed_grad
        r.hidden_grad[...] = (
            middle_grad_ref[...]
            + scale_one * raised
            - inputs * (scale_one * scale_one * scale_one)
            * jnp.mean(inputs * raised, axis=-1, keepdims=True)
        )
        gain_grad = jnp.sum(normed_grad * inputs * scale_one, axis=0, keepdims=True)
        for tile in range(tiles):
            small[tile : tile + 1] = gain_grad[:, tile * LANES : (tile + 1) * LANES]

    partners = [spot.twin, spot.far]
    bit = 1
    while bit < count:
        partners.append((spot.dp, exclusive(spot.me, bit)))
        bit *= 2
    small_out, small_in = r.small_out, r.small_in
    small_copies = []

    def small_send():
        index = len(small_copies)
        if index < len(partners):
            small_out[index] = small[...]
            small_copies.append(
                push(
                    small_out.at[index], small_in.at[index],
                    r.small_s.at[index], r.small_r.at[index], partners[index],
                )
            )

    def small_step():
        if len(small_copies) <= len(partners) and small_copies:
            index = len(small_copies) - 1
            small_copies[index].wait_recv()
            small[...] += small_in[index]
            small_send()

    def pass_round(gather, hop):
        gather.step(hop)
        gather.step_far(hop)

    outs.over()
    down_sum.step(1)
    pair_sum.step(0)
    down_sum.step(2)
    pair_sum.step(1)
    finish_down()
    pair_sum.step(2)
    branch_start()
    r.block_out[...] = (middle + outs.total()).astype(BF)
    finish_pair()
    branches.step(0)
    down.begin_far()
    attend_pair(0)
    branches.step(1)
    pair.begin_far()
    attend_pair(1)
    branches.step(2)
    pass_round(down, 0)
    attend_pair(2)
    branches.step(3)
    attend_back(spot.at(spot.half))
    near = finish_heads()
    pass_round(pair, 0)
    far = heads_over()
    pass_round(down, 1)
    trade()
    pass_round(pair, 1)
    finish_proj()
    pass_round(down, 2)
    finish_table()
    pass_round(pair, 2)
    proj.begin_far()
    pass_round(down, 3)
    down.step_far(4)
    pass_round(proj, 0)
    pass_round(pair, 3)
    finish_input()
    small_send()
    pair.step_far(4)
    pass_round(proj, 1)
    small_step()
    pass_round(proj, 2)
    small_step()
    pass_round(proj, 3)
    small_step()
    proj.step_far(4)
    small_step()
    small_step()
    r.small_sum[...] = small[...]
    for name in ("down_own", "pair_own", "proj_own"):
        loads[name].wait()
    wait_all(mixed_heads.at[pl.ds(0, length - rows)], r.mixed_s)
    wait_all(dqkv.at[pl.ds(0, length - rows)], r.trade_s)
    for copy in [near, far] + small_copies:
        copy.wait_send()
    for item in (cots, toks, grads, outs, down_sum, pair_sum, branches, down, pair, proj):
        item.finish()


SHARES = (80, 70, 57)
SPLITS = (1, 1)


def layer(arrays, count, heads, depth, ff):
    rows, width = arrays["hidden"].shape
    length = count * rows
    inner = heads * depth
    half = count // 2
    span = (ff + LANES - 1) // LANES * LANES
    pair_rows = 2 * ff // LANES * rows
    proj_rows = 3 * (width // 4) + inner // 4 * (width // LANES)
    small_rows = 2 * (width // LANES) + count * heads
    steps = 2 + (count - 1).bit_length()
    dma = pltpu.SemaphoreType.DMA
    specs = dict(
        hidden=VMEM,
        out_grad=VMEM,
        gain_one=VMEM,
        gain_two=VMEM,
        row_ids=VMEM,
        table=VMEM,
    )
    shape = jax.ShapeDtypeStruct
    results = dict(
        block_out=(shape((rows, width), BF), VMEM),
        hidden_grad=(shape((rows, width), F32), VMEM),
        small_sum=(shape((small_rows, LANES), F32), VMEM),
        down_all=(shape((4, count, ff, LANES), BF), ANY),
        pair_all=(shape((4, count, pair_rows, LANES), BF), ANY),
        proj_all=(shape((4, count, proj_rows, LANES), BF), ANY),
    )
    vm = pltpu.VMEM
    ring_buf = lambda n: vm((2, half, 2, n // 2, LANES), BF)
    pairs = {}
    for name in ("grad", "out"):
        pairs[name + "_kept"] = vm((2, rows, width), F32)
        pairs[name + "_outs"] = vm((2, rows, width), BF)
        pairs[name + "_ins"] = vm((2, rows, width), BF)
        pairs[name + "_far_out"] = vm((rows, width), BF)
        pairs[name + "_far_in"] = vm((rows, width), BF)
        pairs[name + "_s"] = dma((3,))
        pairs[name + "_r"] = dma((3,))
    for name in ("cot", "tok"):
        pairs[name] = vm((2, 2 * rows, width), BF)
        pairs[name + "_s"] = dma((3,))
        pairs[name + "_r"] = dma((3,))
    pairs["row"] = vm((count, rows, width), BF)
    for name in ("row", "branch"):
        pairs[name + "_s"] = dma(())
        pairs[name + "_r"] = dma((2, half, 2))
    for name, size in (("down", ff), ("pair", pair_rows)):
        pairs[name + "_terms"] = vm((count, size, LANES), BF)
        pairs[name + "_buf"] = ring_buf(size)
        pairs[name + "_block"] = vm((size, LANES), BF)
        pairs[name + "_s"] = dma(())
        pairs[name + "_r"] = dma((2, half, 2))
    scratch = dict(
        **pairs,
        score_strip=vm((heads, 2 * rows, 2 * length - rows), F32),
        normed=vm((length, width), BF),
        qkv=vm((length, 3 * inner), BF),
        weights=vm((heads, length, length), BF),
        mixed_heads=vm((length, inner), BF),
        mixed=vm((rows, width), BF),
        qkv_w=vm((width, 3 * inner), BF),
        full_w=vm((3, width, width), BF),
        out_w=vm((width, width), BF),
        gate_w=vm((width, span), BF),
        up_w=vm((width, span), BF),
        down_w=vm((span, width), BF),
        middle=vm((rows, width), F32),
        middle_grad=vm((rows, width), F32),
        act=vm((4 * rows, span), BF),
        gate_g=vm((4 * rows, span), BF),
        up_g=vm((4 * rows, span), BF),
        own_branch=vm((rows, width), BF),
        keys=vm((length, inner), F32),
        values=vm((length, inner), F32),
        dqkv=vm((length, 3 * inner), BF),
        own_dqkv=vm((3, rows, width), BF),
        packed=vm((4, proj_rows, LANES), F32),
        near_out=vm((2, proj_rows, LANES), BF),
        near_in=vm((2, proj_rows, LANES), BF),
        far_out=vm((proj_rows, LANES), BF),
        far_in=vm((proj_rows, LANES), BF),
        proj_block=vm((proj_rows, LANES), BF),
        levels=vm((arrays["table"].shape[1], LANES), F32),
        small=vm((small_rows, LANES), F32),
        small_out=vm((steps, small_rows, LANES), F32),
        small_in=vm((steps, small_rows, LANES), F32),
        load_sems=dma((16,)),
        mixed_s=dma(()),
        mixed_r=dma(()),
        trade_s=dma(()),
        trade_r=dma(()),
        proj_s=dma((2,)),
        proj_r=dma((2,)),
        small_s=dma((steps,)),
        small_r=dma((steps,)),
    )
    names = tuple(arrays) + tuple(results) + tuple(scratch)

    def body(*refs):
        plain = refs[: len(names)]
        layer_body(
            count, heads, depth, ff, names + ("gather_sems",), *plain, refs[len(names) :]
        )

    outs = pl.pallas_call(
        body,
        name="layer",
        out_shape=tuple(value[0] for value in results.values()),
        in_specs=[specs.get(name, ANY) for name in arrays],
        out_specs=tuple(value[1] for value in results.values()),
        scratch_shapes=list(scratch.values()) + mesh_sems(count) * 3,
        compiler_params=comm_params(0, 60 << 20),
    )(*arrays.values())
    return types.SimpleNamespace(**dict(zip(results, outs)))


def widen_body(
    part, down_ref, pair_ref, proj_ref, slim_ref, block_ref, hidden_ref, small_ref,
    down_out, gate_out, up_out, query_out, key_out, value_out, out_out,
    block_out, hidden_out, one_out, two_out, bias_out, small, sems,
):
    copies = [
        pltpu.make_async_copy(source, target, sems.at[index])
        for index, (source, target) in enumerate(
            ((small_ref, small), (block_ref, block_out), (hidden_ref, hidden_out))
        )
    ]
    step = pl.program_id(0)

    @pl.when(step == 0)
    def _():
        for copy in copies:
            copy.start()

    full, half = part // LANES, LANES // 2
    for source in range(down_ref.shape[1]):
        columns = slice(source * LANES, (source + 1) * LANES)
        down_out[:, columns] = down_ref[0, source].astype(F32)
        for index, o_ref in enumerate((query_out, key_out, value_out)):
            o_ref[:, columns] = proj_ref[0, source, index].astype(F32)
    dps = pair_ref.shape[0]
    slim = out_out.shape[0] // dps
    for dp in range(dps):
        base = dp * part
        shift = half if dp % 2 else 0
        for which, o_ref in enumerate((gate_out, up_out)):
            for tile in range(full):
                column = base + shift + tile * LANES
                o_ref[:, column : column + LANES] = pair_ref[dp, 0, which * full + tile].astype(F32)
        edge = pair_ref[dp, 0, 2 * full].astype(F32)
        column = base if dp % 2 else base + full * LANES
        gate_half = slice(half, LANES) if dp % 2 else slice(0, half)
        up_half = slice(0, half) if dp % 2 else slice(half, LANES)
        gate_out[:, column : column + half] = edge[:, gate_half]
        up_out[:, column : column + half] = edge[:, up_half]
        for tile in range(out_out.shape[1] // LANES):
            out_out[dp * slim : (dp + 1) * slim, tile * LANES : (tile + 1) * LANES] = slim_ref[
                dp, 0, 0, tile * slim : (tile + 1) * slim
            ].astype(F32)

    @pl.when(step == pl.num_programs(0) - 1)
    def _():
        for copy in copies:
            copy.wait()
        tiles = one_out.shape[0]
        one_out[...] = small[:tiles]
        two_out[...] = small[tiles : 2 * tiles]
        bias_out[...] = small[2 * tiles :, : bias_out.shape[1]]


def widen(out, levels, ff):
    rows, width = out.hidden_grad.shape
    dps, count = out.down_all.shape[:2]
    quarter = width // dps
    small_rows = out.small_sum.shape[0]
    tiles = width // LANES
    heads = small_rows - 2 * tiles
    pieces = count // dps
    pair = out.pair_all.reshape(dps, count, -1, rows, LANES)
    proj = out.proj_all.reshape(dps, count, 4, quarter, LANES)
    shape = lambda *dims: jax.ShapeDtypeStruct(dims, F32)
    spec = pl.BlockSpec
    whole = lambda *dims: spec(dims, lambda i: (0,) * len(dims))
    row = lambda size, span: spec((size, span), lambda i: (i, 0))
    return pl.pallas_call(
        functools.partial(widen_body, ff),
        name="widen",
        grid=(count,),
        out_shape=(
            shape(dps * ff, width),
            shape(width, dps * ff),
            shape(width, dps * ff),
            *[shape(width, width)] * 4,
            jax.ShapeDtypeStruct((rows, width), BF),
            shape(rows, width),
            shape(tiles, LANES),
            shape(tiles, LANES),
            shape(heads, levels),
        ),
        in_specs=[
            spec((1, count, ff // pieces, LANES), lambda i: (i // pieces, 0, i % pieces, 0)),
            spec((dps, 1, pair.shape[2], rows, LANES), lambda i: (0, i, 0, 0, 0)),
            spec((1, count, 3, quarter // pieces, LANES), lambda i: (i // pieces, 0, 0, i % pieces, 0)),
            spec((dps, 1, 1, quarter, LANES), lambda i: (0, i, 3, 0, 0)),
            ANY,
            ANY,
            ANY,
        ],
        out_specs=(
            row(ff // pieces, width),
            row(rows, dps * ff),
            row(rows, dps * ff),
            *[row(quarter // pieces, width)] * 3,
            row(width // count, width),
            ANY,
            ANY,
            whole(tiles, LANES),
            whole(tiles, LANES),
            whole(heads, levels),
        ),
        scratch_shapes=[pltpu.VMEM((small_rows, LANES), F32), pltpu.SemaphoreType.DMA((3,))],
        compiler_params=pltpu.CompilerParams(vmem_limit_bytes=56 << 20),
    )(out.down_all, pair, proj, proj, out.block_out, out.hidden_grad, out.small_sum)


def split_shards(
    hidden,
    group_ids,
    norm1_gain,
    query_weight,
    key_weight,
    value_weight,
    out_weight,
    relative_bias,
    norm2_gain,
    gate_weight,
    up_weight,
    down_projection_weight,
    out_grad,
    *,
    count,
):
    width = hidden.shape[2]
    levels, head_count = relative_bias.shape
    depth = query_weight.shape[1] // head_count
    heads = head_count // count
    ff = gate_weight.shape[1] // 4
    arrays = dict(
        hidden=hidden[0],
        out_grad=out_grad[0],
        gain_one=norm1_gain,
        gain_two=norm2_gain,
        row_ids=group_ids,
        table=relative_bias.T,
        query_weight=query_weight,
        key_weight=key_weight,
        value_weight=value_weight,
        out_weight=out_weight,
        gate_weight=gate_weight,
        up_weight=up_weight,
        down_weight=down_projection_weight,
    )
    out = layer(arrays, count, heads, depth, ff)
    down, gate, up, query, key, value, projected, block, grad, one, two, bias = widen(
        out, levels, ff
    )
    return (
        block[None], grad[None], one.reshape(-1), query, key, value, projected, bias.T,
        two.reshape(-1), gate, up, down,
    )


def rms_norm(vector, norm_gain):
    return (
        vector * lax.rsqrt(jnp.mean(vector * vector, axis=-1, keepdims=True) + EPSILON) * norm_gain
    )


def activate(gate_proj, up_proj):
    return jax.nn.gelu(gate_proj, approximate=True) * up_proj


def scores_of(
    query_part, key_part, query_places, key_places, query_groups, key_groups, bias_lookup
):
    bucket = bucket_of(key_places[None, :] - query_places[:, None])
    levels = jnp.arange(bias_lookup.shape[0], dtype=jnp.int32)
    one_hot_mask = (bucket[None] == levels[:, None, None]).astype(jnp.bfloat16)
    bias_patch_block = jnp.einsum(
        "ctf,cx->xtf", one_hot_mask, bias_lookup, preferred_element_type=jnp.float32
    )
    raw_scores = (
        jnp.einsum("qhd,khd->hqk", query_part, key_part, preferred_element_type=jnp.float32)
        + bias_patch_block
    )
    same_group = query_groups[:, None] == key_groups[None, :]
    return (one_hot_mask, jnp.where(same_group[None], raw_scores, MASKED))


def shards(
    hidden,
    group_ids,
    norm1_gain,
    query_weight,
    key_weight,
    value_weight,
    out_weight,
    relative_bias,
    norm2_gain,
    gate_weight,
    up_weight,
    down_projection_weight,
    out_grad,
):
    tok_rows = hidden.shape[1]
    head_count = relative_bias.shape[1]
    inner_width = query_weight.shape[1]
    head_depth = inner_width // head_count
    row_length = group_ids.shape[1]
    row_start = lax.axis_index("seq") * tok_rows
    key_block = min(1024, row_length)
    block_count = row_length // key_block
    row_groups = group_ids[0]
    own_groups = lax.dynamic_slice_in_dim(row_groups, row_start, tok_rows)
    own_places = row_start + jnp.arange(tok_rows, dtype=jnp.int32)
    all_places = jnp.arange(row_length, dtype=jnp.int32)

    def key_blocks(key_rows, value_rows):
        return (
            key_rows.reshape(block_count, key_block, head_count, head_depth),
            value_rows.reshape(block_count, key_block, head_count, head_depth),
            row_groups.reshape(block_count, key_block),
            all_places.reshape(block_count, key_block),
        )

    inputs = hidden[0].astype(jnp.float32)
    normed, norm_pull = jax.vjp(rms_norm, inputs, norm1_gain.astype(jnp.float32))
    normed_low = normed.astype(jnp.bfloat16)
    query_low = jnp.dot(normed_low, query_weight, preferred_element_type=jnp.float32).astype(
        jnp.bfloat16
    )
    key_low = jnp.dot(normed_low, key_weight, preferred_element_type=jnp.float32).astype(
        jnp.bfloat16
    )
    value_low = jnp.dot(normed_low, value_weight, preferred_element_type=jnp.float32).astype(
        jnp.bfloat16
    )
    key_all, value_all = (
        lax.all_gather(key_low, "seq", axis=0, tiled=True),
        lax.all_gather(value_low, "seq", axis=0, tiled=True),
    )
    query_heads = query_low.reshape(tok_rows, head_count, head_depth)

    def gather_stats(carry_state, scanned):
        running_max, running_sum = carry_state
        key_part, value_part, key_groups, key_places = scanned
        one_hot_mask, scores = scores_of(
            query_heads, key_part, own_places, key_places, own_groups, key_groups, relative_bias
        )
        new_max = jnp.maximum(running_max, jnp.max(scores, axis=-1))
        running_sum = running_sum * jnp.exp(running_max - new_max) + jnp.sum(
            jnp.exp(scores - new_max[..., None]), axis=-1
        )
        return ((new_max, running_sum), None)

    stats_init = (
        jnp.full((head_count, tok_rows), MASKED, jnp.float32),
        jnp.zeros((head_count, tok_rows), jnp.float32),
    )
    (running_max, running_sum), _ = lax.scan(
        gather_stats, stats_init, key_blocks(key_all, value_all)
    )
    log_total = running_max + jnp.log(running_sum)

    def gather_values(summed, scanned):
        key_part, value_part, key_groups, key_places = scanned
        one_hot_mask, scores = scores_of(
            query_heads, key_part, own_places, key_places, own_groups, key_groups, relative_bias
        )
        attention_low = jnp.exp(scores - log_total[..., None]).astype(jnp.bfloat16)
        return (
            summed
            + jnp.einsum(
                "hqk,khd->qhd", attention_low, value_part, preferred_element_type=jnp.float32
            ),
            None,
        )

    mixed, _ = lax.scan(
        gather_values,
        jnp.zeros((tok_rows, head_count, head_depth), jnp.float32),
        key_blocks(key_all, value_all),
    )
    mixed_low = mixed.reshape(tok_rows, inner_width).astype(jnp.bfloat16)
    middle = inputs + jnp.dot(mixed_low, out_weight, preferred_element_type=jnp.float32)
    normed_two, norm_two_pull = jax.vjp(rms_norm, middle, norm2_gain.astype(jnp.float32))
    normed_two_low = normed_two.astype(jnp.bfloat16)
    gate_proj = jnp.dot(normed_two_low, gate_weight, preferred_element_type=jnp.float32)
    up_proj = jnp.dot(normed_two_low, up_weight, preferred_element_type=jnp.float32)
    activated, act_pull = jax.vjp(activate, gate_proj, up_proj)
    activated_low = activated.astype(jnp.bfloat16)
    result = middle + jnp.dot(
        activated_low, down_projection_weight, preferred_element_type=jnp.float32
    )
    block_out = result.astype(jnp.bfloat16)[None]
    cotangent_low = out_grad[0]
    grad_down = dot_rows(activated_low, cotangent_low)
    act_grad = dot_cols(cotangent_low, down_projection_weight)
    gate_grad, up_grad = act_pull(act_grad)
    gate_grad_low = gate_grad.astype(jnp.bfloat16)
    up_grad_low = up_grad.astype(jnp.bfloat16)
    grad_gate = dot_rows(normed_two_low, gate_grad_low)
    grad_up = dot_rows(normed_two_low, up_grad_low)
    normed_two_grad = dot_cols(gate_grad_low, gate_weight) + dot_cols(up_grad_low, up_weight)
    middle_norm_grad, grad_gain_two = norm_two_pull(normed_two_grad)
    middle_grad = cotangent_low.astype(jnp.float32) + middle_norm_grad
    branch_grad_low = middle_grad.astype(jnp.bfloat16)
    grad_out = dot_rows(mixed_low, branch_grad_low)
    mixed_grad_low = (
        dot_cols(branch_grad_low, out_weight)
        .astype(jnp.bfloat16)
        .reshape(tok_rows, head_count, head_depth)
    )
    row_dots = jnp.einsum("qhd,qhd->hq", mixed_grad_low.astype(jnp.float32), mixed)
    key_back, value_back = (
        lax.all_gather(key_low, "seq", axis=0, tiled=True),
        lax.all_gather(value_low, "seq", axis=0, tiled=True),
    )
    grads_init = (
        jnp.zeros((tok_rows, head_count, head_depth), jnp.float32),
        jnp.zeros(relative_bias.shape, jnp.float32),
    )

    def backward_block(carry_state, scanned):
        query_grad, table_grad = carry_state
        key_part, value_part, key_groups, key_places = scanned
        one_hot_mask, scores = scores_of(
            query_heads, key_part, own_places, key_places, own_groups, key_groups, relative_bias
        )
        attention = jnp.exp(scores - log_total[..., None])
        grad_weights = jnp.einsum(
            "qhd,khd->hqk", mixed_grad_low, value_part, preferred_element_type=jnp.float32
        )
        score_gradients = (attention * (grad_weights - row_dots[..., None])).astype(jnp.bfloat16)
        query_grad = query_grad + jnp.einsum(
            "hqk,khd->qhd", score_gradients, key_part, preferred_element_type=jnp.float32
        )
        table_grad = table_grad + jnp.einsum(
            "oei,cei->oc", one_hot_mask, score_gradients, preferred_element_type=jnp.float32
        )
        key_grad = jnp.einsum(
            "hqk,qhd->khd", score_gradients, query_heads, preferred_element_type=jnp.float32
        )
        value_grad = jnp.einsum(
            "hqk,qhd->khd",
            attention.astype(jnp.bfloat16),
            mixed_grad_low,
            preferred_element_type=jnp.float32,
        )
        return ((query_grad, table_grad), (key_grad, value_grad))

    (query_grad, table_grad), (key_terms, value_terms) = lax.scan(
        backward_block, grads_init, key_blocks(key_back, value_back)
    )
    key_grad, value_grad = (
        lax.psum_scatter(
            key_terms.reshape(row_length, inner_width), "seq", scatter_dimension=0, tiled=True
        ),
        lax.psum_scatter(
            value_terms.reshape(row_length, inner_width), "seq", scatter_dimension=0, tiled=True
        ),
    )
    query_grad_low = query_grad.reshape(tok_rows, inner_width).astype(jnp.bfloat16)
    key_grad_low = key_grad.astype(jnp.bfloat16)
    value_grad_low = value_grad.astype(jnp.bfloat16)
    grad_query = dot_rows(normed_low, query_grad_low)
    grad_key = dot_rows(normed_low, key_grad_low)
    grad_value = dot_rows(normed_low, value_grad_low)
    normed_grad = (
        dot_cols(query_grad_low, query_weight)
        + dot_cols(key_grad_low, key_weight)
        + dot_cols(value_grad_low, value_weight)
    )
    input_norm_grad, grad_gain_one = norm_pull(normed_grad)
    hidden_grad = (middle_grad + input_norm_grad)[None]
    local_grads = (
        grad_gain_one,
        grad_query,
        grad_key,
        grad_value,
        grad_out,
        table_grad.reshape(-1),
        grad_gain_two,
        grad_gate,
        grad_up,
        grad_down,
    )
    shared = (
        lax.psum_scatter(local_grads[0], "seq", scatter_dimension=0, tiled=True),
        lax.psum_scatter(local_grads[1], "seq", scatter_dimension=0, tiled=True),
        lax.psum_scatter(local_grads[2], "seq", scatter_dimension=0, tiled=True),
        lax.psum_scatter(local_grads[3], "seq", scatter_dimension=0, tiled=True),
        lax.psum_scatter(local_grads[4], "seq", scatter_dimension=0, tiled=True),
        lax.psum_scatter(local_grads[5], "seq", scatter_dimension=0, tiled=True),
        lax.psum_scatter(local_grads[6], "seq", scatter_dimension=0, tiled=True),
        lax.psum_scatter(local_grads[7], "seq", scatter_dimension=0, tiled=True),
        lax.psum_scatter(local_grads[8], "seq", scatter_dimension=0, tiled=True),
        lax.psum_scatter(local_grads[9], "seq", scatter_dimension=0, tiled=True),
    )
    shared = (
        lax.psum(shared[0].astype(jnp.bfloat16), "dp").astype(jnp.float32),
        lax.psum(shared[1].astype(jnp.bfloat16), "dp").astype(jnp.float32),
        lax.psum(shared[2].astype(jnp.bfloat16), "dp").astype(jnp.float32),
        lax.psum(shared[3].astype(jnp.bfloat16), "dp").astype(jnp.float32),
        lax.psum(shared[4].astype(jnp.bfloat16), "dp").astype(jnp.float32),
        lax.psum(shared[5].astype(jnp.bfloat16), "dp").astype(jnp.float32),
        lax.psum(shared[6].astype(jnp.bfloat16), "dp").astype(jnp.float32),
        lax.psum(shared[7].astype(jnp.bfloat16), "dp").astype(jnp.float32),
        lax.psum(shared[8].astype(jnp.bfloat16), "dp").astype(jnp.float32),
        lax.psum(shared[9].astype(jnp.bfloat16), "dp").astype(jnp.float32),
    )
    summed = (
        lax.all_gather(shared[0].astype(jnp.bfloat16), "seq", axis=0, tiled=True).astype(
            jnp.float32
        ),
        lax.all_gather(shared[1].astype(jnp.bfloat16), "seq", axis=0, tiled=True).astype(
            jnp.float32
        ),
        lax.all_gather(shared[2].astype(jnp.bfloat16), "seq", axis=0, tiled=True).astype(
            jnp.float32
        ),
        lax.all_gather(shared[3].astype(jnp.bfloat16), "seq", axis=0, tiled=True).astype(
            jnp.float32
        ),
        lax.all_gather(shared[4].astype(jnp.bfloat16), "seq", axis=0, tiled=True).astype(
            jnp.float32
        ),
        lax.all_gather(shared[5].astype(jnp.bfloat16), "seq", axis=0, tiled=True).astype(
            jnp.float32
        ),
        lax.all_gather(shared[6].astype(jnp.bfloat16), "seq", axis=0, tiled=True).astype(
            jnp.float32
        ),
        lax.all_gather(shared[7].astype(jnp.bfloat16), "seq", axis=0, tiled=True).astype(
            jnp.float32
        ),
        lax.all_gather(shared[8].astype(jnp.bfloat16), "seq", axis=0, tiled=True).astype(
            jnp.float32
        ),
        lax.all_gather(shared[9].astype(jnp.bfloat16), "seq", axis=0, tiled=True).astype(
            jnp.float32
        ),
    )
    return (
        block_out,
        hidden_grad,
        summed[0],
        summed[1],
        summed[2],
        summed[3],
        summed[4],
        summed[5].reshape(relative_bias.shape),
        summed[6],
        summed[7],
        summed[8],
        summed[9],
    )


def solution(mesh):
    placed = (P("dp", "seq", None), P("dp", None)) + (P(),) * 10 + (P("dp", "seq", None),)
    out_specs = (P("dp", "seq", None),) * 2 + (P(),) * 10
    count = mesh.shape["seq"]

    def run(*args):
        hidden, query_weight, relative_bias = args[0], args[3], args[7]
        head_count = relative_bias.shape[1]
        inner = query_weight.shape[1] // count
        fits = (
            mesh.shape["dp"] == 4
            and count % 2 == 0
            and head_count % count == 0
            and inner == LANES
            and hidden.shape[2] == count * LANES
            and hidden.shape[1] == count * LANES
            and args[9].shape[1] % (4 * LANES) == 2 * LANES
        )
        body = functools.partial(split_shards, count=count) if fits else shards
        return jax.shard_map(
            body, mesh=mesh, in_specs=placed, out_specs=out_specs, check_vma=False
        )(*args)

    return run
```

```python
import functools
import types

import jax
import jax.numpy as jnp
from jax import lax
from jax.experimental import pallas as pl
from jax.experimental.pallas import tpu as pltpu
from jax.sharding import PartitionSpec as P

EPSILON = 1e-06
MASKED = -1e30
THRESHOLDS = (12, 16, 23, 32, 46, 64, 91)
MESH = pl.DeviceIdType.MESH
BF = jnp.bfloat16
F32 = jnp.float32
LANES = 128
ANY = pl.BlockSpec(memory_space=pl.ANY)
VMEM = pl.BlockSpec(memory_space=pltpu.VMEM)


def bucket_of(relative):
    distance = jnp.abs(relative)
    bucket_level = jnp.full(relative.shape, 8, jnp.int32)
    for boundary in THRESHOLDS:
        bucket_level = bucket_level + (distance >= boundary).astype(jnp.int32)
    near_bucket = jnp.where(distance < 8, distance, bucket_level)
    return near_bucket + 16 * (relative > 0).astype(jnp.int32)


def dot(left_mat, right_mat):
    return jnp.dot(left_mat, right_mat, preferred_element_type=F32)


def dot_rows(left_mat, right_mat):
    return lax.dot_general(
        left_mat, right_mat, (((0,), (0,)), ((), ())), preferred_element_type=F32
    )


def dot_cols(left_mat, right_mat):
    return lax.dot_general(
        left_mat, right_mat, (((1,), (1,)), ((), ())), preferred_element_type=F32
    )


def ring_place(index, count):
    odd = index % 2
    return (1 - odd) * (index // 2) + odd * ((2 * count - 1 - index) // 2)


def ring_index(place, count):
    late = place // (count // 2)
    return (1 - late) * 2 * place + late * (2 * count - 1 - 2 * place)


def greet(targets):
    barrier = pltpu.get_barrier_semaphore()
    for target in targets:
        pl.semaphore_signal(barrier, inc=1, device_id=target, device_id_type=MESH)
    pl.semaphore_wait(barrier, len(targets))


def comm_params(collective_id, vmem=None):
    return pltpu.CompilerParams(
        collective_id=collective_id, has_side_effects=True, vmem_limit_bytes=vmem
    )


class Spot:
    def __init__(self, count):
        self.count = count
        self.half = count // 2
        self.me = lax.axis_index("seq")
        self.dp = lax.axis_index("dp")
        self.place = ring_place(self.me, count)
        self.nexts = tuple((self.dp, self.at(step)) for step in (1, -1))
        self.far_dp = (self.dp + 2) % 4
        self.twin_dp = self.dp + 1 - 2 * (self.dp % 2)
        self.far = (self.far_dp, self.me)
        self.twin = (self.twin_dp, self.me)
        self.others = tuple((self.dp, (self.me + step) % count) for step in range(1, count))

    def at(self, step):
        return ring_index((self.place + (step + self.count) % self.count) % self.count, self.count)

    def back(self, way, hop):
        return self.at(-hop if way == 0 else hop)


def push(source, target, send_sem, recv_sem, device, split=1):
    def copy_of(source, target):
        return pltpu.make_async_remote_copy(
            src_ref=source,
            dst_ref=target,
            send_sem=send_sem,
            recv_sem=recv_sem,
            device_id=device,
            device_id_type=MESH,
        )

    whole = copy_of(source, target)
    if split == 1:
        whole.start()
        return whole
    rows = source.shape[0] // split
    for index in range(split):
        window = pl.ds(index * rows, rows)
        copy_of(source.at[window], target.at[window]).start()
    return whole


def wait_all(like, sem):
    pltpu.make_async_copy(like, like, sem).wait()


class RingGather:
    def __init__(self, spot, own, blocks, send_sem, recv_sems, split=1):
        self.spot, self.own, self.blocks, self.split = spot, own, blocks, split
        self.send_sem, self.recv_sems = send_sem, recv_sems
        self.rows = blocks.shape[1] // 2
        self.copies = {}

    def into(self, origin, piece):
        return self.blocks.at[origin, pl.ds(piece * self.rows, self.rows)]

    def pieces(self, way, hop):
        return (0, 1) if hop < self.spot.half - 1 else (way,)

    def forward(self, hop, way, piece):
        spot = self.spot
        if hop >= spot.half or piece not in self.pieces(way, hop):
            return
        origin = spot.back(way, hop)
        target = self.into(origin, piece)
        self.copies[hop, way, piece] = push(
            self.own.at[pl.ds(piece * self.rows, self.rows)] if hop == 0 else target,
            target,
            self.send_sem,
            self.recv_sems.at[way, hop, piece],
            spot.nexts[way],
            self.split,
        )

    def begin(self, piece):
        for way in range(2):
            self.forward(0, way, piece)

    def step(self, hop):
        for piece in range(2):
            for way in range(2):
                if (hop, way, piece) in self.copies:
                    self.copies[hop, way, piece].wait_recv()
                    self.forward(hop + 1, way, piece)

    def finish(self):
        wait_all(self.blocks.at[pl.ds(0, self.spot.count - 1)], self.send_sem)


class RingSum:
    def __init__(self, spot, terms, buf, send_sem, recv_sems):
        self.spot, self.terms, self.buf = spot, terms, buf
        self.send_sem, self.recv_sems = send_sem, recv_sems
        self.rows = terms.shape[1] // 2
        self.copies = {}

    def term(self, block, piece):
        return self.terms.at[block, pl.ds(piece * self.rows, self.rows)]

    def send(self, hop, way, piece, source):
        self.copies[hop, way, piece] = push(
            source,
            self.buf.at[way, hop, piece],
            self.send_sem,
            self.recv_sems.at[way, hop, piece],
            self.spot.nexts[way],
        )

    def block(self, way, hop):
        step = self.spot.half - hop
        return self.spot.at(step if way == 0 else -step)

    def begin(self):
        for way in range(2):
            self.send(0, way, way, self.term(self.block(way, 0), way))
        for way in range(2):
            self.send(1, way, 1 - way, self.term(self.block(way, 1), 1 - way))

    def step(self, hop):
        for piece in range(2):
            for way in range(2):
                if (hop, way, piece) not in self.copies or hop + 1 >= self.spot.half:
                    continue
                self.copies[hop, way, piece].wait_recv()
                term = self.term(self.block(way, hop + 1), piece)
                self.buf[way, hop, piece] = (
                    self.buf[way, hop, piece].astype(F32) + term[...].astype(F32)
                ).astype(BF)
                self.send(hop + 1, way, piece, self.buf.at[way, hop, piece])

    def total(self, out):
        last = self.spot.half - 1
        for piece in range(2):
            value = self.term(self.spot.me, piece)[...].astype(F32)
            for way in range(2):
                self.copies[last, way, piece].wait_recv()
                value = value + self.buf[way, last, piece].astype(F32)
            out[pl.ds(piece * self.rows, self.rows)] = value.astype(BF)

    def finish(self):
        wait_all(self.terms.at[pl.ds(0, self.spot.count - 1)], self.send_sem)


class PairGather:
    def __init__(self, spot, own_ref, buf, send_sems, recv_sems):
        self.spot, self.buf = spot, buf
        self.send_sems, self.recv_sems = send_sems, recv_sems
        rows = own_ref.shape[0]
        self.low, self.high = pl.ds(0, rows), pl.ds(rows, rows)
        self.far = self.push(1, own_ref, buf.at[1, self.low], spot.far)
        self.near = self.push(0, own_ref, buf.at[0, self.high], spot.twin)

    def push(self, index, source, target, device):
        return push(source, target, self.send_sems.at[index], self.recv_sems.at[index], device)

    def relay(self):
        self.far.wait_recv()
        self.cross = self.push(
            2, self.buf.at[1, self.low], self.buf.at[1, self.high], self.spot.twin
        )

    def finish(self):
        for copy in (self.near, self.far, self.cross):
            copy.wait_send()


class PairSum:
    def __init__(self, spot, kept, outs, ins, far_out, far_in, send_sems, recv_sems):
        self.spot, self.kept, self.outs, self.ins = spot, kept, outs, ins
        self.far_out, self.far_in = far_out, far_in
        self.send_sems, self.recv_sems = send_sems, recv_sems
        self.copies = []

    def near(self, half):
        self.copies.append(
            push(
                self.outs.at[half], self.ins.at[half],
                self.send_sems.at[half], self.recv_sems.at[half], self.spot.twin,
            )
        )

    def over(self):
        self.copies[1].wait_recv()
        self.far_out[...] = (self.kept[1] + self.ins[1].astype(F32)).astype(BF)
        self.copies.append(
            push(
                self.far_out, self.far_in, self.send_sems.at[2], self.recv_sems.at[2], self.spot.far
            )
        )

    def total(self):
        self.copies[0].wait_recv()
        self.copies[2].wait_recv()
        return self.kept[0] + self.ins[0].astype(F32) + self.far_in[...].astype(F32)

    def finish(self):
        for copy in self.copies:
            copy.wait_send()


class MeshGather:
    def __init__(self, spot, x_ref, o_ref, share, sems):
        self.spot, self.x_ref, self.o_ref = spot, x_ref, o_ref
        self.ring_s, self.ring_r, self.x_s, self.far_r, self.own_r, self.core_s, self.core_r = sems
        rows = x_ref.shape[0]
        first = rows * share // 100 // 32 * 32
        cuts = (0, first // 2, first, first + (rows - first) // 2 // 16 * 16, rows)
        self.parts = (pl.ds(0, first), pl.ds(first, rows - first))
        self.windows = [
            [pl.ds(cuts[2 * part + piece], cuts[2 * part + piece + 1] - cuts[2 * part + piece]) for piece in range(2)]
            for part in range(2)
        ]
        self.ring, self.x = {}, {}

    def into(self, dp, origin, part, piece):
        return self.o_ref.at[dp, origin, self.windows[part][piece]]

    def pieces(self, way, hop):
        return (0, 1) if hop < self.spot.half - 1 else (way,)

    def to_core(self, source, target):
        push(source, target, self.core_s, self.core_r, self.spot.twin)

    def pass_on(self, part, lane, hop, way, piece, source):
        spot = self.spot
        dp = spot.far_dp if lane else spot.dp
        origin = spot.me if way is None else spot.back(way, hop)
        target = self.into(dp, origin, part, piece)
        source = target if source is None else source
        slot = 0 if way is None else 2 * hop - 1 + way
        for onward in (0, 1) if way is None else (way,):
            if hop < spot.half and piece in self.pieces(onward, hop):
                self.ring[part, lane, hop, onward, piece] = push(
                    source, target,
                    self.ring_s.at[part + lane],
                    self.ring_r.at[2 * (part + lane) + onward, hop, piece],
                    spot.nexts[onward],
                )
        if part == 0:
            self.x[part, slot, piece] = push(
                source, target, self.x_s.at[0], self.far_r.at[slot, piece], spot.far
            )
        self.to_core(source, target)

    def begin(self):
        spot = self.spot
        for piece in range(2):
            self.x[1, 0, piece] = push(
                self.x_ref.at[self.windows[1][piece]],
                self.into(spot.dp, spot.me, 1, piece),
                self.x_s.at[1], self.own_r.at[piece], spot.far,
            )
        for part in range(2):
            for piece in range(2):
                self.pass_on(part, 0, 0, None, piece, self.x_ref.at[self.windows[part][piece]])

    def begin_far(self):
        for piece in range(2):
            self.x[1, 0, piece].wait_recv()
            self.pass_on(1, 1, 0, None, piece, None)

    def step(self, hop):
        for piece in range(2):
            for part, lane in ((0, 0), (1, 0), (1, 1)):
                for way in range(2):
                    key = (part, lane, hop, way, piece)
                    if key in self.ring:
                        self.ring[key].wait_recv()
                        self.pass_on(part, lane, hop + 1, way, piece, None)

    def step_far(self, hop):
        spot = self.spot
        for piece in range(2):
            for way in (None,) if hop == 0 else range(2):
                slot = 0 if way is None else 2 * hop - 1 + way
                if (0, slot, piece) in self.x:
                    self.x[0, slot, piece].wait_recv()
                    origin = spot.me if way is None else spot.back(way, hop)
                    target = self.into(spot.far_dp, origin, 0, piece)
                    self.to_core(target, target)

    def finish(self):
        o_ref, count = self.o_ref, self.spot.count
        wait_all(o_ref.at[pl.ds(0, 2)], self.core_r)
        wait_all(o_ref.at[pl.ds(0, 2)], self.core_s)
        for index in range(3):
            wait_all(o_ref.at[0, pl.ds(0, count - 1), self.parts[min(index, 1)]], self.ring_s.at[index])
        wait_all(o_ref.at[0, :, self.parts[0]], self.x_s.at[0])
        wait_all(self.x_ref.at[self.parts[1]], self.x_s.at[1])


def mesh_sems(count):
    half = count // 2
    dma = pltpu.SemaphoreType.DMA
    return [
        dma((3,)), dma((6, half, 2)), dma((2,)), dma((2 * half + 1, 2)), dma((2,)), dma(()), dma(())
    ]


def near_buckets(rows):
    shape = (rows, rows + 2 * LANES)
    column = lax.broadcasted_iota(jnp.int32, shape, 1) - LANES
    return bucket_of(column - lax.broadcasted_iota(jnp.int32, shape, 0))


def strip_window(step, rows, length):
    return pl.ds(pl.multiple_of(length - rows - step * rows, LANES), length)


def scale_of(value):
    return lax.rsqrt(jnp.mean(value * value, axis=-1, keepdims=True) + EPSILON)


def row_block(origin, rows):
    return pl.ds(pl.multiple_of(origin * rows, rows), rows)


def exclusive(index, bit):
    return index + bit - 2 * bit * ((index // bit) % 2)


def layer_body(count, heads, depth, ff, names, *refs):
    r = types.SimpleNamespace(**dict(zip(names, refs)))
    spot = Spot(count)
    hidden_ref, grad_ref = r.hidden, r.out_grad
    rows, width = hidden_ref.shape
    length = count * rows
    inner = heads * depth
    span = r.gate_w.shape[1]
    odd = spot.dp % 2
    ff_start = pl.multiple_of(spot.dp * ff - odd * (span - ff), span - ff)
    own_columns = pl.ds(pl.multiple_of(spot.me * LANES, LANES), LANES)
    greet(spot.nexts + (spot.far, spot.twin))

    loads = {}

    def load(name, source, target):
        copy = pltpu.make_async_copy(source, target, r.load_sems.at[len(loads)])
        copy.start()
        loads[name] = copy

    ring = RingGather(
        spot,
        hidden_ref,
        r.row,
        r.row_s,
        r.row_r,
    )
    ring.begin(0)
    sources = (r.query_weight, r.key_weight, r.value_weight)
    for part, source in enumerate(sources):
        load(
            part,
            source.at[:, pl.ds(pl.multiple_of(spot.me * inner, inner), inner)],
            r.qkv_w.at[:, pl.ds(part * inner, inner)],
        )
    load("out", r.out_weight, r.out_w)
    ff_columns = pl.ds(pl.multiple_of(ff_start, LANES), span)
    load("gate", r.gate_weight.at[:, ff_columns], r.gate_w)
    load("up", r.up_weight.at[:, ff_columns], r.up_w)
    load("down", r.down_weight.at[pl.ds(ff_start, span)], r.down_w)
    for part, source in enumerate(sources):
        load(3 + part, source, r.full_w.at[part])

    qkv, normed, weights = r.qkv, r.normed, r.weights
    both_rows = 2 * rows
    low = length - rows - LANES
    bucket = near_buckets(rows)
    near_span = bucket.shape[1]
    score_strip = r.score_strip
    strip = score_strip.at[:, pl.ds(0, rows)]
    score_low = length - both_rows - LANES
    score_bucket = near_buckets(both_rows)
    score_span = score_bucket.shape[1]
    head_count, level_count = r.table.shape
    chosen = lax.broadcasted_iota(jnp.int32, (8, head_count), 1) == (
        spot.me * heads + lax.broadcasted_iota(jnp.int32, (8, head_count), 0)
    )
    table = dot(chosen.astype(BF), r.table[...])
    for head in range(heads):
        entry = lambda level: table[head : head + 1, level : level + 1]
        value = jnp.zeros(score_bucket.shape, F32)
        for level in range(level_count):
            value = jnp.where(score_bucket == level, entry(level), value)
        after = score_strip.shape[2] - score_low - score_span
        score_strip[head, :, :score_low] = jnp.broadcast_to(entry(15), (both_rows, score_low))
        score_strip[head, :, score_low : score_low + score_span] = value
        score_strip[head, :, score_low + score_span :] = jnp.broadcast_to(
            entry(31), (both_rows, after)
        )
    ring.begin(1)
    cots = PairGather(spot, grad_ref, r.cot, r.cot_s, r.cot_r)
    gain_one = r.gain_one[...].astype(F32).reshape(1, width)
    gain_two = r.gain_two[...].astype(F32).reshape(1, width)

    def project(origin, block):
        value = block.astype(F32)
        low_value = (value * scale_of(value) * gain_one).astype(BF)
        mine = row_block(origin, rows)
        normed[mine] = low_value
        qkv[mine] = dot(low_value, r.qkv_w[...]).astype(BF)

    for part in range(3):
        loads[part].wait()
    project(spot.me, hidden_ref[...])
    for hop in range(spot.half):
        ring.step(hop)
        if hop < spot.half - 1:

            def both(side, carry, hop=hop):
                origin = spot.at((1 - 2 * side) * (hop + 1))
                project(origin, r.row[origin])
                return carry

            lax.fori_loop(0, 2, both, 0)
        else:
            origin = spot.at(spot.half)
            project(origin, r.row[origin])
    ring.finish()
    cots.relay()
    r.cot[0, :rows] = grad_ref[...]
    mixed_heads, mixed = r.mixed_heads, r.mixed

    def attend(block):
        mine = row_block(block, both_rows)
        turned_ids = jnp.broadcast_to(r.row_ids[:, mine], (LANES, both_rows)).T
        same = turned_ids[:, :1] == r.row_ids[...]
        window = strip_window(block, both_rows, length)
        for head in range(heads):
            columns = slice(head * depth, (head + 1) * depth)
            key = qkv[:, inner + head * depth : inner + (head + 1) * depth]
            value = qkv[:, 2 * inner + head * depth : 2 * inner + (head + 1) * depth]
            scores = dot_cols(qkv[mine, columns], key) + score_strip[head, :, window]
            scores = jnp.where(same, scores, MASKED)
            top = jnp.max(scores, axis=1, keepdims=True)
            weight = jnp.exp(scores - top)
            weight = weight * (1.0 / jnp.sum(weight, axis=1, keepdims=True))
            weight = weight.astype(BF)
            weights[head, mine] = weight
            mixed_heads[mine, columns] = dot(weight, value).astype(BF)

    def mixed_send(target):
        push(
            mixed_heads.at[row_block(target, rows)],
            mixed.at[:, own_columns],
            r.mixed_s,
            r.mixed_r,
            (spot.dp, target),
        )

    def attend_and_send(step, carry):
        block = (spot.me // 2 + step) % (count // 2)
        attend(block)
        for index in range(2):
            mixed_send(2 * block + index)
        return carry

    lax.fori_loop(1, count // 2, attend_and_send, 0)
    attend(spot.me // 2)
    mixed_send(exclusive(spot.me, 1))
    mixed[:, own_columns] = mixed_heads[row_block(spot.me, rows)]

    loads["out"].wait()
    wait_all(mixed.at[:, pl.ds(0, width - LANES)], r.mixed_r)
    inputs = hidden_ref[...].astype(F32)
    middle_ref = r.middle
    middle = inputs + dot(mixed[...], r.out_w[...])
    middle_ref[...] = middle
    tok, cot = r.tok, r.cot
    tok[0, :rows] = (middle * scale_of(middle) * gain_two).astype(BF)
    toks = PairGather(spot, tok.at[0, pl.ds(0, rows)], tok, r.tok_s, r.tok_r)
    gate_w, up_w, down_w = r.gate_w, r.up_w, r.down_w
    act, gate_g, up_g = r.act, r.gate_g, r.up_g
    for name in ("gate", "up", "down"):
        loads[name].wait()
    chunk = 256
    grads = PairSum(
        spot, r.grad_kept, r.grad_outs, r.grad_ins, r.grad_far_out, r.grad_far_in,
        r.grad_s, r.grad_r,
    )
    outs = PairSum(
        spot, r.out_kept, r.out_outs, r.out_ins, r.out_far_out, r.out_far_in,
        r.out_s, r.out_r,
    )

    def activate_half(half):
        mine = pl.ds(half * both_rows, both_rows)

        def tile(index, carry):
            columns = row_block(index, chunk)
            gate = dot(tok[half], gate_w[:, columns])
            up = dot(tok[half], up_w[:, columns])
            act_grad = dot_cols(cot[half], down_w[columns])
            place = index * chunk + lax.broadcasted_iota(jnp.int32, (1, chunk), 1)
            place = place - odd * (span - ff)
            inside = (place >= 0) & (place < ff)
            root = 0.7978845608028654
            squared = gate * gate
            bend = jnp.tanh(root * (gate + 0.044715 * gate * squared))
            share = 0.5 * (1.0 + bend)
            gelu = gate * share
            slope = share + 0.5 * gate * (1.0 - bend * bend) * root * (
                1.0 + 3 * 0.044715 * squared
            )
            act[mine, columns] = jnp.where(inside, gelu * up, 0.0).astype(BF)
            gate_g[mine, columns] = jnp.where(inside, act_grad * up * slope, 0.0).astype(BF)
            up_g[mine, columns] = jnp.where(inside, act_grad * gelu, 0.0).astype(BF)
            return carry

        lax.fori_loop(0, span // chunk, tile, 0)

    def spread(pair_sum, half, product):
        def tile(index, carry):
            columns = row_block(index, chunk)
            value = product(columns)
            pair_sum.kept[half, :, columns] = value[:rows]
            pair_sum.outs[half, :, columns] = value[rows:].astype(BF)
            return carry

        lax.fori_loop(0, width // chunk, tile, 0)
        pair_sum.near(half)

    def back_half(half):
        mine = pl.ds(half * both_rows, both_rows)
        spread(
            grads,
            half,
            lambda columns: dot_cols(gate_g[mine], gate_w[columns])
            + dot_cols(up_g[mine], up_w[columns]),
        )

    def out_half(half):
        mine = pl.ds(half * both_rows, both_rows)
        spread(outs, half, lambda columns: dot(act[mine], down_w[:, columns]))

    cots.near.wait_recv()
    cots.cross.wait_recv()
    toks.near.wait_recv()
    activate_half(0)
    toks.relay()
    back_half(0)
    toks.cross.wait_recv()
    activate_half(1)
    back_half(1)

    down_terms, pair_terms = r.down_terms, r.pair_terms
    spare = span - ff

    def down_tile(index, carry):
        columns = row_block(index, LANES)
        value = dot_rows(act[:both_rows], cot[0, :, columns]) + dot_rows(
            act[both_rows:], cot[1, :, columns]
        )
        down_terms[index] = jnp.where(odd == 1, value[spare:], value[:ff]).astype(BF)
        return carry

    lax.fori_loop(0, count, down_tile, 0)
    down_sum = RingSum(spot, down_terms, r.down_buf, r.down_s, r.down_r)
    down_sum.begin()
    grads.over()
    full = ff // LANES
    lane = lax.broadcasted_iota(jnp.int32, (LANES, LANES), 1)

    def pair_tile(index, carry):
        columns = row_block(index, LANES)
        parts = []
        for source in (gate_g, up_g):
            parts.append(
                dot_rows(tok[0, :, columns], source[:both_rows])
                + dot_rows(tok[1, :, columns], source[both_rows:])
            )
        cut = lambda value, place: value[:, place * LANES : (place + 1) * LANES]
        for part, value in enumerate(parts):
            for place in range(full):
                start = (part * full + place) * LANES
                pair_terms[index, start : start + LANES] = jnp.where(
                    odd == 1, cut(value, place + 1), cut(value, place)
                ).astype(BF)
        edges = [jnp.where(odd == 1, cut(value, 0), cut(value, full)) for value in parts]
        turned = pltpu.roll(edges[1], LANES // 2, 1)
        lower = (lane < LANES // 2).astype(jnp.int32)
        pair_terms[index, 2 * full * LANES :] = jnp.where(lower == odd, turned, edges[0]).astype(BF)
        return carry

    lax.fori_loop(0, count, pair_tile, 0)
    pair_sum = RingSum(spot, pair_terms, r.pair_buf, r.pair_s, r.pair_r)
    pair_sum.begin()
    down_sum.step(0)
    out_half(0)
    out_half(1)

    normed_two_grad = grads.total()
    middle = middle_ref[...]
    scale_two = scale_of(middle)
    lifted = gain_two * normed_two_grad
    middle_grad = (
        grad_ref[...].astype(F32)
        + scale_two * lifted
        - middle * (scale_two * scale_two * scale_two)
        * jnp.mean(middle * lifted, axis=-1, keepdims=True)
    )
    middle_grad_ref = r.middle_grad
    middle_grad_ref[...] = middle_grad
    small = r.small
    small[...] = jnp.zeros_like(small)
    gain_grad = jnp.sum(normed_two_grad * middle * scale_two, axis=0, keepdims=True)
    tiles = width // LANES
    for tile in range(tiles):
        small[tiles + tile : tiles + tile + 1] = gain_grad[:, tile * LANES : (tile + 1) * LANES]
    branch, own_branch = r.row, r.own_branch
    own_branch[...] = middle_grad.astype(BF)
    branches = RingGather(
        spot,
        own_branch,
        branch,
        r.branch_s,
        r.branch_r,
        SPLITS[0],
    )
    keys, values, dqkv, packed = r.keys, r.values, r.dqkv, r.packed

    own_out = r.out_w.at[row_block(spot.me, inner)]
    quarter, slim = width // 4, inner // 4

    def attend_back(origin):
        mine = row_block(origin, rows)
        window = strip_window(origin, rows, length)
        mixed_grad = dot_cols(branch[origin], own_out[...]).astype(BF)
        for head in range(heads):
            columns = slice(head * depth, (head + 1) * depth)
            key = qkv[:, inner + head * depth : inner + (head + 1) * depth]
            value = qkv[:, 2 * inner + head * depth : 2 * inner + (head + 1) * depth]
            grad = mixed_grad[:, columns]
            weight_low = weights[head, mine]
            weight = weight_low.astype(F32)
            scaled = weight * dot_cols(grad, value)
            score_grad = scaled - weight * jnp.sum(scaled, axis=1, keepdims=True)
            strip[head, :, window] += score_grad
            score_low = score_grad.astype(BF)
            dqkv[mine, columns] = dot(score_low, key).astype(BF)
            keys[:, columns] += dot_rows(score_low, qkv[mine, columns])
            values[:, columns] += dot_rows(weight_low, grad)
        terms = dot_rows(mixed_heads[mine], branch[origin])
        for tile in range(tiles):
            for index in range(4):
                base = 3 * quarter + tile * slim
                packed[index, base : base + slim] += terms[
                    index * slim : (index + 1) * slim, tile * LANES : (tile + 1) * LANES
                ]
        terms = dot_rows(normed[mine], dqkv[mine, :inner])
        for index in range(4):
            packed[index, :quarter] += terms[index * quarter : (index + 1) * quarter]

    mesh_sets = [r.gather_sems[7 * index : 7 * index + 7] for index in range(3)]
    down = MeshGather(spot, r.down_block, r.down_all, SHARES[0], mesh_sets[0])
    pair = MeshGather(spot, r.pair_block, r.pair_all, SHARES[1], mesh_sets[1])
    proj = MeshGather(spot, r.proj_block, r.proj_all, SHARES[2], mesh_sets[2])
    core, side = odd, spot.dp // 2
    own_dqkv = r.own_dqkv

    def branch_start():
        branches.begin(0)
        branch[spot.me] = own_branch[...]
        strip[...] = jnp.zeros_like(strip)
        keys[...] = jnp.zeros_like(keys)
        values[...] = jnp.zeros_like(values)
        branches.begin(1)
        packed[...] = jnp.zeros_like(packed)
        attend_back(spot.me)

    def finish_down():
        down_sum.total(r.down_block)
        down.begin()
        load("down_own", r.down_block, r.down_all.at[spot.dp, spot.me])

    def finish_pair():
        pair_sum.total(r.pair_block)
        pair.begin()
        load("pair_own", r.pair_block, r.pair_all.at[spot.dp, spot.me])

    def attend_pair(hop):
        def both_back(index, carry):
            attend_back(spot.at((1 - 2 * index) * (hop + 1)))
            return carry

        lax.fori_loop(0, 2, both_back, 0)

    def finish_heads():
        dqkv[:, inner : 2 * inner] = keys[...].astype(BF)
        dqkv[:, 2 * inner :] = values[...].astype(BF)

        def quarter_block(index, carry):
            block = dot_rows(normed[:, row_block(index, quarter)], dqkv[:, inner:])
            for part in range(2):
                packed[index, (part + 1) * quarter : (part + 2) * quarter] = block[
                    :, part * LANES : (part + 1) * LANES
                ]
            return carry

        lax.fori_loop(0, 4, quarter_block, 0)
        for index in range(2):
            r.near_out[index] = packed[2 * index + 1 - core].astype(BF)
        return push(r.near_out, r.near_in, r.proj_s.at[0], r.proj_r.at[0], spot.twin)

    def heads_over():
        near.wait_recv()
        r.far_out[...] = (
            packed[2 * (1 - side) + core] + r.near_in[1 - side].astype(F32)
        ).astype(BF)
        return push(r.far_out, r.far_in, r.proj_s.at[1], r.proj_r.at[1], spot.far, SPLITS[1])

    def finish_proj():
        far.wait_recv()
        r.proj_block[...] = (
            packed[2 * side + core] + r.near_in[side].astype(F32) + r.far_in[...].astype(F32)
        ).astype(BF)
        proj.begin()
        load("proj_own", r.proj_block, r.proj_all.at[spot.dp, spot.me])

    def trade():
        for device in spot.others:
            for part in range(3):
                push(
                    dqkv.at[row_block(device[1], rows), pl.ds(part * LANES, LANES)],
                    own_dqkv.at[part, :, own_columns],
                    r.trade_s,
                    r.trade_r,
                    device,
                )
        for part in range(3):
            own_dqkv[part, :, own_columns] = dqkv[
                row_block(spot.me, rows), part * LANES : (part + 1) * LANES
            ]

    def finish_table():
        for head in range(heads):
            middle_part = strip[head, :, low : low + near_span]
            before = jnp.sum(strip[head, :, :low], axis=0, keepdims=True)
            after = jnp.sum(strip[head, :, low + near_span :], axis=0, keepdims=True)
            levels = []
            for level in range(level_count):
                part = jnp.sum(jnp.where(bucket == level, middle_part, 0.0), axis=0, keepdims=True)
                line = part[:, :LANES]
                for tile in range(1, near_span // LANES):
                    line = line + part[:, tile * LANES : (tile + 1) * LANES]
                edge = before if level == 15 else after if level == 31 else None
                if edge is not None:
                    for tile in range(edge.shape[1] // LANES):
                        line = line + edge[:, tile * LANES : (tile + 1) * LANES]
                r.levels[level : level + 1] = line
            sums = lax.dot_general(
                jnp.ones((8, LANES), F32),
                r.levels[...],
                (((1,), (1,)), ((), ())),
                precision=lax.Precision.HIGHEST,
                preferred_element_type=F32,
            )
            small[pl.ds(2 * tiles + spot.me * heads + head, 1), : level_count] = sums[:1]

    def finish_input():
        for part in range(3):
            loads[3 + part].wait()
        wait_all(own_dqkv.at[:, :, pl.ds(0, width - LANES)], r.trade_r)
        normed_grad = dot_cols(own_dqkv[0], r.full_w[0])
        for part in range(1, 3):
            normed_grad = normed_grad + dot_cols(own_dqkv[part], r.full_w[part])
        inputs = hidden_ref[...].astype(F32)
        scale_one = scale_of(inputs)
        raised = gain_one * normed_grad
        r.hidden_grad[...] = (
            middle_grad_ref[...]
            + scale_one * raised
            - inputs * (scale_one * scale_one * scale_one)
            * jnp.mean(inputs * raised, axis=-1, keepdims=True)
        )
        gain_grad = jnp.sum(normed_grad * inputs * scale_one, axis=0, keepdims=True)
        for tile in range(tiles):
            small[tile : tile + 1] = gain_grad[:, tile * LANES : (tile + 1) * LANES]

    partners = [spot.twin, spot.far]
    bit = 1
    while bit < count:
        partners.append((spot.dp, exclusive(spot.me, bit)))
        bit *= 2
    small_out, small_in = r.small_out, r.small_in
    small_copies = []

    def small_send():
        index = len(small_copies)
        if index < len(partners):
            small_out[index] = small[...]
            small_copies.append(
                push(
                    small_out.at[index], small_in.at[index],
                    r.small_s.at[index], r.small_r.at[index], partners[index],
                )
            )

    def small_step():
        if len(small_copies) <= len(partners) and small_copies:
            index = len(small_copies) - 1
            small_copies[index].wait_recv()
            small[...] += small_in[index]
            small_send()

    def pass_round(gather, hop):
        gather.step(hop)
        gather.step_far(hop)

    branch_start()
    branches.step(0)
    attend_pair(0)
    down_sum.step(1)
    branches.step(1)
    attend_pair(1)
    down_sum.step(2)
    branches.step(2)
    finish_down()
    down.begin_far()
    pair_sum.step(0)
    attend_pair(2)
    pass_round(down, 0)
    pair_sum.step(1)
    pass_round(down, 1)
    branches.step(3)
    outs.over()
    attend_back(spot.at(spot.half))
    near = finish_heads()
    finish_table()
    trade()
    pass_round(down, 2)
    far = heads_over()
    pair_sum.step(2)
    pass_round(down, 3)
    finish_input()
    finish_proj()
    small_send()
    proj.begin_far()
    small_step()
    finish_pair()
    pass_round(proj, 0)
    pair.begin_far()
    pass_round(proj, 1)
    small_step()
    pass_round(pair, 0)
    r.block_out[...] = (middle + outs.total()).astype(BF)
    down.step_far(4)
    pass_round(proj, 2)
    small_step()
    pass_round(pair, 1)
    small_step()
    pass_round(proj, 3)
    pass_round(pair, 2)
    pass_round(pair, 3)
    small_step()
    proj.step_far(4)
    pair.step_far(4)
    r.small_sum[...] = small[...]
    for name in ("down_own", "pair_own", "proj_own"):
        loads[name].wait()
    wait_all(mixed_heads.at[pl.ds(0, length - rows)], r.mixed_s)
    wait_all(dqkv.at[pl.ds(0, length - rows)], r.trade_s)
    for copy in [near, far] + small_copies:
        copy.wait_send()
    for item in (cots, toks, grads, outs, down_sum, pair_sum, branches, down, pair, proj):
        item.finish()


SHARES = (95, 35, 95)
SPLITS = (1, 1)


def layer(arrays, count, heads, depth, ff):
    rows, width = arrays["hidden"].shape
    length = count * rows
    inner = heads * depth
    half = count // 2
    span = (ff + LANES - 1) // LANES * LANES
    pair_rows = 2 * ff // LANES * rows
    proj_rows = 3 * (width // 4) + inner // 4 * (width // LANES)
    small_rows = 2 * (width // LANES) + count * heads
    steps = 2 + (count - 1).bit_length()
    dma = pltpu.SemaphoreType.DMA
    specs = dict(
        hidden=VMEM,
        out_grad=VMEM,
        gain_one=VMEM,
        gain_two=VMEM,
        row_ids=VMEM,
        table=VMEM,
    )
    shape = jax.ShapeDtypeStruct
    results = dict(
        block_out=(shape((rows, width), BF), VMEM),
        hidden_grad=(shape((rows, width), F32), VMEM),
        small_sum=(shape((small_rows, LANES), F32), VMEM),
        down_all=(shape((4, count, ff, LANES), BF), ANY),
        pair_all=(shape((4, count, pair_rows, LANES), BF), ANY),
        proj_all=(shape((4, count, proj_rows, LANES), BF), ANY),
    )
    vm = pltpu.VMEM
    ring_buf = lambda n: vm((2, half, 2, n // 2, LANES), BF)
    pairs = {}
    for name in ("grad", "out"):
        pairs[name + "_kept"] = vm((2, rows, width), F32)
        pairs[name + "_outs"] = vm((2, rows, width), BF)
        pairs[name + "_ins"] = vm((2, rows, width), BF)
        pairs[name + "_far_out"] = vm((rows, width), BF)
        pairs[name + "_far_in"] = vm((rows, width), BF)
        pairs[name + "_s"] = dma((3,))
        pairs[name + "_r"] = dma((3,))
    for name in ("cot", "tok"):
        pairs[name] = vm((2, 2 * rows, width), BF)
        pairs[name + "_s"] = dma((3,))
        pairs[name + "_r"] = dma((3,))
    pairs["row"] = vm((count, rows, width), BF)
    for name in ("row", "branch"):
        pairs[name + "_s"] = dma(())
        pairs[name + "_r"] = dma((2, half, 2))
    for name, size in (("down", ff), ("pair", pair_rows)):
        pairs[name + "_terms"] = vm((count, size, LANES), BF)
        pairs[name + "_buf"] = ring_buf(size)
        pairs[name + "_block"] = vm((size, LANES), BF)
        pairs[name + "_s"] = dma(())
        pairs[name + "_r"] = dma((2, half, 2))
    scratch = dict(
        **pairs,
        score_strip=vm((heads, 2 * rows, 2 * length - rows), F32),
        normed=vm((length, width), BF),
        qkv=vm((length, 3 * inner), BF),
        weights=vm((heads, length, length), BF),
        mixed_heads=vm((length, inner), BF),
        mixed=vm((rows, width), BF),
        qkv_w=vm((width, 3 * inner), BF),
        full_w=vm((3, width, width), BF),
        out_w=vm((width, width), BF),
        gate_w=vm((width, span), BF),
        up_w=vm((width, span), BF),
        down_w=vm((span, width), BF),
        middle=vm((rows, width), F32),
        middle_grad=vm((rows, width), F32),
        act=vm((4 * rows, span), BF),
        gate_g=vm((4 * rows, span), BF),
        up_g=vm((4 * rows, span), BF),
        own_branch=vm((rows, width), BF),
        keys=vm((length, inner), F32),
        values=vm((length, inner), F32),
        dqkv=vm((length, 3 * inner), BF),
        own_dqkv=vm((3, rows, width), BF),
        packed=vm((4, proj_rows, LANES), F32),
        near_out=vm((2, proj_rows, LANES), BF),
        near_in=vm((2, proj_rows, LANES), BF),
        far_out=vm((proj_rows, LANES), BF),
        far_in=vm((proj_rows, LANES), BF),
        proj_block=vm((proj_rows, LANES), BF),
        levels=vm((arrays["table"].shape[1], LANES), F32),
        small=vm((small_rows, LANES), F32),
        small_out=vm((steps, small_rows, LANES), F32),
        small_in=vm((steps, small_rows, LANES), F32),
        load_sems=dma((16,)),
        mixed_s=dma(()),
        mixed_r=dma(()),
        trade_s=dma(()),
        trade_r=dma(()),
        proj_s=dma((2,)),
        proj_r=dma((2,)),
        small_s=dma((steps,)),
        small_r=dma((steps,)),
    )
    names = tuple(arrays) + tuple(results) + tuple(scratch)

    def body(*refs):
        plain = refs[: len(names)]
        layer_body(
            count, heads, depth, ff, names + ("gather_sems",), *plain, refs[len(names) :]
        )

    outs = pl.pallas_call(
        body,
        name="layer",
        out_shape=tuple(value[0] for value in results.values()),
        in_specs=[specs.get(name, ANY) for name in arrays],
        out_specs=tuple(value[1] for value in results.values()),
        scratch_shapes=list(scratch.values()) + mesh_sems(count) * 3,
        compiler_params=comm_params(0, 60 << 20),
    )(*arrays.values())
    return types.SimpleNamespace(**dict(zip(results, outs)))


def widen_body(
    part, down_ref, pair_ref, proj_ref, slim_ref, block_ref, hidden_ref, small_ref,
    down_out, gate_out, up_out, query_out, key_out, value_out, out_out,
    block_out, hidden_out, one_out, two_out, bias_out, small, sems,
):
    copies = [
        pltpu.make_async_copy(source, target, sems.at[index])
        for index, (source, target) in enumerate(
            ((small_ref, small), (block_ref, block_out), (hidden_ref, hidden_out))
        )
    ]
    step = pl.program_id(0)

    @pl.when(step == 0)
    def _():
        for copy in copies:
            copy.start()

    full, half = part // LANES, LANES // 2
    for source in range(down_ref.shape[1]):
        columns = slice(source * LANES, (source + 1) * LANES)
        down_out[:, columns] = down_ref[0, source].astype(F32)
        for index, o_ref in enumerate((query_out, key_out, value_out)):
            o_ref[:, columns] = proj_ref[0, source, index].astype(F32)
    dps = pair_ref.shape[0]
    slim = out_out.shape[0] // dps
    for dp in range(dps):
        base = dp * part
        shift = half if dp % 2 else 0
        for which, o_ref in enumerate((gate_out, up_out)):
            for tile in range(full):
                column = base + shift + tile * LANES
                o_ref[:, column : column + LANES] = pair_ref[dp, 0, which * full + tile].astype(F32)
        edge = pair_ref[dp, 0, 2 * full].astype(F32)
        column = base if dp % 2 else base + full * LANES
        gate_half = slice(half, LANES) if dp % 2 else slice(0, half)
        up_half = slice(0, half) if dp % 2 else slice(half, LANES)
        gate_out[:, column : column + half] = edge[:, gate_half]
        up_out[:, column : column + half] = edge[:, up_half]
        for tile in range(out_out.shape[1] // LANES):
            out_out[dp * slim : (dp + 1) * slim, tile * LANES : (tile + 1) * LANES] = slim_ref[
                dp, 0, 0, tile * slim : (tile + 1) * slim
            ].astype(F32)

    @pl.when(step == pl.num_programs(0) - 1)
    def _():
        for copy in copies:
            copy.wait()
        tiles = one_out.shape[0]
        one_out[...] = small[:tiles]
        two_out[...] = small[tiles : 2 * tiles]
        bias_out[...] = small[2 * tiles :, : bias_out.shape[1]]


def widen(out, levels, ff):
    rows, width = out.hidden_grad.shape
    dps, count = out.down_all.shape[:2]
    quarter = width // dps
    small_rows = out.small_sum.shape[0]
    tiles = width // LANES
    heads = small_rows - 2 * tiles
    pieces = count // dps
    pair = out.pair_all.reshape(dps, count, -1, rows, LANES)
    proj = out.proj_all.reshape(dps, count, 4, quarter, LANES)
    shape = lambda *dims: jax.ShapeDtypeStruct(dims, F32)
    spec = pl.BlockSpec
    whole = lambda *dims: spec(dims, lambda i: (0,) * len(dims))
    row = lambda size, span: spec((size, span), lambda i: (i, 0))
    return pl.pallas_call(
        functools.partial(widen_body, ff),
        name="widen",
        grid=(count,),
        out_shape=(
            shape(dps * ff, width),
            shape(width, dps * ff),
            shape(width, dps * ff),
            *[shape(width, width)] * 4,
            jax.ShapeDtypeStruct((rows, width), BF),
            shape(rows, width),
            shape(tiles, LANES),
            shape(tiles, LANES),
            shape(heads, levels),
        ),
        in_specs=[
            spec((1, count, ff // pieces, LANES), lambda i: (i // pieces, 0, i % pieces, 0)),
            spec((dps, 1, pair.shape[2], rows, LANES), lambda i: (0, i, 0, 0, 0)),
            spec((1, count, 3, quarter // pieces, LANES), lambda i: (i // pieces, 0, 0, i % pieces, 0)),
            spec((dps, 1, 1, quarter, LANES), lambda i: (0, i, 3, 0, 0)),
            ANY,
            ANY,
            ANY,
        ],
        out_specs=(
            row(ff // pieces, width),
            row(rows, dps * ff),
            row(rows, dps * ff),
            *[row(quarter // pieces, width)] * 3,
            row(width // count, width),
            whole(rows, width),
            whole(rows, width),
            whole(tiles, LANES),
            whole(tiles, LANES),
            whole(heads, levels),
        ),
        scratch_shapes=[pltpu.VMEM((small_rows, LANES), F32), pltpu.SemaphoreType.DMA((3,))],
        compiler_params=pltpu.CompilerParams(vmem_limit_bytes=56 << 20),
    )(out.down_all, pair, proj, proj, out.block_out, out.hidden_grad, out.small_sum)


def split_shards(
    hidden,
    group_ids,
    norm1_gain,
    query_weight,
    key_weight,
    value_weight,
    out_weight,
    relative_bias,
    norm2_gain,
    gate_weight,
    up_weight,
    down_projection_weight,
    out_grad,
    *,
    count,
):
    width = hidden.shape[2]
    levels, head_count = relative_bias.shape
    depth = query_weight.shape[1] // head_count
    heads = head_count // count
    ff = gate_weight.shape[1] // 4
    arrays = dict(
        hidden=hidden[0],
        out_grad=out_grad[0],
        gain_one=norm1_gain,
        gain_two=norm2_gain,
        row_ids=group_ids,
        table=relative_bias.T,
        query_weight=query_weight,
        key_weight=key_weight,
        value_weight=value_weight,
        out_weight=out_weight,
        gate_weight=gate_weight,
        up_weight=up_weight,
        down_weight=down_projection_weight,
    )
    out = layer(arrays, count, heads, depth, ff)
    down, gate, up, query, key, value, projected, block, grad, one, two, bias = widen(
        out, levels, ff
    )
    return (
        block[None], grad[None], one.reshape(-1), query, key, value, projected, bias.T,
        two.reshape(-1), gate, up, down,
    )


def rms_norm(vector, norm_gain):
    return (
        vector * lax.rsqrt(jnp.mean(vector * vector, axis=-1, keepdims=True) + EPSILON) * norm_gain
    )


def activate(gate_proj, up_proj):
    return jax.nn.gelu(gate_proj, approximate=True) * up_proj


def scores_of(
    query_part, key_part, query_places, key_places, query_groups, key_groups, bias_lookup
):
    bucket = bucket_of(key_places[None, :] - query_places[:, None])
    levels = jnp.arange(bias_lookup.shape[0], dtype=jnp.int32)
    one_hot_mask = (bucket[None] == levels[:, None, None]).astype(jnp.bfloat16)
    bias_patch_block = jnp.einsum(
        "ctf,cx->xtf", one_hot_mask, bias_lookup, preferred_element_type=jnp.float32
    )
    raw_scores = (
        jnp.einsum("qhd,khd->hqk", query_part, key_part, preferred_element_type=jnp.float32)
        + bias_patch_block
    )
    same_group = query_groups[:, None] == key_groups[None, :]
    return (one_hot_mask, jnp.where(same_group[None], raw_scores, MASKED))


def shards(
    hidden,
    group_ids,
    norm1_gain,
    query_weight,
    key_weight,
    value_weight,
    out_weight,
    relative_bias,
    norm2_gain,
    gate_weight,
    up_weight,
    down_projection_weight,
    out_grad,
):
    tok_rows = hidden.shape[1]
    head_count = relative_bias.shape[1]
    inner_width = query_weight.shape[1]
    head_depth = inner_width // head_count
    row_length = group_ids.shape[1]
    row_start = lax.axis_index("seq") * tok_rows
    key_block = min(1024, row_length)
    block_count = row_length // key_block
    row_groups = group_ids[0]
    own_groups = lax.dynamic_slice_in_dim(row_groups, row_start, tok_rows)
    own_places = row_start + jnp.arange(tok_rows, dtype=jnp.int32)
    all_places = jnp.arange(row_length, dtype=jnp.int32)

    def key_blocks(key_rows, value_rows):
        return (
            key_rows.reshape(block_count, key_block, head_count, head_depth),
            value_rows.reshape(block_count, key_block, head_count, head_depth),
            row_groups.reshape(block_count, key_block),
            all_places.reshape(block_count, key_block),
        )

    inputs = hidden[0].astype(jnp.float32)
    normed, norm_pull = jax.vjp(rms_norm, inputs, norm1_gain.astype(jnp.float32))
    normed_low = normed.astype(jnp.bfloat16)
    query_low = jnp.dot(normed_low, query_weight, preferred_element_type=jnp.float32).astype(
        jnp.bfloat16
    )
    key_low = jnp.dot(normed_low, key_weight, preferred_element_type=jnp.float32).astype(
        jnp.bfloat16
    )
    value_low = jnp.dot(normed_low, value_weight, preferred_element_type=jnp.float32).astype(
        jnp.bfloat16
    )
    key_all, value_all = (
        lax.all_gather(key_low, "seq", axis=0, tiled=True),
        lax.all_gather(value_low, "seq", axis=0, tiled=True),
    )
    query_heads = query_low.reshape(tok_rows, head_count, head_depth)

    def gather_stats(carry_state, scanned):
        running_max, running_sum = carry_state
        key_part, value_part, key_groups, key_places = scanned
        one_hot_mask, scores = scores_of(
            query_heads, key_part, own_places, key_places, own_groups, key_groups, relative_bias
        )
        new_max = jnp.maximum(running_max, jnp.max(scores, axis=-1))
        running_sum = running_sum * jnp.exp(running_max - new_max) + jnp.sum(
            jnp.exp(scores - new_max[..., None]), axis=-1
        )
        return ((new_max, running_sum), None)

    stats_init = (
        jnp.full((head_count, tok_rows), MASKED, jnp.float32),
        jnp.zeros((head_count, tok_rows), jnp.float32),
    )
    (running_max, running_sum), _ = lax.scan(
        gather_stats, stats_init, key_blocks(key_all, value_all)
    )
    log_total = running_max + jnp.log(running_sum)

    def gather_values(summed, scanned):
        key_part, value_part, key_groups, key_places = scanned
        one_hot_mask, scores = scores_of(
            query_heads, key_part, own_places, key_places, own_groups, key_groups, relative_bias
        )
        attention_low = jnp.exp(scores - log_total[..., None]).astype(jnp.bfloat16)
        return (
            summed
            + jnp.einsum(
                "hqk,khd->qhd", attention_low, value_part, preferred_element_type=jnp.float32
            ),
            None,
        )

    mixed, _ = lax.scan(
        gather_values,
        jnp.zeros((tok_rows, head_count, head_depth), jnp.float32),
        key_blocks(key_all, value_all),
    )
    mixed_low = mixed.reshape(tok_rows, inner_width).astype(jnp.bfloat16)
    middle = inputs + jnp.dot(mixed_low, out_weight, preferred_element_type=jnp.float32)
    normed_two, norm_two_pull = jax.vjp(rms_norm, middle, norm2_gain.astype(jnp.float32))
    normed_two_low = normed_two.astype(jnp.bfloat16)
    gate_proj = jnp.dot(normed_two_low, gate_weight, preferred_element_type=jnp.float32)
    up_proj = jnp.dot(normed_two_low, up_weight, preferred_element_type=jnp.float32)
    activated, act_pull = jax.vjp(activate, gate_proj, up_proj)
    activated_low = activated.astype(jnp.bfloat16)
    result = middle + jnp.dot(
        activated_low, down_projection_weight, preferred_element_type=jnp.float32
    )
    block_out = result.astype(jnp.bfloat16)[None]
    cotangent_low = out_grad[0]
    grad_down = dot_rows(activated_low, cotangent_low)
    act_grad = dot_cols(cotangent_low, down_projection_weight)
    gate_grad, up_grad = act_pull(act_grad)
    gate_grad_low = gate_grad.astype(jnp.bfloat16)
    up_grad_low = up_grad.astype(jnp.bfloat16)
    grad_gate = dot_rows(normed_two_low, gate_grad_low)
    grad_up = dot_rows(normed_two_low, up_grad_low)
    normed_two_grad = dot_cols(gate_grad_low, gate_weight) + dot_cols(up_grad_low, up_weight)
    middle_norm_grad, grad_gain_two = norm_two_pull(normed_two_grad)
    middle_grad = cotangent_low.astype(jnp.float32) + middle_norm_grad
    branch_grad_low = middle_grad.astype(jnp.bfloat16)
    grad_out = dot_rows(mixed_low, branch_grad_low)
    mixed_grad_low = (
        dot_cols(branch_grad_low, out_weight)
        .astype(jnp.bfloat16)
        .reshape(tok_rows, head_count, head_depth)
    )
    row_dots = jnp.einsum("qhd,qhd->hq", mixed_grad_low.astype(jnp.float32), mixed)
    key_back, value_back = (
        lax.all_gather(key_low, "seq", axis=0, tiled=True),
        lax.all_gather(value_low, "seq", axis=0, tiled=True),
    )
    grads_init = (
        jnp.zeros((tok_rows, head_count, head_depth), jnp.float32),
        jnp.zeros(relative_bias.shape, jnp.float32),
    )

    def backward_block(carry_state, scanned):
        query_grad, table_grad = carry_state
        key_part, value_part, key_groups, key_places = scanned
        one_hot_mask, scores = scores_of(
            query_heads, key_part, own_places, key_places, own_groups, key_groups, relative_bias
        )
        attention = jnp.exp(scores - log_total[..., None])
        grad_weights = jnp.einsum(
            "qhd,khd->hqk", mixed_grad_low, value_part, preferred_element_type=jnp.float32
        )
        score_gradients = (attention * (grad_weights - row_dots[..., None])).astype(jnp.bfloat16)
        query_grad = query_grad + jnp.einsum(
            "hqk,khd->qhd", score_gradients, key_part, preferred_element_type=jnp.float32
        )
        table_grad = table_grad + jnp.einsum(
            "oei,cei->oc", one_hot_mask, score_gradients, preferred_element_type=jnp.float32
        )
        key_grad = jnp.einsum(
            "hqk,qhd->khd", score_gradients, query_heads, preferred_element_type=jnp.float32
        )
        value_grad = jnp.einsum(
            "hqk,qhd->khd",
            attention.astype(jnp.bfloat16),
            mixed_grad_low,
            preferred_element_type=jnp.float32,
        )
        return ((query_grad, table_grad), (key_grad, value_grad))

    (query_grad, table_grad), (key_terms, value_terms) = lax.scan(
        backward_block, grads_init, key_blocks(key_back, value_back)
    )
    key_grad, value_grad = (
        lax.psum_scatter(
            key_terms.reshape(row_length, inner_width), "seq", scatter_dimension=0, tiled=True
        ),
        lax.psum_scatter(
            value_terms.reshape(row_length, inner_width), "seq", scatter_dimension=0, tiled=True
        ),
    )
    query_grad_low = query_grad.reshape(tok_rows, inner_width).astype(jnp.bfloat16)
    key_grad_low = key_grad.astype(jnp.bfloat16)
    value_grad_low = value_grad.astype(jnp.bfloat16)
    grad_query = dot_rows(normed_low, query_grad_low)
    grad_key = dot_rows(normed_low, key_grad_low)
    grad_value = dot_rows(normed_low, value_grad_low)
    normed_grad = (
        dot_cols(query_grad_low, query_weight)
        + dot_cols(key_grad_low, key_weight)
        + dot_cols(value_grad_low, value_weight)
    )
    input_norm_grad, grad_gain_one = norm_pull(normed_grad)
    hidden_grad = (middle_grad + input_norm_grad)[None]
    local_grads = (
        grad_gain_one,
        grad_query,
        grad_key,
        grad_value,
        grad_out,
        table_grad.reshape(-1),
        grad_gain_two,
        grad_gate,
        grad_up,
        grad_down,
    )
    shared = (
        lax.psum_scatter(local_grads[0], "seq", scatter_dimension=0, tiled=True),
        lax.psum_scatter(local_grads[1], "seq", scatter_dimension=0, tiled=True),
        lax.psum_scatter(local_grads[2], "seq", scatter_dimension=0, tiled=True),
        lax.psum_scatter(local_grads[3], "seq", scatter_dimension=0, tiled=True),
        lax.psum_scatter(local_grads[4], "seq", scatter_dimension=0, tiled=True),
        lax.psum_scatter(local_grads[5], "seq", scatter_dimension=0, tiled=True),
        lax.psum_scatter(local_grads[6], "seq", scatter_dimension=0, tiled=True),
        lax.psum_scatter(local_grads[7], "seq", scatter_dimension=0, tiled=True),
        lax.psum_scatter(local_grads[8], "seq", scatter_dimension=0, tiled=True),
        lax.psum_scatter(local_grads[9], "seq", scatter_dimension=0, tiled=True),
    )
    shared = (
        lax.psum(shared[0].astype(jnp.bfloat16), "dp").astype(jnp.float32),
        lax.psum(shared[1].astype(jnp.bfloat16), "dp").astype(jnp.float32),
        lax.psum(shared[2].astype(jnp.bfloat16), "dp").astype(jnp.float32),
        lax.psum(shared[3].astype(jnp.bfloat16), "dp").astype(jnp.float32),
        lax.psum(shared[4].astype(jnp.bfloat16), "dp").astype(jnp.float32),
        lax.psum(shared[5].astype(jnp.bfloat16), "dp").astype(jnp.float32),
        lax.psum(shared[6].astype(jnp.bfloat16), "dp").astype(jnp.float32),
        lax.psum(shared[7].astype(jnp.bfloat16), "dp").astype(jnp.float32),
        lax.psum(shared[8].astype(jnp.bfloat16), "dp").astype(jnp.float32),
        lax.psum(shared[9].astype(jnp.bfloat16), "dp").astype(jnp.float32),
    )
    summed = (
        lax.all_gather(shared[0].astype(jnp.bfloat16), "seq", axis=0, tiled=True).astype(
            jnp.float32
        ),
        lax.all_gather(shared[1].astype(jnp.bfloat16), "seq", axis=0, tiled=True).astype(
            jnp.float32
        ),
        lax.all_gather(shared[2].astype(jnp.bfloat16), "seq", axis=0, tiled=True).astype(
            jnp.float32
        ),
        lax.all_gather(shared[3].astype(jnp.bfloat16), "seq", axis=0, tiled=True).astype(
            jnp.float32
        ),
        lax.all_gather(shared[4].astype(jnp.bfloat16), "seq", axis=0, tiled=True).astype(
            jnp.float32
        ),
        lax.all_gather(shared[5].astype(jnp.bfloat16), "seq", axis=0, tiled=True).astype(
            jnp.float32
        ),
        lax.all_gather(shared[6].astype(jnp.bfloat16), "seq", axis=0, tiled=True).astype(
            jnp.float32
        ),
        lax.all_gather(shared[7].astype(jnp.bfloat16), "seq", axis=0, tiled=True).astype(
            jnp.float32
        ),
        lax.all_gather(shared[8].astype(jnp.bfloat16), "seq", axis=0, tiled=True).astype(
            jnp.float32
        ),
        lax.all_gather(shared[9].astype(jnp.bfloat16), "seq", axis=0, tiled=True).astype(
            jnp.float32
        ),
    )
    return (
        block_out,
        hidden_grad,
        summed[0],
        summed[1],
        summed[2],
        summed[3],
        summed[4],
        summed[5].reshape(relative_bias.shape),
        summed[6],
        summed[7],
        summed[8],
        summed[9],
    )


def solution(mesh):
    placed = (P("dp", "seq", None), P("dp", None)) + (P(),) * 10 + (P("dp", "seq", None),)
    out_specs = (P("dp", "seq", None),) * 2 + (P(),) * 10
    count = mesh.shape["seq"]

    def run(*args):
        hidden, query_weight, relative_bias = args[0], args[3], args[7]
        head_count = relative_bias.shape[1]
        inner = query_weight.shape[1] // count
        fits = (
            mesh.shape["dp"] == 4
            and count % 2 == 0
            and head_count % count == 0
            and inner == LANES
            and hidden.shape[2] == count * LANES
            and hidden.shape[1] == count * LANES
            and args[9].shape[1] % (4 * LANES) == 2 * LANES
        )
        body = functools.partial(split_shards, count=count) if fits else shards
        return jax.shard_map(
            body, mesh=mesh, in_specs=placed, out_specs=out_specs, check_vma=False
        )(*args)

    return run
```

```python
import functools
import types

import jax
import jax.numpy as jnp
from jax import lax
from jax.experimental import pallas as pl
from jax.experimental.pallas import tpu as pltpu
from jax.sharding import PartitionSpec as P

EPSILON = 1e-06
MASKED = -1e30
THRESHOLDS = (12, 16, 23, 32, 46, 64, 91)
MESH = pl.DeviceIdType.MESH
BF = jnp.bfloat16
F32 = jnp.float32
LANES = 128
ANY = pl.BlockSpec(memory_space=pl.ANY)
VMEM = pl.BlockSpec(memory_space=pltpu.VMEM)


def bucket_of(relative):
    distance = jnp.abs(relative)
    bucket_level = jnp.full(relative.shape, 8, jnp.int32)
    for boundary in THRESHOLDS:
        bucket_level = bucket_level + (distance >= boundary).astype(jnp.int32)
    near_bucket = jnp.where(distance < 8, distance, bucket_level)
    return near_bucket + 16 * (relative > 0).astype(jnp.int32)


def dot(left_mat, right_mat):
    return jnp.dot(left_mat, right_mat, preferred_element_type=F32)


def dot_rows(left_mat, right_mat):
    return lax.dot_general(
        left_mat, right_mat, (((0,), (0,)), ((), ())), preferred_element_type=F32
    )


def dot_cols(left_mat, right_mat):
    return lax.dot_general(
        left_mat, right_mat, (((1,), (1,)), ((), ())), preferred_element_type=F32
    )


def ring_place(index, count):
    odd = index % 2
    return (1 - odd) * (index // 2) + odd * ((2 * count - 1 - index) // 2)


def ring_index(place, count):
    late = place // (count // 2)
    return (1 - late) * 2 * place + late * (2 * count - 1 - 2 * place)


def greet(targets):
    barrier = pltpu.get_barrier_semaphore()
    for target in targets:
        pl.semaphore_signal(barrier, inc=1, device_id=target, device_id_type=MESH)
    return lambda: pl.semaphore_wait(barrier, len(targets))


def comm_params(collective_id, vmem=None):
    return pltpu.CompilerParams(
        collective_id=collective_id, has_side_effects=True, vmem_limit_bytes=vmem
    )


class Spot:
    def __init__(self, count):
        self.count = count
        self.half = count // 2
        self.me = lax.axis_index("seq")
        self.dp = lax.axis_index("dp")
        self.place = ring_place(self.me, count)
        self.nexts = tuple((self.dp, self.at(step)) for step in (1, -1))
        self.far_dp = (self.dp + 2) % 4
        self.twin_dp = self.dp + 1 - 2 * (self.dp % 2)
        self.far = (self.far_dp, self.me)
        self.twin = (self.twin_dp, self.me)
        self.others = tuple((self.dp, (self.me + step) % count) for step in range(1, count))

    def at(self, step):
        return ring_index((self.place + (step + self.count) % self.count) % self.count, self.count)

    def back(self, way, hop):
        return self.at(-hop if way == 0 else hop)


def push(source, target, send_sem, recv_sem, device, split=1):
    def copy_of(source, target):
        return pltpu.make_async_remote_copy(
            src_ref=source,
            dst_ref=target,
            send_sem=send_sem,
            recv_sem=recv_sem,
            device_id=device,
            device_id_type=MESH,
        )

    whole = copy_of(source, target)
    if split == 1:
        whole.start()
        return whole
    rows = source.shape[0] // split
    for index in range(split):
        window = pl.ds(index * rows, rows)
        copy_of(source.at[window], target.at[window]).start()
    return whole


def wait_all(like, sem):
    pltpu.make_async_copy(like, like, sem).wait()


class RingGather:
    def __init__(self, spot, own, blocks, send_sem, recv_sems, split=1):
        self.spot, self.own, self.blocks, self.split = spot, own, blocks, split
        self.send_sem, self.recv_sems = send_sem, recv_sems
        self.rows = blocks.shape[1] // 2
        self.copies = {}

    def into(self, origin, piece):
        return self.blocks.at[origin, pl.ds(piece * self.rows, self.rows)]

    def pieces(self, way, hop):
        return (0, 1) if hop < self.spot.half - 1 else (way,)

    def forward(self, hop, way, piece):
        spot = self.spot
        if hop >= spot.half or piece not in self.pieces(way, hop):
            return
        origin = spot.back(way, hop)
        target = self.into(origin, piece)
        self.copies[hop, way, piece] = push(
            self.own.at[pl.ds(piece * self.rows, self.rows)] if hop == 0 else target,
            target,
            self.send_sem,
            self.recv_sems.at[way, hop, piece],
            spot.nexts[way],
            self.split,
        )

    def begin(self, piece):
        for way in range(2):
            self.forward(0, way, piece)

    def step(self, hop):
        for piece in range(2):
            for way in range(2):
                if (hop, way, piece) in self.copies:
                    self.copies[hop, way, piece].wait_recv()
                    self.forward(hop + 1, way, piece)

    def finish(self):
        wait_all(self.blocks.at[pl.ds(0, self.spot.count - 1)], self.send_sem)


class RingSum:
    def __init__(self, spot, terms, buf, send_sem, recv_sems):
        self.spot, self.terms, self.buf = spot, terms, buf
        self.send_sem, self.recv_sems = send_sem, recv_sems
        self.rows = terms.shape[1] // 2
        self.copies = {}

    def term(self, block, piece):
        return self.terms.at[block, pl.ds(piece * self.rows, self.rows)]

    def send(self, hop, way, piece, source):
        self.copies[hop, way, piece] = push(
            source,
            self.buf.at[way, hop, piece],
            self.send_sem,
            self.recv_sems.at[way, hop, piece],
            self.spot.nexts[way],
        )

    def block(self, way, hop):
        step = self.spot.half - hop
        return self.spot.at(step if way == 0 else -step)

    def begin(self):
        for way in range(2):
            self.send(0, way, way, self.term(self.block(way, 0), way))
        for way in range(2):
            self.send(1, way, 1 - way, self.term(self.block(way, 1), 1 - way))

    def step(self, hop):
        for piece in range(2):
            for way in range(2):
                if (hop, way, piece) not in self.copies or hop + 1 >= self.spot.half:
                    continue
                self.copies[hop, way, piece].wait_recv()
                term = self.term(self.block(way, hop + 1), piece)
                self.buf[way, hop, piece] = (
                    self.buf[way, hop, piece].astype(F32) + term[...].astype(F32)
                ).astype(BF)
                self.send(hop + 1, way, piece, self.buf.at[way, hop, piece])

    def total(self, out):
        last = self.spot.half - 1
        for piece in range(2):
            value = self.term(self.spot.me, piece)[...].astype(F32)
            for way in range(2):
                self.copies[last, way, piece].wait_recv()
                value = value + self.buf[way, last, piece].astype(F32)
            out[pl.ds(piece * self.rows, self.rows)] = value.astype(BF)

    def finish(self):
        wait_all(self.terms.at[pl.ds(0, self.spot.count - 1)], self.send_sem)


class PairGather:
    def __init__(self, spot, own_ref, buf, send_sems, recv_sems):
        self.spot, self.buf = spot, buf
        self.send_sems, self.recv_sems = send_sems, recv_sems
        rows = own_ref.shape[0]
        self.low, self.high = pl.ds(0, rows), pl.ds(rows, rows)
        self.far = self.push(1, own_ref, buf.at[1, self.low], spot.far)
        self.near = self.push(0, own_ref, buf.at[0, self.high], spot.twin)

    def push(self, index, source, target, device):
        return push(source, target, self.send_sems.at[index], self.recv_sems.at[index], device)

    def relay(self):
        self.far.wait_recv()
        self.cross = self.push(
            2, self.buf.at[1, self.low], self.buf.at[1, self.high], self.spot.twin
        )

    def finish(self):
        for copy in (self.near, self.far, self.cross):
            copy.wait_send()


class PairSum:
    def __init__(self, spot, kept, outs, ins, far_out, far_in, send_sems, recv_sems):
        self.spot, self.kept, self.outs, self.ins = spot, kept, outs, ins
        self.far_out, self.far_in = far_out, far_in
        self.send_sems, self.recv_sems = send_sems, recv_sems
        self.copies = []

    def near(self, half):
        self.copies.append(
            push(
                self.outs.at[half], self.ins.at[half],
                self.send_sems.at[half], self.recv_sems.at[half], self.spot.twin,
            )
        )

    def over(self):
        self.copies[1].wait_recv()
        self.far_out[...] = (self.kept[1] + self.ins[1].astype(F32)).astype(BF)
        self.copies.append(
            push(
                self.far_out, self.far_in, self.send_sems.at[2], self.recv_sems.at[2], self.spot.far
            )
        )

    def total(self):
        self.copies[0].wait_recv()
        self.copies[2].wait_recv()
        return self.kept[0] + self.ins[0].astype(F32) + self.far_in[...].astype(F32)

    def finish(self):
        for copy in self.copies:
            copy.wait_send()


class MeshGather:
    def __init__(self, spot, x_ref, o_ref, share, sems):
        self.spot, self.x_ref, self.o_ref = spot, x_ref, o_ref
        self.ring_s, self.ring_r, self.x_s, self.far_r, self.own_r, self.core_s, self.core_r = sems
        rows = x_ref.shape[0]
        first = rows * share // 100 // 32 * 32
        cuts = (0, first // 2, first, first + (rows - first) // 2 // 16 * 16, rows)
        self.parts = (pl.ds(0, first), pl.ds(first, rows - first))
        self.windows = [
            [pl.ds(cuts[2 * part + piece], cuts[2 * part + piece + 1] - cuts[2 * part + piece]) for piece in range(2)]
            for part in range(2)
        ]
        self.ring, self.x = {}, {}

    def into(self, dp, origin, part, piece):
        return self.o_ref.at[dp, origin, self.windows[part][piece]]

    def pieces(self, way, hop):
        return (0, 1) if hop < self.spot.half - 1 else (way,)

    def to_core(self, source, target):
        push(source, target, self.core_s, self.core_r, self.spot.twin)

    def pass_on(self, part, lane, hop, way, piece, source):
        spot = self.spot
        dp = spot.far_dp if lane else spot.dp
        origin = spot.me if way is None else spot.back(way, hop)
        target = self.into(dp, origin, part, piece)
        source = target if source is None else source
        slot = 0 if way is None else 2 * hop - 1 + way
        for onward in (0, 1) if way is None else (way,):
            if hop < spot.half and piece in self.pieces(onward, hop):
                self.ring[part, lane, hop, onward, piece] = push(
                    source, target,
                    self.ring_s.at[part + lane],
                    self.ring_r.at[2 * (part + lane) + onward, hop, piece],
                    spot.nexts[onward],
                )
        if part == 0:
            self.x[part, slot, piece] = push(
                source, target, self.x_s.at[0], self.far_r.at[slot, piece], spot.far
            )
        self.to_core(source, target)

    def begin(self):
        spot = self.spot
        for piece in range(2):
            self.x[1, 0, piece] = push(
                self.x_ref.at[self.windows[1][piece]],
                self.into(spot.dp, spot.me, 1, piece),
                self.x_s.at[1], self.own_r.at[piece], spot.far,
            )
        for part in range(2):
            for piece in range(2):
                self.pass_on(part, 0, 0, None, piece, self.x_ref.at[self.windows[part][piece]])

    def begin_far(self):
        for piece in range(2):
            self.x[1, 0, piece].wait_recv()
            self.pass_on(1, 1, 0, None, piece, None)

    def step(self, hop):
        for piece in range(2):
            for part, lane in ((0, 0), (1, 0), (1, 1)):
                for way in range(2):
                    key = (part, lane, hop, way, piece)
                    if key in self.ring:
                        self.ring[key].wait_recv()
                        self.pass_on(part, lane, hop + 1, way, piece, None)

    def step_far(self, hop):
        spot = self.spot
        for piece in range(2):
            for way in (None,) if hop == 0 else range(2):
                slot = 0 if way is None else 2 * hop - 1 + way
                if (0, slot, piece) in self.x:
                    self.x[0, slot, piece].wait_recv()
                    origin = spot.me if way is None else spot.back(way, hop)
                    target = self.into(spot.far_dp, origin, 0, piece)
                    self.to_core(target, target)

    def finish(self):
        o_ref, count = self.o_ref, self.spot.count
        wait_all(o_ref.at[pl.ds(0, 2)], self.core_r)
        wait_all(o_ref.at[pl.ds(0, 2)], self.core_s)
        for index in range(3):
            wait_all(o_ref.at[0, pl.ds(0, count - 1), self.parts[min(index, 1)]], self.ring_s.at[index])
        wait_all(o_ref.at[0, :, self.parts[0]], self.x_s.at[0])
        wait_all(self.x_ref.at[self.parts[1]], self.x_s.at[1])


def mesh_sems(count):
    half = count // 2
    dma = pltpu.SemaphoreType.DMA
    return [
        dma((3,)), dma((6, half, 2)), dma((2,)), dma((2 * half + 1, 2)), dma((2,)), dma(()), dma(())
    ]


def near_buckets(rows):
    shape = (rows, rows + 2 * LANES)
    column = lax.broadcasted_iota(jnp.int32, shape, 1) - LANES
    return bucket_of(column - lax.broadcasted_iota(jnp.int32, shape, 0))


def strip_window(step, rows, length):
    return pl.ds(pl.multiple_of(length - rows - step * rows, LANES), length)


def scale_of(value):
    return lax.rsqrt(jnp.mean(value * value, axis=-1, keepdims=True) + EPSILON)


def row_block(origin, rows):
    return pl.ds(pl.multiple_of(origin * rows, rows), rows)


def exclusive(index, bit):
    return index + bit - 2 * bit * ((index // bit) % 2)


def layer_body(count, heads, depth, ff, names, *refs):
    r = types.SimpleNamespace(**dict(zip(names, refs)))
    spot = Spot(count)
    hidden_ref, grad_ref = r.hidden, r.out_grad
    rows, width = hidden_ref.shape
    length = count * rows
    inner = heads * depth
    span = r.gate_w.shape[1]
    odd = spot.dp % 2
    ff_start = pl.multiple_of(spot.dp * ff - odd * (span - ff), span - ff)
    own_columns = pl.ds(pl.multiple_of(spot.me * LANES, LANES), LANES)
    all_in = greet(spot.nexts + (spot.far, spot.twin))

    loads = {}

    def load(name, source, target):
        copy = pltpu.make_async_copy(source, target, r.load_sems.at[len(loads)])
        copy.start()
        loads[name] = copy

    ring = RingGather(
        spot,
        hidden_ref,
        r.row,
        r.row_s,
        r.row_r,
    )
    sources = (r.query_weight, r.key_weight, r.value_weight)
    for part, source in enumerate(sources):
        load(
            part,
            source.at[:, pl.ds(pl.multiple_of(spot.me * inner, inner), inner)],
            r.qkv_w.at[:, pl.ds(part * inner, inner)],
        )
    load("out", r.out_weight, r.out_w)
    ff_columns = pl.ds(pl.multiple_of(ff_start, LANES), span)
    load("gate", r.gate_weight.at[:, ff_columns], r.gate_w)
    load("up", r.up_weight.at[:, ff_columns], r.up_w)
    load("down", r.down_weight.at[pl.ds(ff_start, span)], r.down_w)
    for part, source in enumerate(sources):
        load(3 + part, source, r.full_w.at[part])

    qkv, normed, weights = r.qkv, r.normed, r.weights
    both_rows = 2 * rows
    low = length - rows - LANES
    bucket = near_buckets(rows)
    near_span = bucket.shape[1]
    score_strip = r.score_strip
    strip = score_strip.at[:, pl.ds(0, rows)]
    score_low = length - both_rows - LANES
    score_bucket = near_buckets(both_rows)
    score_span = score_bucket.shape[1]
    head_count, level_count = r.table.shape
    chosen = lax.broadcasted_iota(jnp.int32, (8, head_count), 1) == (
        spot.me * heads + lax.broadcasted_iota(jnp.int32, (8, head_count), 0)
    )
    table = dot(chosen.astype(BF), r.table[...])
    for head in range(heads):
        entry = lambda level: table[head : head + 1, level : level + 1]
        value = jnp.zeros(score_bucket.shape, F32)
        for level in range(level_count):
            value = jnp.where(score_bucket == level, entry(level), value)
        after = score_strip.shape[2] - score_low - score_span
        score_strip[head, :, :score_low] = jnp.broadcast_to(entry(15), (both_rows, score_low))
        score_strip[head, :, score_low : score_low + score_span] = value
        score_strip[head, :, score_low + score_span :] = jnp.broadcast_to(
            entry(31), (both_rows, after)
        )
        if head == 0:
            all_in()
            ring.begin(0)
    ring.begin(1)
    cots = PairGather(spot, grad_ref, r.cot, r.cot_s, r.cot_r)
    gain_one = r.gain_one[...].astype(F32).reshape(1, width)
    gain_two = r.gain_two[...].astype(F32).reshape(1, width)

    def project(origin, block):
        value = block.astype(F32)
        low_value = (value * scale_of(value) * gain_one).astype(BF)
        mine = row_block(origin, rows)
        normed[mine] = low_value
        qkv[mine] = dot(low_value, r.qkv_w[...]).astype(BF)

    for part in range(3):
        loads[part].wait()
    project(spot.me, hidden_ref[...])
    for hop in range(spot.half):
        ring.step(hop)
        if hop < spot.half - 1:

            def both(side, carry, hop=hop):
                origin = spot.at((1 - 2 * side) * (hop + 1))
                project(origin, r.row[origin])
                return carry

            lax.fori_loop(0, 2, both, 0)
        else:
            origin = spot.at(spot.half)
            project(origin, r.row[origin])
    ring.finish()
    cots.relay()
    r.cot[0, :rows] = grad_ref[...]
    mixed_heads, mixed = r.mixed_heads, r.mixed

    def attend(block):
        mine = row_block(block, both_rows)
        turned_ids = jnp.broadcast_to(r.row_ids[:, mine], (LANES, both_rows)).T
        same = turned_ids[:, :1] == r.row_ids[...]
        window = strip_window(block, both_rows, length)
        for head in range(heads):
            columns = slice(head * depth, (head + 1) * depth)
            key = qkv[:, inner + head * depth : inner + (head + 1) * depth]
            value = qkv[:, 2 * inner + head * depth : 2 * inner + (head + 1) * depth]
            scores = dot_cols(qkv[mine, columns], key) + score_strip[head, :, window]
            scores = jnp.where(same, scores, MASKED)
            top = jnp.max(scores, axis=1, keepdims=True)
            weight = jnp.exp(scores - top)
            share = 1.0 / jnp.sum(weight, axis=1, keepdims=True)
            r.shares[head, mine] = share
            weight = weight.astype(BF)
            weights[head, mine] = weight
            mixed_heads[mine, columns] = (dot(weight, value) * share).astype(BF)

    def mixed_send(target):
        push(
            mixed_heads.at[row_block(target, rows)],
            mixed.at[:, own_columns],
            r.mixed_s,
            r.mixed_r,
            (spot.dp, target),
        )

    def attend_and_send(step, carry):
        block = (spot.me // 2 + step) % (count // 2)
        attend(block)
        for index in range(2):
            mixed_send(2 * block + index)
        return carry

    lax.fori_loop(1, count // 2, attend_and_send, 0)
    attend(spot.me // 2)
    mixed_send(exclusive(spot.me, 1))
    mixed[:, own_columns] = mixed_heads[row_block(spot.me, rows)]

    loads["out"].wait()
    wait_all(mixed.at[:, pl.ds(0, width - LANES)], r.mixed_r)
    inputs = hidden_ref[...].astype(F32)
    middle_ref = r.middle
    middle = inputs + dot(mixed[...], r.out_w[...])
    middle_ref[...] = middle
    tok, cot = r.tok, r.cot
    tok[0, :rows] = (middle * scale_of(middle) * gain_two).astype(BF)
    toks = PairGather(spot, tok.at[0, pl.ds(0, rows)], tok, r.tok_s, r.tok_r)
    gate_w, up_w, down_w = r.gate_w, r.up_w, r.down_w
    act, gate_g, up_g = r.act, r.gate_g, r.up_g
    for name in ("gate", "up", "down"):
        loads[name].wait()
    chunk = 256
    grads = PairSum(
        spot, r.grad_kept, r.grad_outs, r.grad_ins, r.grad_far_out, r.grad_far_in,
        r.grad_s, r.grad_r,
    )
    outs = PairSum(
        spot, r.out_kept, r.out_outs, r.out_ins, r.out_far_out, r.out_far_in,
        r.out_s, r.out_r,
    )

    def activate_half(half):
        mine = pl.ds(half * both_rows, both_rows)

        def tile(index, carry):
            columns = row_block(index, chunk)
            gate = dot(tok[half], gate_w[:, columns])
            up = dot(tok[half], up_w[:, columns])
            act_grad = dot_cols(cot[half], down_w[columns])
            place = index * chunk + lax.broadcasted_iota(jnp.int32, (1, chunk), 1)
            place = place - odd * (span - ff)
            inside = (place >= 0) & (place < ff)
            root = 0.7978845608028654
            squared = gate * gate
            bend = jnp.tanh(root * (gate + 0.044715 * gate * squared))
            share = 0.5 * (1.0 + bend)
            gelu = gate * share
            slope = share + 0.5 * gate * (1.0 - bend * bend) * root * (
                1.0 + 3 * 0.044715 * squared
            )
            act[mine, columns] = jnp.where(inside, gelu * up, 0.0).astype(BF)
            gate_g[mine, columns] = jnp.where(inside, act_grad * up * slope, 0.0).astype(BF)
            up_g[mine, columns] = jnp.where(inside, act_grad * gelu, 0.0).astype(BF)
            return carry

        lax.fori_loop(0, span // chunk, tile, 0)

    def spread(pair_sum, half, product):
        def tile(index, carry):
            columns = row_block(index, chunk)
            value = product(columns)
            pair_sum.kept[half, :, columns] = value[:rows]
            pair_sum.outs[half, :, columns] = value[rows:].astype(BF)
            return carry

        lax.fori_loop(0, width // chunk, tile, 0)
        pair_sum.near(half)

    def back_half(half):
        mine = pl.ds(half * both_rows, both_rows)
        spread(
            grads,
            half,
            lambda columns: dot_cols(gate_g[mine], gate_w[columns])
            + dot_cols(up_g[mine], up_w[columns]),
        )

    def out_half(half):
        mine = pl.ds(half * both_rows, both_rows)
        spread(outs, half, lambda columns: dot(act[mine], down_w[:, columns]))

    cots.near.wait_recv()
    cots.cross.wait_recv()
    toks.near.wait_recv()
    activate_half(0)
    toks.relay()
    back_half(0)
    toks.cross.wait_recv()
    activate_half(1)

    down_terms, pair_terms = r.down_terms, r.pair_terms
    spare = span - ff

    def down_tile(index, carry):
        columns = row_block(index, LANES)
        value = dot_rows(act[:both_rows], cot[0, :, columns]) + dot_rows(
            act[both_rows:], cot[1, :, columns]
        )
        down_terms[index] = jnp.where(odd == 1, value[spare:], value[:ff]).astype(BF)
        return carry

    down_sum = RingSum(spot, down_terms, r.down_buf, r.down_s, r.down_r)

    def down_ready():
        lax.fori_loop(0, count, down_tile, 0)
        down_sum.begin()

    full = ff // LANES
    lane = lax.broadcasted_iota(jnp.int32, (LANES, LANES), 1)

    def pair_tile(index, carry):
        columns = row_block(index, LANES)
        parts = []
        for source in (gate_g, up_g):
            parts.append(
                dot_rows(tok[0, :, columns], source[:both_rows])
                + dot_rows(tok[1, :, columns], source[both_rows:])
            )
        cut = lambda value, place: value[:, place * LANES : (place + 1) * LANES]
        for part, value in enumerate(parts):
            for place in range(full):
                start = (part * full + place) * LANES
                pair_terms[index, start : start + LANES] = jnp.where(
                    odd == 1, cut(value, place + 1), cut(value, place)
                ).astype(BF)
        edges = [jnp.where(odd == 1, cut(value, 0), cut(value, full)) for value in parts]
        turned = pltpu.roll(edges[1], LANES // 2, 1)
        lower = (lane < LANES // 2).astype(jnp.int32)
        pair_terms[index, 2 * full * LANES :] = jnp.where(lower == odd, turned, edges[0]).astype(BF)
        return carry

    pair_sum = RingSum(spot, pair_terms, r.pair_buf, r.pair_s, r.pair_r)

    def pair_ready():
        lax.fori_loop(0, count, pair_tile, 0)
        pair_sum.begin()

    small, middle_grad_ref, own_branch = r.small, r.middle_grad, r.own_branch
    tiles = width // LANES

    def finish_middle():
        normed_two_grad = grads.total()
        middle = middle_ref[...]
        scale_two = scale_of(middle)
        lifted = gain_two * normed_two_grad
        middle_grad = (
            grad_ref[...].astype(F32)
            + scale_two * lifted
            - middle * (scale_two * scale_two * scale_two)
            * jnp.mean(middle * lifted, axis=-1, keepdims=True)
        )
        middle_grad_ref[...] = middle_grad
        own_branch[...] = middle_grad.astype(BF)
        small[...] = jnp.zeros_like(small)
        gain_grad = jnp.sum(normed_two_grad * middle * scale_two, axis=0, keepdims=True)
        for tile in range(tiles):
            small[tiles + tile : tiles + tile + 1] = gain_grad[:, tile * LANES : (tile + 1) * LANES]

    def finish_out():
        r.block_out[...] = (middle_ref[...] + outs.total()).astype(BF)

    branch = r.row
    branches = RingGather(
        spot,
        own_branch,
        branch,
        r.branch_s,
        r.branch_r,
        SPLITS[0],
    )
    keys, values, dqkv, packed = r.keys, r.values, r.dqkv, r.packed

    own_out = r.out_w.at[row_block(spot.me, inner)]
    quarter, slim = width // 4, inner // 4

    def attend_back(origin):
        mine = row_block(origin, rows)
        window = strip_window(origin, rows, length)
        mixed_grad = dot_cols(branch[origin], own_out[...])
        for head in range(heads):
            columns = slice(head * depth, (head + 1) * depth)
            key = qkv[:, inner + head * depth : inner + (head + 1) * depth]
            value = qkv[:, 2 * inner + head * depth : 2 * inner + (head + 1) * depth]
            share = r.shares[head, mine]
            grad = (mixed_grad[:, columns] * share).astype(BF)
            weight_low = weights[head, mine]
            weight = weight_low.astype(F32)
            scaled = weight * dot_cols(grad, value)
            score_grad = scaled - weight * (share * jnp.sum(scaled, axis=1, keepdims=True))
            strip[head, :, window] += score_grad
            score_low = score_grad.astype(BF)
            dqkv[mine, columns] = dot(score_low, key).astype(BF)
            keys[:, columns] += dot_rows(score_low, qkv[mine, columns])
            values[:, columns] += dot_rows(weight_low, grad)
        terms = dot_rows(mixed_heads[mine], branch[origin])
        for tile in range(tiles):
            for index in range(4):
                base = 3 * quarter + tile * slim
                packed[index, base : base + slim] += terms[
                    index * slim : (index + 1) * slim, tile * LANES : (tile + 1) * LANES
                ]
        terms = dot_rows(normed[mine], dqkv[mine, :inner])
        for index in range(4):
            packed[index, :quarter] += terms[index * quarter : (index + 1) * quarter]

    mesh_sets = [r.gather_sems[7 * index : 7 * index + 7] for index in range(3)]
    down = MeshGather(spot, r.down_block, r.down_all, SHARES[0], mesh_sets[0])
    pair = MeshGather(spot, r.pair_block, r.pair_all, SHARES[1], mesh_sets[1])
    proj = MeshGather(spot, r.proj_block, r.proj_all, SHARES[2], mesh_sets[2])
    core, side = odd, spot.dp // 2
    own_dqkv = r.own_dqkv

    def branch_start():
        branches.begin(0)
        branch[spot.me] = own_branch[...]
        strip[...] = jnp.zeros_like(strip)
        keys[...] = jnp.zeros_like(keys)
        values[...] = jnp.zeros_like(values)
        branches.begin(1)
        packed[...] = jnp.zeros_like(packed)
        attend_back(spot.me)

    def finish_down():
        down_sum.total(r.down_block)
        down.begin()
        load("down_own", r.down_block, r.down_all.at[spot.dp, spot.me])

    def finish_pair():
        pair_sum.total(r.pair_block)
        pair.begin()
        load("pair_own", r.pair_block, r.pair_all.at[spot.dp, spot.me])

    def attend_pair(hop):
        def both_back(index, carry):
            attend_back(spot.at((1 - 2 * index) * (hop + 1)))
            return carry

        lax.fori_loop(0, 2, both_back, 0)

    def finish_heads():
        dqkv[:, inner : 2 * inner] = keys[...].astype(BF)
        dqkv[:, 2 * inner :] = values[...].astype(BF)

        def quarter_block(index, carry):
            block = dot_rows(normed[:, row_block(index, quarter)], dqkv[:, inner:])
            for part in range(2):
                packed[index, (part + 1) * quarter : (part + 2) * quarter] = block[
                    :, part * LANES : (part + 1) * LANES
                ]
            return carry

        lax.fori_loop(0, 4, quarter_block, 0)
        for index in range(2):
            r.near_out[index] = packed[2 * index + 1 - core].astype(BF)
        return push(r.near_out, r.near_in, r.proj_s.at[0], r.proj_r.at[0], spot.twin)

    def heads_over():
        near.wait_recv()
        r.far_out[...] = (
            packed[2 * (1 - side) + core] + r.near_in[1 - side].astype(F32)
        ).astype(BF)
        return push(r.far_out, r.far_in, r.proj_s.at[1], r.proj_r.at[1], spot.far, SPLITS[1])

    def finish_proj():
        far.wait_recv()
        r.proj_block[...] = (
            packed[2 * side + core] + r.near_in[side].astype(F32) + r.far_in[...].astype(F32)
        ).astype(BF)
        proj.begin()
        load("proj_own", r.proj_block, r.proj_all.at[spot.dp, spot.me])

    def trade():
        for device in spot.others:
            for part in range(3):
                push(
                    dqkv.at[row_block(device[1], rows), pl.ds(part * LANES, LANES)],
                    own_dqkv.at[part, :, own_columns],
                    r.trade_s,
                    r.trade_r,
                    device,
                )
        for part in range(3):
            own_dqkv[part, :, own_columns] = dqkv[
                row_block(spot.me, rows), part * LANES : (part + 1) * LANES
            ]

    def finish_table():
        for head in range(heads):
            middle_part = strip[head, :, low : low + near_span]
            before = jnp.sum(strip[head, :, :low], axis=0, keepdims=True)
            after = jnp.sum(strip[head, :, low + near_span :], axis=0, keepdims=True)
            levels = []
            for level in range(level_count):
                part = jnp.sum(jnp.where(bucket == level, middle_part, 0.0), axis=0, keepdims=True)
                line = part[:, :LANES]
                for tile in range(1, near_span // LANES):
                    line = line + part[:, tile * LANES : (tile + 1) * LANES]
                edge = before if level == 15 else after if level == 31 else None
                if edge is not None:
                    for tile in range(edge.shape[1] // LANES):
                        line = line + edge[:, tile * LANES : (tile + 1) * LANES]
                r.levels[level : level + 1] = line
            sums = lax.dot_general(
                jnp.ones((8, LANES), F32),
                r.levels[...],
                (((1,), (1,)), ((), ())),
                precision=lax.Precision.HIGHEST,
                preferred_element_type=F32,
            )
            small[pl.ds(2 * tiles + spot.me * heads + head, 1), : level_count] = sums[:1]

    def finish_input():
        for part in range(3):
            loads[3 + part].wait()
        wait_all(own_dqkv.at[:, :, pl.ds(0, width - LANES)], r.trade_r)
        normed_grad = dot_cols(own_dqkv[0], r.full_w[0])
        for part in range(1, 3):
            normed_grad = normed_grad + dot_cols(own_dqkv[part], r.full_w[part])
        inputs = hidden_ref[...].astype(F32)
        scale_one = scale_of(inputs)
        raised = gain_one * normed_grad
        r.hidden_grad[...] = (
            middle_grad_ref[...]
            + scale_one * raised
            - inputs * (scale_one * scale_one * scale_one)
            * jnp.mean(inputs * raised, axis=-1, keepdims=True)
        )
        gain_grad = jnp.sum(normed_grad * inputs * scale_one, axis=0, keepdims=True)
        for tile in range(tiles):
            small[tile : tile + 1] = gain_grad[:, tile * LANES : (tile + 1) * LANES]

    partners = [spot.twin, spot.far]
    bit = 1
    while bit < count:
        partners.append((spot.dp, exclusive(spot.me, bit)))
        bit *= 2
    small_out, small_in = r.small_out, r.small_in
    small_copies = []

    def small_send():
        index = len(small_copies)
        if index < len(partners):
            small_out[index] = small[...]
            small_copies.append(
                push(
                    small_out.at[index], small_in.at[index],
                    r.small_s.at[index], r.small_r.at[index], partners[index],
                )
            )

    def small_step():
        if len(small_copies) <= len(partners) and small_copies:
            index = len(small_copies) - 1
            small_copies[index].wait_recv()
            small[...] += small_in[index]
            small_send()

    def pass_round(gather, hop):
        gather.step(hop)
        gather.step_far(hop)

    down_ready()
    pair_ready()
    back_half(1)
    down_sum.step(0)
    grads.over()
    out_half(0)
    down_sum.step(1)
    finish_middle()
    branch_start()
    down_sum.step(2)
    branches.step(0)
    attend_pair(0)
    branches.step(1)
    attend_pair(1)
    pair_sum.step(0)
    finish_down()
    down.begin_far()
    down.step(0)
    branches.step(2)
    attend_pair(2)
    down.step(1)
    pair_sum.step(1)
    down.step_far(0)
    out_half(1)
    branches.step(3)
    attend_back(spot.at(spot.half))
    near = finish_heads()
    far = heads_over()
    outs.over()
    down.step(2)
    trade()
    finish_table()
    pair_sum.step(2)
    finish_proj()
    down.step_far(1)
    down.step_far(2)
    finish_pair()
    down.step_far(3)
    finish_input()
    down.step(3)
    proj.begin_far()
    small_send()
    small_step()
    proj.step(0)
    pair.begin_far()
    proj.step(1)
    small_step()
    pair.step(0)
    proj.step_far(0)
    down.step_far(4)
    proj.step(2)
    pair.step(1)
    small_step()
    pair.step_far(0)
    proj.step(3)
    pair.step(2)
    small_step()
    proj.step_far(1)
    proj.step_far(2)
    pair.step(3)
    pair.step_far(1)
    pair.step_far(2)
    proj.step_far(3)
    finish_out()
    proj.step_far(4)
    pair.step_far(3)
    pair.step_far(4)
    small_step()
    r.small_sum[...] = small[...]
    for name in ("down_own", "pair_own", "proj_own"):
        loads[name].wait()
    wait_all(mixed_heads.at[pl.ds(0, length - rows)], r.mixed_s)
    wait_all(dqkv.at[pl.ds(0, length - rows)], r.trade_s)
    for copy in [near, far] + small_copies:
        copy.wait_send()
    for item in (cots, toks, grads, outs, down_sum, pair_sum, branches, down, pair, proj):
        item.finish()


SHARES = (95, 40, 90)
SPLITS = (1, 1)


def layer(arrays, count, heads, depth, ff):
    rows, width = arrays["hidden"].shape
    length = count * rows
    inner = heads * depth
    half = count // 2
    span = (ff + LANES - 1) // LANES * LANES
    pair_rows = 2 * ff // LANES * rows
    proj_rows = 3 * (width // 4) + inner // 4 * (width // LANES)
    small_rows = 2 * (width // LANES) + count * heads
    steps = 2 + (count - 1).bit_length()
    dma = pltpu.SemaphoreType.DMA
    specs = dict(
        hidden=VMEM,
        out_grad=VMEM,
        gain_one=VMEM,
        gain_two=VMEM,
        row_ids=VMEM,
        table=VMEM,
    )
    shape = jax.ShapeDtypeStruct
    results = dict(
        block_out=(shape((rows, width), BF), VMEM),
        hidden_grad=(shape((rows, width), F32), VMEM),
        small_sum=(shape((small_rows, LANES), F32), VMEM),
        down_all=(shape((4, count, ff, LANES), BF), ANY),
        pair_all=(shape((4, count, pair_rows, LANES), BF), ANY),
        proj_all=(shape((4, count, proj_rows, LANES), BF), ANY),
    )
    vm = pltpu.VMEM
    ring_buf = lambda n: vm((2, half, 2, n // 2, LANES), BF)
    pairs = {}
    for name in ("grad", "out"):
        pairs[name + "_kept"] = vm((2, rows, width), F32)
        pairs[name + "_outs"] = vm((2, rows, width), BF)
        pairs[name + "_ins"] = vm((2, rows, width), BF)
        pairs[name + "_far_out"] = vm((rows, width), BF)
        pairs[name + "_far_in"] = vm((rows, width), BF)
        pairs[name + "_s"] = dma((3,))
        pairs[name + "_r"] = dma((3,))
    for name in ("cot", "tok"):
        pairs[name] = vm((2, 2 * rows, width), BF)
        pairs[name + "_s"] = dma((3,))
        pairs[name + "_r"] = dma((3,))
    pairs["row"] = vm((count, rows, width), BF)
    for name in ("row", "branch"):
        pairs[name + "_s"] = dma(())
        pairs[name + "_r"] = dma((2, half, 2))
    for name, size in (("down", ff), ("pair", pair_rows)):
        pairs[name + "_terms"] = vm((count, size, LANES), BF)
        pairs[name + "_buf"] = ring_buf(size)
        pairs[name + "_block"] = vm((size, LANES), BF)
        pairs[name + "_s"] = dma(())
        pairs[name + "_r"] = dma((2, half, 2))
    scratch = dict(
        **pairs,
        score_strip=vm((heads, 2 * rows, 2 * length - rows), F32),
        normed=vm((length, width), BF),
        qkv=vm((length, 3 * inner), BF),
        weights=vm((heads, length, length), BF),
        shares=vm((heads, length, 1), F32),
        mixed_heads=vm((length, inner), BF),
        mixed=vm((rows, width), BF),
        qkv_w=vm((width, 3 * inner), BF),
        full_w=vm((3, width, width), BF),
        out_w=vm((width, width), BF),
        gate_w=vm((width, span), BF),
        up_w=vm((width, span), BF),
        down_w=vm((span, width), BF),
        middle=vm((rows, width), F32),
        middle_grad=vm((rows, width), F32),
        act=vm((4 * rows, span), BF),
        gate_g=vm((4 * rows, span), BF),
        up_g=vm((4 * rows, span), BF),
        own_branch=vm((rows, width), BF),
        keys=vm((length, inner), F32),
        values=vm((length, inner), F32),
        dqkv=vm((length, 3 * inner), BF),
        own_dqkv=vm((3, rows, width), BF),
        packed=vm((4, proj_rows, LANES), F32),
        near_out=vm((2, proj_rows, LANES), BF),
        near_in=vm((2, proj_rows, LANES), BF),
        far_out=vm((proj_rows, LANES), BF),
        far_in=vm((proj_rows, LANES), BF),
        proj_block=vm((proj_rows, LANES), BF),
        levels=vm((arrays["table"].shape[1], LANES), F32),
        small=vm((small_rows, LANES), F32),
        small_out=vm((steps, small_rows, LANES), F32),
        small_in=vm((steps, small_rows, LANES), F32),
        load_sems=dma((16,)),
        mixed_s=dma(()),
        mixed_r=dma(()),
        trade_s=dma(()),
        trade_r=dma(()),
        proj_s=dma((2,)),
        proj_r=dma((2,)),
        small_s=dma((steps,)),
        small_r=dma((steps,)),
    )
    names = tuple(arrays) + tuple(results) + tuple(scratch)

    def body(*refs):
        plain = refs[: len(names)]
        layer_body(
            count, heads, depth, ff, names + ("gather_sems",), *plain, refs[len(names) :]
        )

    outs = pl.pallas_call(
        body,
        name="layer",
        out_shape=tuple(value[0] for value in results.values()),
        in_specs=[specs.get(name, ANY) for name in arrays],
        out_specs=tuple(value[1] for value in results.values()),
        scratch_shapes=list(scratch.values()) + mesh_sems(count) * 3,
        compiler_params=comm_params(0, 60 << 20),
    )(*arrays.values())
    return types.SimpleNamespace(**dict(zip(results, outs)))


def widen_body(
    part, down_ref, pair_ref, proj_ref, slim_ref, block_ref, hidden_ref, small_ref,
    down_out, gate_out, up_out, query_out, key_out, value_out, out_out,
    block_out, hidden_out, one_out, two_out, bias_out, small, sems,
):
    copies = [
        pltpu.make_async_copy(source, target, sems.at[index])
        for index, (source, target) in enumerate(
            ((small_ref, small), (block_ref, block_out), (hidden_ref, hidden_out))
        )
    ]
    step = pl.program_id(0)

    @pl.when(step == 0)
    def _():
        for copy in copies:
            copy.start()

    full, half = part // LANES, LANES // 2
    for source in range(down_ref.shape[1]):
        columns = slice(source * LANES, (source + 1) * LANES)
        down_out[:, columns] = down_ref[0, source].astype(F32)
        for index, o_ref in enumerate((query_out, key_out, value_out)):
            o_ref[:, columns] = proj_ref[0, source, index].astype(F32)
    dps = pair_ref.shape[0]
    slim = out_out.shape[0] // dps
    for dp in range(dps):
        base = dp * part
        shift = half if dp % 2 else 0
        for which, o_ref in enumerate((gate_out, up_out)):
            for tile in range(full):
                column = base + shift + tile * LANES
                o_ref[:, column : column + LANES] = pair_ref[dp, 0, which * full + tile].astype(F32)
        edge = pair_ref[dp, 0, 2 * full].astype(F32)
        column = base if dp % 2 else base + full * LANES
        gate_half = slice(half, LANES) if dp % 2 else slice(0, half)
        up_half = slice(0, half) if dp % 2 else slice(half, LANES)
        gate_out[:, column : column + half] = edge[:, gate_half]
        up_out[:, column : column + half] = edge[:, up_half]
        for tile in range(out_out.shape[1] // LANES):
            out_out[dp * slim : (dp + 1) * slim, tile * LANES : (tile + 1) * LANES] = slim_ref[
                dp, 0, 0, tile * slim : (tile + 1) * slim
            ].astype(F32)

    @pl.when(step == pl.num_programs(0) - 1)
    def _():
        for copy in copies:
            copy.wait()
        tiles = one_out.shape[0]
        one_out[...] = small[:tiles]
        two_out[...] = small[tiles : 2 * tiles]
        bias_out[...] = small[2 * tiles :, : bias_out.shape[1]]


def widen(out, levels, ff):
    rows, width = out.hidden_grad.shape
    dps, count = out.down_all.shape[:2]
    quarter = width // dps
    small_rows = out.small_sum.shape[0]
    tiles = width // LANES
    heads = small_rows - 2 * tiles
    pieces = count // dps
    pair = out.pair_all.reshape(dps, count, -1, rows, LANES)
    proj = out.proj_all.reshape(dps, count, 4, quarter, LANES)
    shape = lambda *dims: jax.ShapeDtypeStruct(dims, F32)
    spec = pl.BlockSpec
    whole = lambda *dims: spec(dims, lambda i: (0,) * len(dims))
    row = lambda size, span: spec((size, span), lambda i: (i, 0))
    return pl.pallas_call(
        functools.partial(widen_body, ff),
        name="widen",
        grid=(count,),
        out_shape=(
            shape(dps * ff, width),
            shape(width, dps * ff),
            shape(width, dps * ff),
            *[shape(width, width)] * 4,
            jax.ShapeDtypeStruct((rows, width), BF),
            shape(rows, width),
            shape(tiles, LANES),
            shape(tiles, LANES),
            shape(heads, levels),
        ),
        in_specs=[
            spec((1, count, ff // pieces, LANES), lambda i: (i // pieces, 0, i % pieces, 0)),
            spec((dps, 1, pair.shape[2], rows, LANES), lambda i: (0, i, 0, 0, 0)),
            spec((1, count, 3, quarter // pieces, LANES), lambda i: (i // pieces, 0, 0, i % pieces, 0)),
            spec((dps, 1, 1, quarter, LANES), lambda i: (0, i, 3, 0, 0)),
            ANY,
            ANY,
            ANY,
        ],
        out_specs=(
            row(ff // pieces, width),
            row(rows, dps * ff),
            row(rows, dps * ff),
            *[row(quarter // pieces, width)] * 3,
            row(width // count, width),
            whole(rows, width),
            whole(rows, width),
            whole(tiles, LANES),
            whole(tiles, LANES),
            whole(heads, levels),
        ),
        scratch_shapes=[pltpu.VMEM((small_rows, LANES), F32), pltpu.SemaphoreType.DMA((3,))],
        compiler_params=pltpu.CompilerParams(vmem_limit_bytes=56 << 20),
    )(out.down_all, pair, proj, proj, out.block_out, out.hidden_grad, out.small_sum)


def split_shards(
    hidden,
    group_ids,
    norm1_gain,
    query_weight,
    key_weight,
    value_weight,
    out_weight,
    relative_bias,
    norm2_gain,
    gate_weight,
    up_weight,
    down_projection_weight,
    out_grad,
    *,
    count,
):
    width = hidden.shape[2]
    levels, head_count = relative_bias.shape
    depth = query_weight.shape[1] // head_count
    heads = head_count // count
    ff = gate_weight.shape[1] // 4
    arrays = dict(
        hidden=hidden[0],
        out_grad=out_grad[0],
        gain_one=norm1_gain,
        gain_two=norm2_gain,
        row_ids=group_ids,
        table=relative_bias.T,
        query_weight=query_weight,
        key_weight=key_weight,
        value_weight=value_weight,
        out_weight=out_weight,
        gate_weight=gate_weight,
        up_weight=up_weight,
        down_weight=down_projection_weight,
    )
    out = layer(arrays, count, heads, depth, ff)
    down, gate, up, query, key, value, projected, block, grad, one, two, bias = widen(
        out, levels, ff
    )
    return (
        block[None], grad[None], one.reshape(-1), query, key, value, projected, bias.T,
        two.reshape(-1), gate, up, down,
    )


def rms_norm(vector, norm_gain):
    return (
        vector * lax.rsqrt(jnp.mean(vector * vector, axis=-1, keepdims=True) + EPSILON) * norm_gain
    )


def activate(gate_proj, up_proj):
    return jax.nn.gelu(gate_proj, approximate=True) * up_proj


def scores_of(
    query_part, key_part, query_places, key_places, query_groups, key_groups, bias_lookup
):
    bucket = bucket_of(key_places[None, :] - query_places[:, None])
    levels = jnp.arange(bias_lookup.shape[0], dtype=jnp.int32)
    one_hot_mask = (bucket[None] == levels[:, None, None]).astype(jnp.bfloat16)
    bias_patch_block = jnp.einsum(
        "ctf,cx->xtf", one_hot_mask, bias_lookup, preferred_element_type=jnp.float32
    )
    raw_scores = (
        jnp.einsum("qhd,khd->hqk", query_part, key_part, preferred_element_type=jnp.float32)
        + bias_patch_block
    )
    same_group = query_groups[:, None] == key_groups[None, :]
    return (one_hot_mask, jnp.where(same_group[None], raw_scores, MASKED))


def shards(
    hidden,
    group_ids,
    norm1_gain,
    query_weight,
    key_weight,
    value_weight,
    out_weight,
    relative_bias,
    norm2_gain,
    gate_weight,
    up_weight,
    down_projection_weight,
    out_grad,
):
    tok_rows = hidden.shape[1]
    head_count = relative_bias.shape[1]
    inner_width = query_weight.shape[1]
    head_depth = inner_width // head_count
    row_length = group_ids.shape[1]
    row_start = lax.axis_index("seq") * tok_rows
    key_block = min(1024, row_length)
    block_count = row_length // key_block
    row_groups = group_ids[0]
    own_groups = lax.dynamic_slice_in_dim(row_groups, row_start, tok_rows)
    own_places = row_start + jnp.arange(tok_rows, dtype=jnp.int32)
    all_places = jnp.arange(row_length, dtype=jnp.int32)

    def key_blocks(key_rows, value_rows):
        return (
            key_rows.reshape(block_count, key_block, head_count, head_depth),
            value_rows.reshape(block_count, key_block, head_count, head_depth),
            row_groups.reshape(block_count, key_block),
            all_places.reshape(block_count, key_block),
        )

    inputs = hidden[0].astype(jnp.float32)
    normed, norm_pull = jax.vjp(rms_norm, inputs, norm1_gain.astype(jnp.float32))
    normed_low = normed.astype(jnp.bfloat16)
    query_low = jnp.dot(normed_low, query_weight, preferred_element_type=jnp.float32).astype(
        jnp.bfloat16
    )
    key_low = jnp.dot(normed_low, key_weight, preferred_element_type=jnp.float32).astype(
        jnp.bfloat16
    )
    value_low = jnp.dot(normed_low, value_weight, preferred_element_type=jnp.float32).astype(
        jnp.bfloat16
    )
    key_all, value_all = (
        lax.all_gather(key_low, "seq", axis=0, tiled=True),
        lax.all_gather(value_low, "seq", axis=0, tiled=True),
    )
    query_heads = query_low.reshape(tok_rows, head_count, head_depth)

    def gather_stats(carry_state, scanned):
        running_max, running_sum = carry_state
        key_part, value_part, key_groups, key_places = scanned
        one_hot_mask, scores = scores_of(
            query_heads, key_part, own_places, key_places, own_groups, key_groups, relative_bias
        )
        new_max = jnp.maximum(running_max, jnp.max(scores, axis=-1))
        running_sum = running_sum * jnp.exp(running_max - new_max) + jnp.sum(
            jnp.exp(scores - new_max[..., None]), axis=-1
        )
        return ((new_max, running_sum), None)

    stats_init = (
        jnp.full((head_count, tok_rows), MASKED, jnp.float32),
        jnp.zeros((head_count, tok_rows), jnp.float32),
    )
    (running_max, running_sum), _ = lax.scan(
        gather_stats, stats_init, key_blocks(key_all, value_all)
    )
    log_total = running_max + jnp.log(running_sum)

    def gather_values(summed, scanned):
        key_part, value_part, key_groups, key_places = scanned
        one_hot_mask, scores = scores_of(
            query_heads, key_part, own_places, key_places, own_groups, key_groups, relative_bias
        )
        attention_low = jnp.exp(scores - log_total[..., None]).astype(jnp.bfloat16)
        return (
            summed
            + jnp.einsum(
                "hqk,khd->qhd", attention_low, value_part, preferred_element_type=jnp.float32
            ),
            None,
        )

    mixed, _ = lax.scan(
        gather_values,
        jnp.zeros((tok_rows, head_count, head_depth), jnp.float32),
        key_blocks(key_all, value_all),
    )
    mixed_low = mixed.reshape(tok_rows, inner_width).astype(jnp.bfloat16)
    middle = inputs + jnp.dot(mixed_low, out_weight, preferred_element_type=jnp.float32)
    normed_two, norm_two_pull = jax.vjp(rms_norm, middle, norm2_gain.astype(jnp.float32))
    normed_two_low = normed_two.astype(jnp.bfloat16)
    gate_proj = jnp.dot(normed_two_low, gate_weight, preferred_element_type=jnp.float32)
    up_proj = jnp.dot(normed_two_low, up_weight, preferred_element_type=jnp.float32)
    activated, act_pull = jax.vjp(activate, gate_proj, up_proj)
    activated_low = activated.astype(jnp.bfloat16)
    result = middle + jnp.dot(
        activated_low, down_projection_weight, preferred_element_type=jnp.float32
    )
    block_out = result.astype(jnp.bfloat16)[None]
    cotangent_low = out_grad[0]
    grad_down = dot_rows(activated_low, cotangent_low)
    act_grad = dot_cols(cotangent_low, down_projection_weight)
    gate_grad, up_grad = act_pull(act_grad)
    gate_grad_low = gate_grad.astype(jnp.bfloat16)
    up_grad_low = up_grad.astype(jnp.bfloat16)
    grad_gate = dot_rows(normed_two_low, gate_grad_low)
    grad_up = dot_rows(normed_two_low, up_grad_low)
    normed_two_grad = dot_cols(gate_grad_low, gate_weight) + dot_cols(up_grad_low, up_weight)
    middle_norm_grad, grad_gain_two = norm_two_pull(normed_two_grad)
    middle_grad = cotangent_low.astype(jnp.float32) + middle_norm_grad
    branch_grad_low = middle_grad.astype(jnp.bfloat16)
    grad_out = dot_rows(mixed_low, branch_grad_low)
    mixed_grad_low = (
        dot_cols(branch_grad_low, out_weight)
        .astype(jnp.bfloat16)
        .reshape(tok_rows, head_count, head_depth)
    )
    row_dots = jnp.einsum("qhd,qhd->hq", mixed_grad_low.astype(jnp.float32), mixed)
    key_back, value_back = (
        lax.all_gather(key_low, "seq", axis=0, tiled=True),
        lax.all_gather(value_low, "seq", axis=0, tiled=True),
    )
    grads_init = (
        jnp.zeros((tok_rows, head_count, head_depth), jnp.float32),
        jnp.zeros(relative_bias.shape, jnp.float32),
    )

    def backward_block(carry_state, scanned):
        query_grad, table_grad = carry_state
        key_part, value_part, key_groups, key_places = scanned
        one_hot_mask, scores = scores_of(
            query_heads, key_part, own_places, key_places, own_groups, key_groups, relative_bias
        )
        attention = jnp.exp(scores - log_total[..., None])
        grad_weights = jnp.einsum(
            "qhd,khd->hqk", mixed_grad_low, value_part, preferred_element_type=jnp.float32
        )
        score_gradients = (attention * (grad_weights - row_dots[..., None])).astype(jnp.bfloat16)
        query_grad = query_grad + jnp.einsum(
            "hqk,khd->qhd", score_gradients, key_part, preferred_element_type=jnp.float32
        )
        table_grad = table_grad + jnp.einsum(
            "oei,cei->oc", one_hot_mask, score_gradients, preferred_element_type=jnp.float32
        )
        key_grad = jnp.einsum(
            "hqk,qhd->khd", score_gradients, query_heads, preferred_element_type=jnp.float32
        )
        value_grad = jnp.einsum(
            "hqk,qhd->khd",
            attention.astype(jnp.bfloat16),
            mixed_grad_low,
            preferred_element_type=jnp.float32,
        )
        return ((query_grad, table_grad), (key_grad, value_grad))

    (query_grad, table_grad), (key_terms, value_terms) = lax.scan(
        backward_block, grads_init, key_blocks(key_back, value_back)
    )
    key_grad, value_grad = (
        lax.psum_scatter(
            key_terms.reshape(row_length, inner_width), "seq", scatter_dimension=0, tiled=True
        ),
        lax.psum_scatter(
            value_terms.reshape(row_length, inner_width), "seq", scatter_dimension=0, tiled=True
        ),
    )
    query_grad_low = query_grad.reshape(tok_rows, inner_width).astype(jnp.bfloat16)
    key_grad_low = key_grad.astype(jnp.bfloat16)
    value_grad_low = value_grad.astype(jnp.bfloat16)
    grad_query = dot_rows(normed_low, query_grad_low)
    grad_key = dot_rows(normed_low, key_grad_low)
    grad_value = dot_rows(normed_low, value_grad_low)
    normed_grad = (
        dot_cols(query_grad_low, query_weight)
        + dot_cols(key_grad_low, key_weight)
        + dot_cols(value_grad_low, value_weight)
    )
    input_norm_grad, grad_gain_one = norm_pull(normed_grad)
    hidden_grad = (middle_grad + input_norm_grad)[None]
    local_grads = (
        grad_gain_one,
        grad_query,
        grad_key,
        grad_value,
        grad_out,
        table_grad.reshape(-1),
        grad_gain_two,
        grad_gate,
        grad_up,
        grad_down,
    )
    shared = (
        lax.psum_scatter(local_grads[0], "seq", scatter_dimension=0, tiled=True),
        lax.psum_scatter(local_grads[1], "seq", scatter_dimension=0, tiled=True),
        lax.psum_scatter(local_grads[2], "seq", scatter_dimension=0, tiled=True),
        lax.psum_scatter(local_grads[3], "seq", scatter_dimension=0, tiled=True),
        lax.psum_scatter(local_grads[4], "seq", scatter_dimension=0, tiled=True),
        lax.psum_scatter(local_grads[5], "seq", scatter_dimension=0, tiled=True),
        lax.psum_scatter(local_grads[6], "seq", scatter_dimension=0, tiled=True),
        lax.psum_scatter(local_grads[7], "seq", scatter_dimension=0, tiled=True),
        lax.psum_scatter(local_grads[8], "seq", scatter_dimension=0, tiled=True),
        lax.psum_scatter(local_grads[9], "seq", scatter_dimension=0, tiled=True),
    )
    shared = (
        lax.psum(shared[0].astype(jnp.bfloat16), "dp").astype(jnp.float32),
        lax.psum(shared[1].astype(jnp.bfloat16), "dp").astype(jnp.float32),
        lax.psum(shared[2].astype(jnp.bfloat16), "dp").astype(jnp.float32),
        lax.psum(shared[3].astype(jnp.bfloat16), "dp").astype(jnp.float32),
        lax.psum(shared[4].astype(jnp.bfloat16), "dp").astype(jnp.float32),
        lax.psum(shared[5].astype(jnp.bfloat16), "dp").astype(jnp.float32),
        lax.psum(shared[6].astype(jnp.bfloat16), "dp").astype(jnp.float32),
        lax.psum(shared[7].astype(jnp.bfloat16), "dp").astype(jnp.float32),
        lax.psum(shared[8].astype(jnp.bfloat16), "dp").astype(jnp.float32),
        lax.psum(shared[9].astype(jnp.bfloat16), "dp").astype(jnp.float32),
    )
    summed = (
        lax.all_gather(shared[0].astype(jnp.bfloat16), "seq", axis=0, tiled=True).astype(
            jnp.float32
        ),
        lax.all_gather(shared[1].astype(jnp.bfloat16), "seq", axis=0, tiled=True).astype(
            jnp.float32
        ),
        lax.all_gather(shared[2].astype(jnp.bfloat16), "seq", axis=0, tiled=True).astype(
            jnp.float32
        ),
        lax.all_gather(shared[3].astype(jnp.bfloat16), "seq", axis=0, tiled=True).astype(
            jnp.float32
        ),
        lax.all_gather(shared[4].astype(jnp.bfloat16), "seq", axis=0, tiled=True).astype(
            jnp.float32
        ),
        lax.all_gather(shared[5].astype(jnp.bfloat16), "seq", axis=0, tiled=True).astype(
            jnp.float32
        ),
        lax.all_gather(shared[6].astype(jnp.bfloat16), "seq", axis=0, tiled=True).astype(
            jnp.float32
        ),
        lax.all_gather(shared[7].astype(jnp.bfloat16), "seq", axis=0, tiled=True).astype(
            jnp.float32
        ),
        lax.all_gather(shared[8].astype(jnp.bfloat16), "seq", axis=0, tiled=True).astype(
            jnp.float32
        ),
        lax.all_gather(shared[9].astype(jnp.bfloat16), "seq", axis=0, tiled=True).astype(
            jnp.float32
        ),
    )
    return (
        block_out,
        hidden_grad,
        summed[0],
        summed[1],
        summed[2],
        summed[3],
        summed[4],
        summed[5].reshape(relative_bias.shape),
        summed[6],
        summed[7],
        summed[8],
        summed[9],
    )


def solution(mesh):
    placed = (P("dp", "seq", None), P("dp", None)) + (P(),) * 10 + (P("dp", "seq", None),)
    out_specs = (P("dp", "seq", None),) * 2 + (P(),) * 10
    count = mesh.shape["seq"]

    def run(*args):
        hidden, query_weight, relative_bias = args[0], args[3], args[7]
        head_count = relative_bias.shape[1]
        inner = query_weight.shape[1] // count
        fits = (
            mesh.shape["dp"] == 4
            and count % 2 == 0
            and head_count % count == 0
            and inner == LANES
            and hidden.shape[2] == count * LANES
            and hidden.shape[1] == count * LANES
            and args[9].shape[1] % (4 * LANES) == 2 * LANES
        )
        body = functools.partial(split_shards, count=count) if fits else shards
        return jax.shard_map(
            body, mesh=mesh, in_specs=placed, out_specs=out_specs, check_vma=False
        )(*args)

    return run
```
